128 devices in a mesh: row: 16 (over y, x_hi, core), col: 8 (over z, x_lo).
Axes of the slice: x: 4 (x_hi: 2, x_lo: 2; x = x_hi * 2 + x_lo), y: 4, z: 4, core: 2. Of those that a mesh axis runs over, the one named last changes fastest.
Arguments:
- layer_input: bfloat16 [8192, 8192], P('row', 'col'), may hold values from -48 to 48
- w_query: bfloat16 [8192, 8192], P('row', 'col'), may hold values from -0.0625 to 0.0625
- w_key: bfloat16 [8192, 1024], P('row', 'col'), may hold values from -0.0625 to 0.0625
- w_value: bfloat16 [8192, 1024], P('row', 'col'), may hold values from -0.0625 to 0.0625
- counts: int32 [64], replicated, may hold values from 1 to 128
- pattern: int32 [64, 4], P('row'), may hold values from 0 to 63, as said below
- cotangent: bfloat16 [8192, 8192], P('row', 'col'), may hold values from -6 to 6
Outputs:
- attended: bfloat16 [8192, 8192], P('row', 'col')
- input_grad: bfloat16 [8192, 8192], P('row', 'col')
The draws below stay inside these ranges and needn't reach their ends.
Inputs may be any that keep to these rules, and one draw needn't show every extreme that they name: `pattern`: row b lists 4 different blocks, b itself first; every entry lies at a cyclic distance of at most 4 blocks from b, and the second entry exactly at that distance.
All inputs are finite; a program needn't handle non-finite values.
Results may differ from the reference program's by a relative error of at most 0.035.
The reference program's roundings to bfloat16 on the way count: a program that leaves them out, or rounds other values in their place, can miss the bound.
Values may be sent and summed in bfloat16 or wider, within the bound.
A program may use at most 128 MiB of HBM per device.

```python
import jax
import jax.numpy as jnp
from jax import lax

D = 8192
HEADS = 64
KV_HEADS = 8
HEAD_DIM = 128
BLOCK = 128
NEIGHBOURS = 4
TOK_ROW = 512
TOKENS = 8192
NBLK = 64
QCOLS = 8192
KVCOLS = 1024
N_COL = 8


def draw_layer_input(key, part):
    key_one = jax.random.fold_in(jax.random.fold_in(key, 11), 0)
    base_draw = jnp.clip(jax.random.normal(key_one, (TOKENS, D), jnp.float32), -4.0, 4.0)
    return base_draw.astype(jnp.bfloat16)


def draw_pattern(key, part):
    block_count = TOKENS // BLOCK
    reach_blocks = TOK_ROW // BLOCK
    key_one, key_two = jax.random.split(jax.random.fold_in(key, 23))
    anchor = jnp.arange(block_count, dtype=jnp.int32)
    sign_flip = jax.random.randint(key_one, (block_count,), 0, 2).astype(jnp.int32) * 2 - 1
    far_offset = sign_flip * reach_blocks
    offsets = jnp.concatenate([jnp.arange(-(reach_blocks - 1), 0, dtype=jnp.int32), jnp.arange(1, reach_blocks, dtype=jnp.int32)])
    width_span = 2 * reach_blocks - 2
    scores = jax.random.randint(key_two, (block_count, width_span), 0, 2 ** 20).astype(jnp.int32) * width_span + jnp.arange(width_span, dtype=jnp.int32)[None, :]
    order_rank = jnp.argsort(scores, axis=1, stable=True).astype(jnp.int32)
    near_one = offsets[order_rank[:, 0]]
    near_two = offsets[order_rank[:, 1]]
    table_rows = jnp.stack([anchor, anchor + far_offset, anchor + near_one, anchor + near_two], axis=1)
    return jnp.mod(table_rows, block_count).astype(jnp.int32)


def set_ends(drawn, own_key, low, high):
    spot = [jax.random.randint(jax.random.fold_in(own_key, axis), (), 0, length) for axis, length in enumerate(drawn.shape)]
    longest = drawn.shape.index(max(drawn.shape))
    neighbour = spot[:longest] + [(spot[longest] + 1) % drawn.shape[longest]] + spot[longest + 1:]
    return drawn.at[tuple(spot)].set(low).at[tuple(neighbour)].set(high)


def block_levels(stream_key, dims, shards, least, largest):
    def one(dim, parts):
        heights = jax.random.uniform(jax.random.fold_in(jax.random.fold_in(stream_key, 6), dim), (parts,), jnp.float32, least / len(shards), largest / len(shards))
        return jnp.repeat(jnp.exp(heights), dims[dim] // parts).reshape((-1,) + (1,) * (len(dims) - dim - 1))

    loudness = one(*shards[0])
    for cut in shards[1:]:
        loudness = loudness * one(*cut)
    return loudness


def noise(own_key, shape, spread, reach, cuts=(), held_as=jnp.bfloat16):
    drawn = spread * jax.random.normal(own_key, shape, jnp.float32)
    if cuts:
        drawn = drawn * block_levels(own_key, shape, cuts, -0.22, 0.18)
    return jnp.clip(drawn, -reach, reach).astype(held_as)


def setup_inputs(seed: int = 0) -> dict:
    seeds = jax.random.split(jax.random.key(seed), 8)
    return {
        "layer_input": draw_layer_input(jax.random.fold_in(seeds[7], 71), 0),
        "w_query": noise(seeds[1], (D, QCOLS), D ** -0.5, 0.0625, ((0, 16), (1, 8))),
        "w_key": noise(seeds[2], (D, KVCOLS), D ** -0.5, 0.0625, ((0, 16), (1, 8))),
        "w_value": noise(seeds[3], (D, KVCOLS), D ** -0.5, 0.0625, ((0, 16), (1, 8))),
        "counts": set_ends(jax.random.randint(seeds[4], (NBLK,), 1, BLOCK + 1), jax.random.fold_in(seeds[4], 1), 1, BLOCK).astype(jnp.int32),
        "pattern": draw_pattern(jax.random.fold_in(seeds[7], 71), 0),
        "cotangent": noise(seeds[6], (TOKENS, QCOLS), 1.0, 6.0, ((0, 16), (1, 8))),
    }


def round_low(array_in):
    return lax.optimization_barrier(array_in.astype(jnp.bfloat16))


def reference(layer_input, w_query, w_key, w_value, counts, pattern, cotangent):
    score_scale = HEAD_DIM ** -0.5
    group_size = HEADS // KV_HEADS
    block_count = TOKENS // BLOCK
    query = round_low(jnp.dot(layer_input, w_query, preferred_element_type=jnp.float32))
    keys = round_low(jnp.dot(layer_input, w_key, preferred_element_type=jnp.float32))
    values = round_low(jnp.dot(layer_input, w_value, preferred_element_type=jnp.float32))
    query_blocks = query.reshape(block_count, BLOCK, KV_HEADS, group_size, HEAD_DIM)
    key_blocks = keys.reshape(block_count, BLOCK, KV_HEADS, HEAD_DIM)
    value_blocks = values.reshape(block_count, BLOCK, KV_HEADS, HEAD_DIM)
    grad_blocks = cotangent.reshape(block_count, BLOCK, KV_HEADS, group_size, HEAD_DIM)
    positions = jnp.arange(BLOCK, dtype=jnp.int32)

    def one_block(totals, block_id):
        key_total, value_total = totals
        chosen_ids = pattern[block_id]
        query_now = query_blocks[block_id].astype(jnp.float32)
        key_now = key_blocks[chosen_ids].reshape(NEIGHBOURS * BLOCK, KV_HEADS, HEAD_DIM).astype(jnp.float32)
        value_now = value_blocks[chosen_ids].reshape(NEIGHBOURS * BLOCK, KV_HEADS, HEAD_DIM).astype(jnp.float32)
        key_live = (positions[None, :] < counts[chosen_ids][:, None]).reshape(-1)
        query_live = (positions < counts[block_id]).astype(jnp.float32)[:, None, None, None]
        scores = jnp.einsum('qkgd,jkd->kgqj', query_now, key_now) * score_scale
        scores = jnp.where(key_live, scores, -1e30)
        score_max = jnp.max(scores, axis=-1, keepdims=True)
        exponent = jnp.exp(scores - score_max)
        prob_full = exponent / jnp.sum(exponent, axis=-1, keepdims=True)
        probs_low = round_low(prob_full).astype(jnp.float32)
        mixed_out = jnp.einsum('kgqj,jkd->qkgd', probs_low, value_now) * query_live
        attended = round_low(mixed_out)
        grad_out = round_low(grad_blocks[block_id].astype(jnp.float32) * query_live).astype(jnp.float32)
        row_delta = jnp.einsum('qkgd,qkgd->kgq', grad_out, attended.astype(jnp.float32))
        grad_probs = jnp.einsum('qkgd,jkd->kgqj', grad_out, value_now)
        grad_scores = round_low(prob_full * (grad_probs - row_delta[..., None]) * score_scale).astype(jnp.float32)
        grad_query = round_low(jnp.einsum('kgqj,jkd->qkgd', grad_scores, key_now))
        key_part = jnp.einsum('kgqj,qkgd->jkd', grad_scores, query_now).reshape(NEIGHBOURS, BLOCK, KV_HEADS, HEAD_DIM)
        value_part = jnp.einsum('kgqj,qkgd->jkd', probs_low, grad_out).reshape(NEIGHBOURS, BLOCK, KV_HEADS, HEAD_DIM)
        key_total = key_total.at[chosen_ids].add(key_part)
        value_total = value_total.at[chosen_ids].add(value_part)
        return (key_total, value_total), (attended, grad_query)

    initial = (jnp.zeros((block_count, BLOCK, KV_HEADS, HEAD_DIM), jnp.float32), jnp.zeros((block_count, BLOCK, KV_HEADS, HEAD_DIM), jnp.float32))
    (key_total, value_total), (attended, grad_query) = lax.scan(one_block, initial, jnp.arange(block_count, dtype=jnp.int32))
    attended = attended.reshape(TOKENS, HEADS * HEAD_DIM)
    grad_query = grad_query.reshape(TOKENS, HEADS * HEAD_DIM)
    grad_keys = round_low(key_total.reshape(TOKENS, KV_HEADS * HEAD_DIM))
    grad_values = round_low(value_total.reshape(TOKENS, KV_HEADS * HEAD_DIM))
    query_width = HEADS * HEAD_DIM // N_COL
    key_width = KV_HEADS * HEAD_DIM // N_COL
    grad_sum = jnp.zeros((TOKENS, D), jnp.float32)
    for group in range(N_COL):
        q_lo = group * query_width
        k_lo = group * key_width
        partial_value = jnp.dot(grad_query[:, q_lo:q_lo + query_width], w_query[:, q_lo:q_lo + query_width].T, preferred_element_type=jnp.float32)
        partial_value = partial_value + jnp.dot(grad_keys[:, k_lo:k_lo + key_width], w_key[:, k_lo:k_lo + key_width].T, preferred_element_type=jnp.float32)
        partial_value = partial_value + jnp.dot(grad_values[:, k_lo:k_lo + key_width], w_value[:, k_lo:k_lo + key_width].T, preferred_element_type=jnp.float32)
        grad_sum = grad_sum + round_low(partial_value).astype(jnp.float32)
    return attended, grad_sum.astype(jnp.bfloat16)
```

```python
import functools

import jax
import jax.numpy as jnp
from jax import lax
from jax.experimental import pallas as pl
from jax.experimental.pallas import tpu as pltpu
from jax.sharding import PartitionSpec as P

HEADS = 64
KV_HEADS = 8
HEAD_DIM = 128
BLOCK = 128
GROUP = HEADS // KV_HEADS
ROWS = 16
COLS = 8
TOK = 512
HALF = 256
FEAT = 1024
KV = 256
WIDE = FEAT + KV
MESH = pl.DeviceIdType.MESH
MIB = 1024 * 1024


def place():
    row, col = lax.axis_index("row"), lax.axis_index("col")
    return row, col, row // 4, (row // 2) % 2, row % 2, col // 2, col % 2


def remote(src, dst, send, recv, row, col):
    return pltpu.make_async_remote_copy(
        src_ref=src,
        dst_ref=dst,
        send_sem=send,
        recv_sem=recv,
        device_id=(row, col),
        device_id_type=MESH,
    )


BRINGS = {0: (3, 0), 1: (3, 1), 2: (1, 1), 3: (1, 0), 4: (2, 0), 5: (2, 1)}


def gather_kernel(
    x_in, wq_in, wk_in, wv_in,
    q_out, kv_out, w_out,
    xf, wf, acc, kv_buf,
    load_sem, xs, xr, xps, xpr, ws, wr, wps, wpr, cs, cr, hs, hr, out_sem, kv_sem,
):
    row, col, y, h, k, z, l = place()
    prev_row, next_row = (row + ROWS - 1) % ROWS, (row + 1) % ROWS

    def row_of(yy, hh, kk):
        return (yy * 2 + hh) * 2 + kk

    y_next, y_prev = row_of((y + 1) % 4, h, k), row_of((y + 3) % 4, h, k)
    h_pair, sibling = row_of(y, 1 - h, k), row_of(y, h, 1 - k)
    z_next, z_prev = ((z + 1) % 4) * 2 + l, ((z + 3) % 4) * 2 + l
    l_pair = z * 2 + 1 - l

    own_x, own_w = col, row // 2
    own_rows = pl.ds(k * TOK, TOK)
    loads = [
        pltpu.make_async_copy(x_in, xf.at[own_x], load_sem.at[0]),
        pltpu.make_async_copy(wq_in, wf.at[own_w, own_rows, pl.ds(0, FEAT)], load_sem.at[1]),
        pltpu.make_async_copy(wk_in, wf.at[own_w, own_rows, pl.ds(FEAT, 128)], load_sem.at[2]),
        pltpu.make_async_copy(
            wv_in, wf.at[own_w, own_rows, pl.ds(FEAT + 128, 128)], load_sem.at[3]
        ),
    ]
    for load in loads:
        load.start()

    barrier = pltpu.get_barrier_semaphore()
    peers = [
        (row, z_next), (row, z_prev), (row, l_pair),
        (y_next, col), (y_prev, col), (h_pair, col), (sibling, col),
        (prev_row, col), (next_row, col),
    ]
    for peer in peers:
        pl.semaphore_signal(barrier, inc=1, device_id=peer, device_id_type=MESH)
    pl.semaphore_wait(barrier, len(peers))
    for load in loads:
        load.wait()

    def x_piece(step, plane, half):
        slot = ((z + step) % 4) * 2 + (l + plane) % 2
        return xf.at[slot, pl.ds(half * HALF, HALF)]

    def w_piece(step, plane, half, core=None):
        slot = ((y + step) % 4) * 2 + (h + plane) % 2
        core = k if core is None else core
        return wf.at[slot, pl.ds(core * TOK + half * HALF, HALF)]

    started = []

    def x_ring(plane, kind):
        step, half = (0, (0, 1, 1, 0)[kind]) if kind < 4 else ((3, 0) if kind == 4 else (1, 1))
        ref = x_piece(step, plane, half)
        peer = z_next if kind in (0, 1, 4) else z_prev
        i = plane * 6 + kind
        copy = remote(ref, ref, xs.at[i], xr.at[i], row, peer)
        copy.start()
        started.append(copy)

    def x_got(plane, kind):
        step, half = BRINGS[kind]
        ref = x_piece(step, plane, half)
        i = plane * 6 + kind
        remote(ref, ref, xs.at[i], xr.at[i], row, z_prev).wait_recv()

    def w_ring(plane, kind):
        step, half = (0, (0, 1, 1, 0)[kind]) if kind < 4 else ((3, 0) if kind == 4 else (1, 1))
        ref = w_piece(step, plane, half)
        peer = y_next if kind in (0, 1, 4) else y_prev
        i = plane * 6 + kind
        copy = remote(ref, ref, ws.at[i], wr.at[i], peer, col)
        copy.start()
        started.append(copy)

    def w_share(step, plane, half):
        ref = w_piece(step, plane, half)
        i = (step * 2 + plane) * 2 + half
        copy = remote(ref, ref, cs.at[i], cr.at[i], sibling, col)
        copy.start()
        started.append(copy)

    def w_shared(step, plane, half):
        ref = w_piece(step, plane, half, 1 - k)
        i = (step * 2 + plane) * 2 + half
        remote(ref, ref, cs.at[i], cr.at[i], sibling, col).wait_recv()

    def w_got(plane, kind):
        step, half = BRINGS[kind]
        ref = w_piece(step, plane, half)
        i = plane * 6 + kind
        remote(ref, ref, ws.at[i], wr.at[i], y_prev, col).wait_recv()
        if kind in (0, 2):
            w_ring(plane, 4 if kind == 0 else 5)
        w_share(step, plane, half)

    for kind in (0, 2, 1, 3):
        x_ring(0, kind)
        w_ring(0, kind)
    for half in range(2):
        ref = x_piece(0, 0, half)
        copy = remote(ref, ref, xps.at[half], xpr.at[half], row, l_pair)
        copy.start()
        started.append(copy)
        ref = w_piece(0, 0, half)
        copy = remote(ref, ref, wps.at[half], wpr.at[half], h_pair, col)
        copy.start()
        started.append(copy)
        w_share(0, 0, half)

    for kind in (0, 2):
        x_got(0, kind)
        x_ring(0, 4 if kind == 0 else 5)
        w_got(0, kind)
    for half in range(2):
        ref = x_piece(0, 1, half)
        remote(ref, ref, xps.at[half], xpr.at[half], row, l_pair).wait_recv()
        for kind in ((0, 3), (1, 2))[half]:
            x_ring(1, kind)
        ref = w_piece(0, 1, half)
        remote(ref, ref, wps.at[half], wpr.at[half], h_pair, col).wait_recv()
        for kind in ((0, 3), (1, 2))[half]:
            w_ring(1, kind)
        w_share(0, 1, half)
    for kind in (1, 3, 4, 5):
        x_got(0, kind)
        w_got(0, kind)
    for kind in (0, 2):
        x_got(1, kind)
        x_ring(1, 4 if kind == 0 else 5)
        w_got(1, kind)
    for kind in (1, 3):
        x_got(1, kind)
        w_got(1, kind)
    for step in (0, 1, 3):
        for plane in range(2):
            for half in range(2):
                w_shared(step, plane, half)
    for half in range(2):
        w_shared(2, 0, half)

    late_x = ((z + 2) % 4) * 2 + 1 - l
    late_w = ((y + 2) % 4) * 2 + 1 - h

    def multiply(slot, tile):
        cols = pl.ds(pl.multiple_of(tile * 256, 256), 256)
        return jnp.dot(xf[slot], wf[slot, :, cols], preferred_element_type=jnp.float32)

    @pl.loop(0, WIDE // 256)
    def _(tile):
        acc[tile] = jnp.zeros((TOK, 256), jnp.float32)

    for slot in range(COLS):
        @pl.when((slot != late_x) & (slot != late_w))
        def _():
            @pl.loop(0, WIDE // 256)
            def _(tile):
                acc[tile] += multiply(slot, tile)

        @pl.when(slot != late_w)
        def _():
            pltpu.make_async_copy(wf.at[slot], w_out.at[slot], out_sem.at[slot]).start()

    for kind in (4, 5):
        x_got(1, kind)
        w_got(1, kind)
    for half in range(2):
        w_shared(2, 1, half)
    for slot in range(COLS):
        @pl.when(slot == late_w)
        def _():
            pltpu.make_async_copy(wf.at[slot], w_out.at[slot], out_sem.at[slot]).start()

    def finish(tile):
        acc[tile] += multiply(late_x, tile)

        @pl.when(late_w != late_x)
        def _():
            acc[tile] += multiply(late_w, tile)

        return acc[tile].astype(jnp.bfloat16)

    kv_buf[...] = finish(FEAT // 256)
    halo = [
        remote(kv_buf, kv_out.at[0], hs.at[0], hr.at[0], next_row, col),
        remote(kv_buf, kv_out.at[2], hs.at[1], hr.at[1], prev_row, col),
    ]
    for copy in halo:
        copy.start()
    own_kv = pltpu.make_async_copy(kv_buf, kv_out.at[1], kv_sem)
    own_kv.start()

    @pl.loop(0, FEAT // 256)
    def _(tile):
        cols = pl.ds(pl.multiple_of(tile * 256, 256), 256)
        q_out[:, cols] = finish(tile)

    for copy in started:
        copy.wait_send()
    for copy in halo:
        copy.wait()
    own_kv.wait()
    for slot in range(COLS):
        pltpu.make_async_copy(wf.at[slot], w_out.at[slot], out_sem.at[slot]).wait()


def gather(layer_input, w_query, w_key, w_value):
    dma = pltpu.SemaphoreType.DMA
    return pl.pallas_call(
        gather_kernel,
        name="gather_project",
        out_shape=(
            jax.ShapeDtypeStruct((TOK, FEAT), jnp.bfloat16),
            jax.ShapeDtypeStruct((3, TOK, KV), jnp.bfloat16),
            jax.ShapeDtypeStruct((COLS, FEAT, WIDE), jnp.bfloat16),
        ),
        in_specs=[pl.BlockSpec(memory_space=pl.ANY)] * 4,
        out_specs=(
            pl.BlockSpec(memory_space=pltpu.VMEM),
            pl.BlockSpec(memory_space=pl.ANY),
            pl.BlockSpec(memory_space=pl.ANY),
        ),
        scratch_shapes=[
            pltpu.VMEM((COLS, TOK, FEAT), jnp.bfloat16),
            pltpu.VMEM((COLS, FEAT, WIDE), jnp.bfloat16),
            pltpu.VMEM((WIDE // 256, TOK, 256), jnp.float32),
            pltpu.VMEM((TOK, KV), jnp.bfloat16),
            dma((4,)),
            dma((12,)), dma((12,)), dma((2,)), dma((2,)),
            dma((12,)), dma((12,)), dma((2,)), dma((2,)),
            dma((16,)), dma((16,)),
            dma((2,)), dma((2,)),
            dma((COLS,)), dma,
        ],
        compiler_params=pltpu.CompilerParams(
            collective_id=0, has_side_effects=True, vmem_limit_bytes=56 * MIB
        ),
        cost_estimate=pl.CostEstimate(
            flops=2 * TOK * 8192 * WIDE, bytes_accessed=40 * MIB, transcendentals=0
        ),
    )(layer_input, w_query, w_key, w_value)


def shifted(block, axis, distance):
    devices = range(lax.axis_size(axis))
    route = [((i - distance) % len(devices), i) for i in devices]
    return lax.ppermute(block, axis, route)


def body(layer_input, w_query, w_key, w_value, counts, pattern, cotangent):
    score_scale = HEAD_DIM ** (-0.5)
    group_size = HEADS // KV_HEADS
    tok_rows = layer_input.shape[0]
    per_dev = tok_rows // BLOCK
    block_count = per_dev * lax.axis_size("row")
    myself = lax.axis_index("row")
    query, source, full_wide = gather(layer_input, w_query, w_key, w_value)
    kv_heads = 1
    kv_cols = 128
    first_block = myself * per_dev - per_dev
    span_blocks = 3 * per_dev
    nearby = pattern.shape[1]
    local_index = jnp.mod(pattern - first_block, block_count)
    stacked = source.reshape(span_blocks, BLOCK, 2 * kv_cols)
    picked = jnp.take(stacked, local_index, axis=0).reshape(
        per_dev, nearby * BLOCK, 2, kv_heads, HEAD_DIM
    )
    key_blocks = picked[:, :, 0]
    value_blocks = picked[:, :, 1]
    positions = jnp.arange(BLOCK, dtype=jnp.int32)
    key_counts = jnp.take(counts, pattern, axis=0)
    key_live = (positions[None, None, :] < key_counts[:, :, None]).reshape(per_dev, nearby * BLOCK)
    own_counts = lax.dynamic_slice_in_dim(counts, myself * per_dev, per_dev)
    query_live = (positions[None, :] < own_counts[:, None])[:, :, None, None, None]
    query_blocks = query.reshape(per_dev, BLOCK, kv_heads, group_size, HEAD_DIM)
    scores = (
        jnp.einsum(
            "bqkgd,bjkd->bkgqj", query_blocks, key_blocks, preferred_element_type=jnp.float32
        )
        * score_scale
    )
    scores = jnp.where(key_live[:, None, None, None, :], scores, -1e30)
    score_max = jnp.max(scores, axis=-1, keepdims=True)
    exponent = jnp.exp(scores - score_max)
    prob_full = exponent / jnp.sum(exponent, axis=-1, keepdims=True)
    probs_low = prob_full.astype(jnp.bfloat16)
    mixed_out = jnp.einsum(
        "bkgqj,bjkd->bqkgd", probs_low, value_blocks, preferred_element_type=jnp.float32
    )
    attended = (mixed_out * query_live.astype(jnp.float32)).astype(jnp.bfloat16)
    grad_out = cotangent.reshape(
        per_dev, BLOCK, kv_heads, group_size, HEAD_DIM
    ) * query_live.astype(jnp.bfloat16)
    row_delta = jnp.einsum(
        "bqkgd,bqkgd->bkgq", grad_out, attended, preferred_element_type=jnp.float32
    )
    grad_probs = jnp.einsum(
        "bqkgd,bjkd->bkgqj", grad_out, value_blocks, preferred_element_type=jnp.float32
    )
    grad_scores = (prob_full * (grad_probs - row_delta[..., None]) * score_scale).astype(
        jnp.bfloat16
    )
    grad_query = jnp.einsum(
        "bkgqj,bjkd->bqkgd", grad_scores, key_blocks, preferred_element_type=jnp.float32
    )
    grad_query = grad_query.astype(jnp.bfloat16).reshape(tok_rows, -1)
    key_part = jnp.einsum(
        "bkgqj,bqkgd->bjkd", grad_scores, query_blocks, preferred_element_type=jnp.float32
    )
    value_part = jnp.einsum(
        "bkgqj,bqkgd->bjkd", probs_low, grad_out, preferred_element_type=jnp.float32
    )
    grad_parts = jnp.concatenate(
        [
            key_part.reshape(per_dev * nearby, BLOCK, kv_cols),
            value_part.reshape(per_dev * nearby, BLOCK, kv_cols),
        ],
        axis=-1,
    )
    owed_grads = (
        jnp.zeros((span_blocks, BLOCK, 2 * kv_cols), jnp.float32)
        .at[local_index.reshape(-1)]
        .add(grad_parts)
    )
    from_next = shifted(owed_grads[:per_dev].astype(jnp.bfloat16), "row", -1).astype(jnp.float32)
    from_prev = shifted(owed_grads[2 * per_dev :].astype(jnp.bfloat16), "row", 1).astype(
        jnp.float32
    )
    settled = owed_grads[per_dev : 2 * per_dev] + from_next + from_prev
    settled = settled.reshape(tok_rows, 2 * kv_cols)
    grad_keys = settled[:, :kv_cols].astype(jnp.bfloat16)
    grad_values = settled[:, kv_cols:].astype(jnp.bfloat16)
    contract = (((1,), (1,)), ((), ()))
    joined = jnp.concatenate([grad_query, grad_keys, grad_values], axis=1)
    partial_grad = lax.dot_general(
        joined, full_wide.reshape(-1, WIDE), contract, preferred_element_type=jnp.float32
    )
    input_grad = lax.psum_scatter(
        partial_grad.astype(jnp.bfloat16), "col", scatter_dimension=1, tiled=True
    )
    return (attended.reshape(tok_rows, -1), input_grad)


def solution(mesh):
    placed = (
        P("row", "col"),
        P("row", "col"),
        P("row", "col"),
        P("row", "col"),
        P(),
        P("row", None),
        P("row", "col"),
    )
    return jax.shard_map(
        body,
        mesh=mesh,
        in_specs=placed,
        out_specs=(P("row", "col"), P("row", "col")),
        check_vma=False,
    )
```

```python
import functools

import jax
import jax.numpy as jnp
from jax import lax
from jax.experimental import pallas as pl
from jax.experimental.pallas import tpu as pltpu
from jax.sharding import PartitionSpec as P

HEADS = 64
KV_HEADS = 8
HEAD_DIM = 128
BLOCK = 128
GROUP = HEADS // KV_HEADS
ROWS = 16
COLS = 8
TOK = 512
HALF = 256
FEAT = 1024
KV = 256
WIDE = FEAT + KV
MESH = pl.DeviceIdType.MESH
MIB = 1024 * 1024


def place():
    row, col = lax.axis_index("row"), lax.axis_index("col")
    return row, col, row // 4, (row // 2) % 2, row % 2, col // 2, col % 2


def remote(src, dst, send, recv, row, col):
    return pltpu.make_async_remote_copy(
        src_ref=src,
        dst_ref=dst,
        send_sem=send,
        recv_sem=recv,
        device_id=(row, col),
        device_id_type=MESH,
    )


BRINGS = {0: (3, 0), 1: (3, 1), 2: (1, 1), 3: (1, 0), 4: (2, 0), 5: (2, 1)}


def gather_kernel(
    x_in, wq_in, wk_in, wv_in,
    q_out, kv_out, w_out,
    xf, wf, acc, kv_buf,
    load_sem, xs, xr, xps, xpr, ws, wr, wps, wpr, cs, cr, hs, hr, out_sem, kv_sem,
):
    row, col, y, h, k, z, l = place()
    prev_row, next_row = (row + ROWS - 1) % ROWS, (row + 1) % ROWS

    def row_of(yy, hh, kk):
        return (yy * 2 + hh) * 2 + kk

    y_next, y_prev = row_of((y + 1) % 4, h, k), row_of((y + 3) % 4, h, k)
    h_pair, sibling = row_of(y, 1 - h, k), row_of(y, h, 1 - k)
    z_next, z_prev = ((z + 1) % 4) * 2 + l, ((z + 3) % 4) * 2 + l
    l_pair = z * 2 + 1 - l

    own_x, own_w = col, row // 2
    own_rows = pl.ds(k * TOK, TOK)
    loads = [
        pltpu.make_async_copy(x_in, xf.at[own_x], load_sem.at[0]),
        pltpu.make_async_copy(wq_in, wf.at[own_w, own_rows, pl.ds(0, FEAT)], load_sem.at[1]),
        pltpu.make_async_copy(wk_in, wf.at[own_w, own_rows, pl.ds(FEAT, 128)], load_sem.at[2]),
        pltpu.make_async_copy(
            wv_in, wf.at[own_w, own_rows, pl.ds(FEAT + 128, 128)], load_sem.at[3]
        ),
    ]
    for load in loads:
        load.start()

    barrier = pltpu.get_barrier_semaphore()
    peers = [
        (row, z_next), (row, z_prev), (row, l_pair),
        (y_next, col), (y_prev, col), (h_pair, col), (sibling, col),
        (prev_row, col), (next_row, col),
    ]
    for peer in peers:
        pl.semaphore_signal(barrier, inc=1, device_id=peer, device_id_type=MESH)
    pl.semaphore_wait(barrier, len(peers))
    for load in loads:
        load.wait()

    def x_piece(step, plane, half):
        slot = ((z + step) % 4) * 2 + (l + plane) % 2
        return xf.at[slot, pl.ds(half * HALF, HALF)]

    def w_piece(step, plane, half, core=None):
        slot = ((y + step) % 4) * 2 + (h + plane) % 2
        core = k if core is None else core
        return wf.at[slot, pl.ds(core * TOK + half * HALF, HALF)]

    started = []

    def x_ring(plane, kind):
        step, half = (0, (0, 1, 1, 0)[kind]) if kind < 4 else ((3, 0) if kind == 4 else (1, 1))
        ref = x_piece(step, plane, half)
        peer = z_next if kind in (0, 1, 4) else z_prev
        i = plane * 6 + kind
        copy = remote(ref, ref, xs.at[i], xr.at[i], row, peer)
        copy.start()
        started.append(copy)

    def x_got(plane, kind):
        step, half = BRINGS[kind]
        ref = x_piece(step, plane, half)
        i = plane * 6 + kind
        remote(ref, ref, xs.at[i], xr.at[i], row, z_prev).wait_recv()

    def w_ring(plane, kind):
        step, half = (0, (0, 1, 1, 0)[kind]) if kind < 4 else ((3, 0) if kind == 4 else (1, 1))
        ref = w_piece(step, plane, half)
        peer = y_next if kind in (0, 1, 4) else y_prev
        i = plane * 6 + kind
        copy = remote(ref, ref, ws.at[i], wr.at[i], peer, col)
        copy.start()
        started.append(copy)

    def w_share(step, plane, half):
        ref = w_piece(step, plane, half)
        i = (step * 2 + plane) * 2 + half
        copy = remote(ref, ref, cs.at[i], cr.at[i], sibling, col)
        copy.start()
        started.append(copy)

    def w_shared(step, plane, half):
        ref = w_piece(step, plane, half, 1 - k)
        i = (step * 2 + plane) * 2 + half
        remote(ref, ref, cs.at[i], cr.at[i], sibling, col).wait_recv()

    def w_got(plane, kind):
        step, half = BRINGS[kind]
        ref = w_piece(step, plane, half)
        i = plane * 6 + kind
        remote(ref, ref, ws.at[i], wr.at[i], y_prev, col).wait_recv()
        if kind in (0, 2):
            w_ring(plane, 4 if kind == 0 else 5)
        w_share(step, plane, half)

    for kind in (0, 2, 1, 3):
        x_ring(0, kind)
        w_ring(0, kind)
    for half in range(2):
        ref = x_piece(0, 0, half)
        copy = remote(ref, ref, xps.at[half], xpr.at[half], row, l_pair)
        copy.start()
        started.append(copy)
        ref = w_piece(0, 0, half)
        copy = remote(ref, ref, wps.at[half], wpr.at[half], h_pair, col)
        copy.start()
        started.append(copy)
        w_share(0, 0, half)

    for kind in (0, 2):
        x_got(0, kind)
        x_ring(0, 4 if kind == 0 else 5)
        w_got(0, kind)
    for half in range(2):
        ref = x_piece(0, 1, half)
        remote(ref, ref, xps.at[half], xpr.at[half], row, l_pair).wait_recv()
        for kind in ((0, 3), (1, 2))[half]:
            x_ring(1, kind)
        ref = w_piece(0, 1, half)
        remote(ref, ref, wps.at[half], wpr.at[half], h_pair, col).wait_recv()
        for kind in ((0, 3), (1, 2))[half]:
            w_ring(1, kind)
        w_share(0, 1, half)
    for kind in (1, 3, 4, 5):
        x_got(0, kind)
        w_got(0, kind)
    for kind in (0, 2):
        x_got(1, kind)
        x_ring(1, 4 if kind == 0 else 5)
        w_got(1, kind)
    for kind in (1, 3):
        x_got(1, kind)
        w_got(1, kind)
    for step in (0, 1, 3):
        for plane in range(2):
            for half in range(2):
                w_shared(step, plane, half)
    for half in range(2):
        w_shared(2, 0, half)

    late_x = ((z + 2) % 4) * 2 + 1 - l
    late_w = ((y + 2) % 4) * 2 + 1 - h

    def multiply(slot, tile):
        cols = pl.ds(pl.multiple_of(tile * 256, 256), 256)
        return jnp.dot(xf[slot], wf[slot, :, cols], preferred_element_type=jnp.float32)

    @pl.loop(0, WIDE // 256)
    def _(tile):
        acc[tile] = jnp.zeros((TOK, 256), jnp.float32)

    for slot in range(COLS):
        @pl.when((slot != late_x) & (slot != late_w))
        def _():
            @pl.loop(0, WIDE // 256)
            def _(tile):
                acc[tile] += multiply(slot, tile)

        @pl.when(slot != late_w)
        def _():
            pltpu.make_async_copy(wf.at[slot], w_out.at[slot], out_sem.at[slot]).start()

    for kind in (4, 5):
        x_got(1, kind)
        w_got(1, kind)
    for half in range(2):
        w_shared(2, 1, half)
    for slot in range(COLS):
        @pl.when(slot == late_w)
        def _():
            pltpu.make_async_copy(wf.at[slot], w_out.at[slot], out_sem.at[slot]).start()

    def finish(tile):
        acc[tile] += multiply(late_x, tile)

        @pl.when(late_w != late_x)
        def _():
            acc[tile] += multiply(late_w, tile)

        return acc[tile].astype(jnp.bfloat16)

    kv_buf[...] = finish(FEAT // 256)
    halo = [
        remote(kv_buf, kv_out.at[0], hs.at[0], hr.at[0], next_row, col),
        remote(kv_buf, kv_out.at[2], hs.at[1], hr.at[1], prev_row, col),
    ]
    for copy in halo:
        copy.start()
    own_kv = pltpu.make_async_copy(kv_buf, kv_out.at[1], kv_sem)
    own_kv.start()

    @pl.loop(0, FEAT // 256)
    def _(tile):
        cols = pl.ds(pl.multiple_of(tile * 256, 256), 256)
        q_out[:, cols] = finish(tile)

    for copy in started:
        copy.wait_send()
    for copy in halo:
        copy.wait()
    own_kv.wait()
    for slot in range(COLS):
        pltpu.make_async_copy(wf.at[slot], w_out.at[slot], out_sem.at[slot]).wait()


def gather(layer_input, w_query, w_key, w_value):
    dma = pltpu.SemaphoreType.DMA
    return pl.pallas_call(
        gather_kernel,
        name="gather_project",
        out_shape=(
            jax.ShapeDtypeStruct((TOK, FEAT), jnp.bfloat16),
            jax.ShapeDtypeStruct((3, TOK, KV), jnp.bfloat16),
            jax.ShapeDtypeStruct((COLS, FEAT, WIDE), jnp.bfloat16),
        ),
        in_specs=[pl.BlockSpec(memory_space=pl.ANY)] * 4,
        out_specs=(
            pl.BlockSpec(memory_space=pltpu.VMEM),
            pl.BlockSpec(memory_space=pl.ANY),
            pl.BlockSpec(memory_space=pl.ANY),
        ),
        scratch_shapes=[
            pltpu.VMEM((COLS, TOK, FEAT), jnp.bfloat16),
            pltpu.VMEM((COLS, FEAT, WIDE), jnp.bfloat16),
            pltpu.VMEM((WIDE // 256, TOK, 256), jnp.float32),
            pltpu.VMEM((TOK, KV), jnp.bfloat16),
            dma((4,)),
            dma((12,)), dma((12,)), dma((2,)), dma((2,)),
            dma((12,)), dma((12,)), dma((2,)), dma((2,)),
            dma((16,)), dma((16,)),
            dma((2,)), dma((2,)),
            dma((COLS,)), dma,
        ],
        compiler_params=pltpu.CompilerParams(
            collective_id=0, has_side_effects=True, vmem_limit_bytes=56 * MIB
        ),
        cost_estimate=pl.CostEstimate(
            flops=2 * TOK * 8192 * WIDE, bytes_accessed=40 * MIB, transcendentals=0
        ),
    )(layer_input, w_query, w_key, w_value)


def scatter_kernel(
    dq_in, side_in, mid_in, w_in,
    out,
    jn, wv, acc, pb, far, near, pair_out, pair_in, side_got,
    w_sem, ds, dr, fs, fr, ns, nr, ps, pr,
):
    row, col, y, h, k, z, l = place()
    prev_row, next_row = (row + ROWS - 1) % ROWS, (row + 1) % ROWS
    z_next, z_prev = ((z + 1) % 4) * 2 + l, ((z + 3) % 4) * 2 + l
    l_pair = z * 2 + 1 - l

    def slot_of(step, plane):
        return ((z + step) % 4) * 2 + (l + plane) % 2

    order = [(2, 1), (1, 1), (3, 1), (2, 0), (1, 0), (3, 0), (0, 1), (0, 0)]
    loads = {}
    for i, (step, plane) in enumerate(order):
        slot = slot_of(step, plane)
        loads[step, plane] = pltpu.make_async_copy(w_in.at[slot], wv.at[slot], w_sem.at[i])
        loads[step, plane].start()

    barrier = pltpu.get_barrier_semaphore()
    peers = [(row, z_next), (row, z_prev), (row, l_pair), (prev_row, col), (next_row, col)]
    for peer in peers:
        pl.semaphore_signal(barrier, inc=1, device_id=peer, device_id_type=MESH)
    jn[:, :FEAT] = dq_in[...]
    pl.semaphore_wait(barrier, len(peers))

    started = []

    def send(src, dst, send_sem, recv_sem, to_row, to_col):
        copy = remote(src, dst, send_sem, recv_sem, to_row, to_col)
        copy.start()
        started.append(copy)

    def got(ref, send_sem, recv_sem):
        remote(ref, ref, send_sem, recv_sem, row, z_prev).wait_recv()

    send(side_in.at[0], side_got.at[1], ds.at[0], dr.at[0], prev_row, col)
    send(side_in.at[1], side_got.at[0], ds.at[1], dr.at[1], next_row, col)

    def product(slot, tile, rows, cols):
        tall = pl.ds(pl.multiple_of(tile * 256, 256), 256)
        return lax.dot_general(
            jn[rows, cols], wv[slot, tall, cols], (((1,), (1,)), ((), ())),
            preferred_element_type=jnp.float32,
        )

    every = pl.ds(0, WIDE)

    def fill(target, step, plane, rows, extra=None):
        slot = slot_of(step, plane)

        @pl.loop(0, FEAT // 256)
        def _(tile):
            cols = pl.ds(pl.multiple_of(tile * 256, 256), 256)
            value = product(slot, tile, rows, every)
            if extra is not None:
                value += extra[:, cols].astype(jnp.float32)
            target[rows, cols] = value.astype(jnp.bfloat16)

    low, high = pl.ds(0, HALF), pl.ds(HALF, HALF)
    both = pl.ds(0, TOK)

    loads[2, 1].wait()

    @pl.loop(0, FEAT // 256)
    def _(tile):
        acc[tile] = product(slot_of(2, 1), tile, both, pl.ds(0, FEAT))

    for i in range(2):
        got(side_got.at[1 - i], ds.at[i], dr.at[i])
    jn[:, FEAT:] = (
        mid_in[...] + side_got[0].astype(jnp.float32) + side_got[1].astype(jnp.float32)
    ).astype(jnp.bfloat16)

    @pl.loop(0, FEAT // 256)
    def _(tile):
        cols = pl.ds(pl.multiple_of(tile * 256, 256), 256)
        value = acc[tile] + product(slot_of(2, 1), tile, both, pl.ds(FEAT, KV))
        pb[1, 0, :, cols] = value.astype(jnp.bfloat16)

    def send_far(plane):
        i = plane * 2
        send(pb.at[plane, 0, low], far.at[plane, 0], fs.at[i], fr.at[i], row, z_next)
        send(pb.at[plane, 0, high], far.at[plane, 1], fs.at[i + 1], fr.at[i + 1], row, z_prev)

    def near_half(plane, way, half, extra=None):
        step = 1 if way == 0 else 3
        rows = low if half == 0 else high
        fill(pb.at[plane, 1 + way], step, plane, rows, extra)
        i = (plane * 2 + way) * 2 + half
        send(
            pb.at[plane, 1 + way, rows], near.at[plane, way, rows], ns.at[i], nr.at[i],
            row, z_next if way == 0 else z_prev,
        )

    def near_free(plane):
        near_half(plane, 0, 1)
        near_half(plane, 1, 0)

    def near_joined(plane):
        i = plane * 2
        got(far.at[plane, 0], fs.at[i], fr.at[i])
        near_half(plane, 0, 0, far.at[plane, 0])
        got(far.at[plane, 1], fs.at[i + 1], fr.at[i + 1])
        near_half(plane, 1, 1, far.at[plane, 1])

    send_far(1)
    loads[1, 1].wait()
    loads[3, 1].wait()
    near_free(1)
    loads[2, 0].wait()
    fill(pb.at[0, 0], 2, 0, both)
    send_far(0)
    near_joined(1)
    loads[1, 0].wait()
    loads[3, 0].wait()
    near_free(0)
    near_joined(0)

    def own(plane):
        loads[0, plane].wait()

        @pl.loop(0, FEAT // 256)
        def _(tile):
            acc[tile] = product(slot_of(0, plane), tile, both, every)

    def near_wait(plane, half):
        rows = low if half == 0 else high
        for way in range(2):
            i = (plane * 2 + way) * 2 + half
            got(near.at[plane, way, rows], ns.at[i], nr.at[i])

    own(1)
    for half in range(2):
        near_wait(1, half)
        rows = low if half == 0 else high

        @pl.loop(0, FEAT // 256)
        def _(tile):
            cols = pl.ds(pl.multiple_of(tile * 256, 256), 256)
            value = acc[tile, rows] + near[1, 0, rows, cols].astype(jnp.float32)
            value += near[1, 1, rows, cols].astype(jnp.float32)
            pair_out[rows, cols] = value.astype(jnp.bfloat16)

        send(pair_out.at[rows], pair_in.at[rows], ps.at[half], pr.at[half], row, l_pair)
    own(0)
    for half in range(2):
        near_wait(0, half)
        rows = low if half == 0 else high
        got(pair_in.at[rows], ps.at[half], pr.at[half])

        @pl.loop(0, FEAT // 256)
        def _(tile):
            cols = pl.ds(pl.multiple_of(tile * 256, 256), 256)
            value = acc[tile, rows] + near[0, 0, rows, cols].astype(jnp.float32)
            value += near[0, 1, rows, cols].astype(jnp.float32)
            value += pair_in[rows, cols].astype(jnp.float32)
            out[rows, cols] = value.astype(jnp.bfloat16)

    for copy in started:
        copy.wait_send()


def scatter(grad_query, side, mid, full_wide):
    dma = pltpu.SemaphoreType.DMA
    vmem = pl.BlockSpec(memory_space=pltpu.VMEM)
    low = jnp.bfloat16
    return pl.pallas_call(
        scatter_kernel,
        name="project_scatter",
        out_shape=jax.ShapeDtypeStruct((TOK, FEAT), low),
        in_specs=[vmem, vmem, vmem, pl.BlockSpec(memory_space=pl.ANY)],
        out_specs=vmem,
        scratch_shapes=[
            pltpu.VMEM((TOK, WIDE), low),
            pltpu.VMEM((COLS, FEAT, WIDE), low),
            pltpu.VMEM((FEAT // 256, TOK, 256), jnp.float32),
            pltpu.VMEM((2, 3, TOK, FEAT), low),
            pltpu.VMEM((2, 2, HALF, FEAT), low),
            pltpu.VMEM((2, 2, TOK, FEAT), low),
            pltpu.VMEM((TOK, FEAT), low),
            pltpu.VMEM((TOK, FEAT), low),
            pltpu.VMEM((2, TOK, KV), low),
            dma((COLS,)),
            dma((2,)), dma((2,)),
            dma((4,)), dma((4,)),
            dma((8,)), dma((8,)),
            dma((2,)), dma((2,)),
        ],
        compiler_params=pltpu.CompilerParams(
            collective_id=1, has_side_effects=True, vmem_limit_bytes=56 * MIB
        ),
        cost_estimate=pl.CostEstimate(
            flops=2 * TOK * 8192 * WIDE, bytes_accessed=24 * MIB, transcendentals=0
        ),
    )(grad_query, side, mid, full_wide)


def body(layer_input, w_query, w_key, w_value, counts, pattern, cotangent):
    score_scale = HEAD_DIM ** (-0.5)
    group_size = HEADS // KV_HEADS
    tok_rows = layer_input.shape[0]
    per_dev = tok_rows // BLOCK
    block_count = per_dev * lax.axis_size("row")
    myself = lax.axis_index("row")
    query, source, full_wide = gather(layer_input, w_query, w_key, w_value)
    kv_heads = 1
    kv_cols = 128
    first_block = myself * per_dev - per_dev
    span_blocks = 3 * per_dev
    nearby = pattern.shape[1]
    local_index = jnp.mod(pattern - first_block, block_count)
    stacked = source.reshape(span_blocks, BLOCK, 2 * kv_cols)
    picked = jnp.take(stacked, local_index, axis=0).reshape(
        per_dev, nearby * BLOCK, 2, kv_heads, HEAD_DIM
    )
    key_blocks = picked[:, :, 0]
    value_blocks = picked[:, :, 1]
    positions = jnp.arange(BLOCK, dtype=jnp.int32)
    key_counts = jnp.take(counts, pattern, axis=0)
    key_live = (positions[None, None, :] < key_counts[:, :, None]).reshape(per_dev, nearby * BLOCK)
    own_counts = lax.dynamic_slice_in_dim(counts, myself * per_dev, per_dev)
    query_live = (positions[None, :] < own_counts[:, None])[:, :, None, None, None]
    query_blocks = query.reshape(per_dev, BLOCK, kv_heads, group_size, HEAD_DIM)
    scores = (
        jnp.einsum(
            "bqkgd,bjkd->bkgqj", query_blocks, key_blocks, preferred_element_type=jnp.float32
        )
        * score_scale
    )
    scores = jnp.where(key_live[:, None, None, None, :], scores, -1e30)
    score_max = jnp.max(scores, axis=-1, keepdims=True)
    exponent = jnp.exp(scores - score_max)
    prob_full = exponent / jnp.sum(exponent, axis=-1, keepdims=True)
    probs_low = prob_full.astype(jnp.bfloat16)
    mixed_out = jnp.einsum(
        "bkgqj,bjkd->bqkgd", probs_low, value_blocks, preferred_element_type=jnp.float32
    )
    attended = (mixed_out * query_live.astype(jnp.float32)).astype(jnp.bfloat16)
    grad_out = cotangent.reshape(
        per_dev, BLOCK, kv_heads, group_size, HEAD_DIM
    ) * query_live.astype(jnp.bfloat16)
    row_delta = jnp.einsum(
        "bqkgd,bqkgd->bkgq", grad_out, attended, preferred_element_type=jnp.float32
    )
    grad_probs = jnp.einsum(
        "bqkgd,bjkd->bkgqj", grad_out, value_blocks, preferred_element_type=jnp.float32
    )
    grad_scores = (prob_full * (grad_probs - row_delta[..., None]) * score_scale).astype(
        jnp.bfloat16
    )
    grad_query = jnp.einsum(
        "bkgqj,bjkd->bqkgd", grad_scores, key_blocks, preferred_element_type=jnp.float32
    )
    grad_query = grad_query.astype(jnp.bfloat16).reshape(tok_rows, -1)
    key_part = jnp.einsum(
        "bkgqj,bqkgd->bjkd", grad_scores, query_blocks, preferred_element_type=jnp.float32
    )
    value_part = jnp.einsum(
        "bkgqj,bqkgd->bjkd", probs_low, grad_out, preferred_element_type=jnp.float32
    )
    grad_parts = jnp.concatenate(
        [
            key_part.reshape(per_dev * nearby, BLOCK, kv_cols),
            value_part.reshape(per_dev * nearby, BLOCK, kv_cols),
        ],
        axis=-1,
    )
    owed_grads = (
        jnp.zeros((span_blocks, BLOCK, 2 * kv_cols), jnp.float32)
        .at[local_index.reshape(-1)]
        .add(grad_parts)
    )
    side = jnp.stack([owed_grads[:per_dev], owed_grads[2 * per_dev :]])
    side = side.astype(jnp.bfloat16).reshape(2, TOK, KV)
    mid = owed_grads[per_dev : 2 * per_dev].reshape(TOK, KV)
    input_grad = scatter(grad_query, side, mid, full_wide)
    return (attended.reshape(tok_rows, -1), input_grad)


def solution(mesh):
    placed = (
        P("row", "col"),
        P("row", "col"),
        P("row", "col"),
        P("row", "col"),
        P(),
        P("row", None),
        P("row", "col"),
    )
    return jax.shard_map(
        body,
        mesh=mesh,
        in_specs=placed,
        out_specs=(P("row", "col"), P("row", "col")),
        check_vma=False,
    )
```

```python
import functools

import jax
import jax.numpy as jnp
from jax import lax
from jax.experimental import pallas as pl
from jax.experimental.pallas import tpu as pltpu
from jax.sharding import PartitionSpec as P

HEADS = 64
KV_HEADS = 8
HEAD_DIM = 128
BLOCK = 128
GROUP = HEADS // KV_HEADS
ROWS = 16
COLS = 8
TOK = 512
HALF = 256
FEAT = 1024
KV = 256
WIDE = FEAT + KV
MESH = pl.DeviceIdType.MESH
MIB = 1024 * 1024


def place():
    row, col = lax.axis_index("row"), lax.axis_index("col")
    return row, col, row // 4, (row // 2) % 2, row % 2, col // 2, col % 2


def remote(src, dst, send, recv, row, col):
    return pltpu.make_async_remote_copy(
        src_ref=src,
        dst_ref=dst,
        send_sem=send,
        recv_sem=recv,
        device_id=(row, col),
        device_id_type=MESH,
    )


BRINGS = {0: (3, 0), 1: (3, 1), 2: (1, 1), 3: (1, 0), 4: (2, 0), 5: (2, 1)}


def gather_kernel(
    x_in, wq_in, wk_in, wv_in,
    q_out, kv_out, w_out,
    xf, wf, acc, kv_buf,
    load_sem, xs, xr, xps, xpr, ws, wr, wps, wpr, cs, cr, hs, hr, out_sem, kv_sem,
):
    row, col, y, h, k, z, l = place()
    prev_row, next_row = (row + ROWS - 1) % ROWS, (row + 1) % ROWS

    def row_of(yy, hh, kk):
        return (yy * 2 + hh) * 2 + kk

    y_next, y_prev = row_of((y + 1) % 4, h, k), row_of((y + 3) % 4, h, k)
    h_pair, sibling = row_of(y, 1 - h, k), row_of(y, h, 1 - k)
    z_next, z_prev = ((z + 1) % 4) * 2 + l, ((z + 3) % 4) * 2 + l
    l_pair = z * 2 + 1 - l

    own_x, own_w = col, row // 2
    own_rows = pl.ds(k * TOK, TOK)
    loads = [
        pltpu.make_async_copy(x_in, xf.at[own_x], load_sem.at[0]),
        pltpu.make_async_copy(wq_in, wf.at[own_w, own_rows, pl.ds(0, FEAT)], load_sem.at[1]),
        pltpu.make_async_copy(wk_in, wf.at[own_w, own_rows, pl.ds(FEAT, 128)], load_sem.at[2]),
        pltpu.make_async_copy(
            wv_in, wf.at[own_w, own_rows, pl.ds(FEAT + 128, 128)], load_sem.at[3]
        ),
    ]
    for load in loads:
        load.start()

    barrier = pltpu.get_barrier_semaphore()
    peers = [
        (row, z_next), (row, z_prev), (row, l_pair),
        (y_next, col), (y_prev, col), (h_pair, col), (sibling, col),
        (prev_row, col), (next_row, col),
    ]
    for peer in peers:
        pl.semaphore_signal(barrier, inc=1, device_id=peer, device_id_type=MESH)
    pl.semaphore_wait(barrier, len(peers))
    for load in loads:
        load.wait()

    def x_piece(step, plane, half):
        slot = ((z + step) % 4) * 2 + (l + plane) % 2
        return xf.at[slot, pl.ds(half * HALF, HALF)]

    def w_piece(step, plane, half, core=None):
        slot = ((y + step) % 4) * 2 + (h + plane) % 2
        core = k if core is None else core
        return wf.at[slot, pl.ds(core * TOK + half * HALF, HALF)]

    started = []

    def x_ring(plane, kind):
        step, half = (0, (0, 1, 1, 0)[kind]) if kind < 4 else ((3, 0) if kind == 4 else (1, 1))
        ref = x_piece(step, plane, half)
        peer = z_next if kind in (0, 1, 4) else z_prev
        i = plane * 6 + kind
        copy = remote(ref, ref, xs.at[i], xr.at[i], row, peer)
        copy.start()
        started.append(copy)

    def x_got(plane, kind):
        step, half = BRINGS[kind]
        ref = x_piece(step, plane, half)
        i = plane * 6 + kind
        remote(ref, ref, xs.at[i], xr.at[i], row, z_prev).wait_recv()

    def w_ring(plane, kind):
        step, half = (0, (0, 1, 1, 0)[kind]) if kind < 4 else ((3, 0) if kind == 4 else (1, 1))
        ref = w_piece(step, plane, half)
        peer = y_next if kind in (0, 1, 4) else y_prev
        i = plane * 6 + kind
        copy = remote(ref, ref, ws.at[i], wr.at[i], peer, col)
        copy.start()
        started.append(copy)

    def w_share(step, plane, half):
        ref = w_piece(step, plane, half)
        i = (step * 2 + plane) * 2 + half
        copy = remote(ref, ref, cs.at[i], cr.at[i], sibling, col)
        copy.start()
        started.append(copy)

    def w_shared(step, plane, half):
        ref = w_piece(step, plane, half, 1 - k)
        i = (step * 2 + plane) * 2 + half
        remote(ref, ref, cs.at[i], cr.at[i], sibling, col).wait_recv()

    def w_got(plane, kind):
        step, half = BRINGS[kind]
        ref = w_piece(step, plane, half)
        i = plane * 6 + kind
        remote(ref, ref, ws.at[i], wr.at[i], y_prev, col).wait_recv()
        if kind in (0, 2):
            w_ring(plane, 4 if kind == 0 else 5)
        w_share(step, plane, half)

    for kind in (0, 2, 1, 3):
        x_ring(0, kind)
        w_ring(0, kind)
    for half in range(2):
        ref = x_piece(0, 0, half)
        copy = remote(ref, ref, xps.at[half], xpr.at[half], row, l_pair)
        copy.start()
        started.append(copy)
        ref = w_piece(0, 0, half)
        copy = remote(ref, ref, wps.at[half], wpr.at[half], h_pair, col)
        copy.start()
        started.append(copy)
        w_share(0, 0, half)

    for kind in (0, 2):
        x_got(0, kind)
        x_ring(0, 4 if kind == 0 else 5)
        w_got(0, kind)
    for half in range(2):
        ref = x_piece(0, 1, half)
        remote(ref, ref, xps.at[half], xpr.at[half], row, l_pair).wait_recv()
        for kind in ((0, 3), (1, 2))[half]:
            x_ring(1, kind)
        ref = w_piece(0, 1, half)
        remote(ref, ref, wps.at[half], wpr.at[half], h_pair, col).wait_recv()
        for kind in ((0, 3), (1, 2))[half]:
            w_ring(1, kind)
        w_share(0, 1, half)
    for kind in (1, 3, 4, 5):
        x_got(0, kind)
        w_got(0, kind)
    for kind in (0, 2):
        x_got(1, kind)
        x_ring(1, 4 if kind == 0 else 5)
        w_got(1, kind)
    for kind in (1, 3):
        x_got(1, kind)
        w_got(1, kind)
    for step in (0, 1, 3):
        for plane in range(2):
            for half in range(2):
                w_shared(step, plane, half)
    for half in range(2):
        w_shared(2, 0, half)

    late_x = ((z + 2) % 4) * 2 + 1 - l
    late_w = ((y + 2) % 4) * 2 + 1 - h

    def multiply(slot, tile):
        cols = pl.ds(pl.multiple_of(tile * 256, 256), 256)
        return jnp.dot(xf[slot], wf[slot, :, cols], preferred_element_type=jnp.float32)

    @pl.loop(0, WIDE // 256)
    def _(tile):
        acc[tile] = jnp.zeros((TOK, 256), jnp.float32)

    for slot in range(COLS):
        @pl.when((slot != late_x) & (slot != late_w))
        def _():
            @pl.loop(0, WIDE // 256)
            def _(tile):
                acc[tile] += multiply(slot, tile)

        @pl.when(slot != late_w)
        def _():
            pltpu.make_async_copy(wf.at[slot], w_out.at[slot], out_sem.at[slot]).start()

    for kind in (4, 5):
        x_got(1, kind)
        w_got(1, kind)
    for half in range(2):
        w_shared(2, 1, half)
    for slot in range(COLS):
        @pl.when(slot == late_w)
        def _():
            pltpu.make_async_copy(wf.at[slot], w_out.at[slot], out_sem.at[slot]).start()

    def finish(tile):
        acc[tile] += multiply(late_x, tile)

        @pl.when(late_w != late_x)
        def _():
            acc[tile] += multiply(late_w, tile)

        return acc[tile].astype(jnp.bfloat16)

    kv_buf[...] = finish(FEAT // 256)
    halo = [
        remote(kv_buf, kv_out.at[0], hs.at[0], hr.at[0], next_row, col),
        remote(kv_buf, kv_out.at[2], hs.at[1], hr.at[1], prev_row, col),
    ]
    for copy in halo:
        copy.start()
    own_kv = pltpu.make_async_copy(kv_buf, kv_out.at[1], kv_sem)
    own_kv.start()

    @pl.loop(0, FEAT // 256)
    def _(tile):
        cols = pl.ds(pl.multiple_of(tile * 256, 256), 256)
        q_out[:, cols] = finish(tile)

    for copy in started:
        copy.wait_send()
    for copy in halo:
        copy.wait()
    own_kv.wait()
    for slot in range(COLS):
        pltpu.make_async_copy(wf.at[slot], w_out.at[slot], out_sem.at[slot]).wait()


def gather(layer_input, w_query, w_key, w_value):
    dma = pltpu.SemaphoreType.DMA
    return pl.pallas_call(
        gather_kernel,
        name="gather_project",
        out_shape=(
            jax.ShapeDtypeStruct((TOK, FEAT), jnp.bfloat16),
            jax.ShapeDtypeStruct((3, TOK, KV), jnp.bfloat16),
            jax.ShapeDtypeStruct((COLS, FEAT, WIDE), jnp.bfloat16),
        ),
        in_specs=[pl.BlockSpec(memory_space=pl.ANY)] * 4,
        out_specs=(
            pl.BlockSpec(memory_space=pltpu.VMEM),
            pl.BlockSpec(memory_space=pl.ANY),
            pl.BlockSpec(memory_space=pl.ANY),
        ),
        scratch_shapes=[
            pltpu.VMEM((COLS, TOK, FEAT), jnp.bfloat16),
            pltpu.VMEM((COLS, FEAT, WIDE), jnp.bfloat16),
            pltpu.VMEM((WIDE // 256, TOK, 256), jnp.float32),
            pltpu.VMEM((TOK, KV), jnp.bfloat16),
            dma((4,)),
            dma((12,)), dma((12,)), dma((2,)), dma((2,)),
            dma((12,)), dma((12,)), dma((2,)), dma((2,)),
            dma((16,)), dma((16,)),
            dma((2,)), dma((2,)),
            dma((COLS,)), dma,
        ],
        compiler_params=pltpu.CompilerParams(
            collective_id=0, has_side_effects=True, vmem_limit_bytes=56 * MIB
        ),
        cost_estimate=pl.CostEstimate(
            flops=2 * TOK * 8192 * WIDE, bytes_accessed=40 * MIB, transcendentals=0
        ),
    )(layer_input, w_query, w_key, w_value)


def scatter_kernel(
    dq_in, side_in, mid_in, w_in,
    out,
    jn, wv, acc, pb, far, near, pair_out, pair_in, side_got,
    w_sem, ds, dr, fs, fr, ns, nr, ps, pr,
):
    row, col, y, h, k, z, l = place()
    prev_row, next_row = (row + ROWS - 1) % ROWS, (row + 1) % ROWS
    z_next, z_prev = ((z + 1) % 4) * 2 + l, ((z + 3) % 4) * 2 + l
    l_pair = z * 2 + 1 - l

    def slot_of(step, plane):
        return ((z + step) % 4) * 2 + (l + plane) % 2

    order = [(2, 1), (1, 1), (3, 1), (2, 0), (1, 0), (3, 0), (0, 1), (0, 0)]
    loads = {}
    for i, (step, plane) in enumerate(order):
        slot = slot_of(step, plane)
        loads[step, plane] = pltpu.make_async_copy(w_in.at[slot], wv.at[slot], w_sem.at[i])
        loads[step, plane].start()

    barrier = pltpu.get_barrier_semaphore()
    peers = [(row, z_next), (row, z_prev), (row, l_pair), (prev_row, col), (next_row, col)]
    for peer in peers:
        pl.semaphore_signal(barrier, inc=1, device_id=peer, device_id_type=MESH)
    jn[:, :FEAT] = dq_in[...]
    pl.semaphore_wait(barrier, len(peers))

    started = []

    def send(src, dst, send_sem, recv_sem, to_row, to_col):
        copy = remote(src, dst, send_sem, recv_sem, to_row, to_col)
        copy.start()
        started.append(copy)

    def got(ref, send_sem, recv_sem):
        remote(ref, ref, send_sem, recv_sem, row, z_prev).wait_recv()

    send(side_in.at[0], side_got.at[1], ds.at[0], dr.at[0], prev_row, col)
    send(side_in.at[1], side_got.at[0], ds.at[1], dr.at[1], next_row, col)

    def product(slot, tile, rows, cols):
        tall = pl.ds(pl.multiple_of(tile * 256, 256), 256)
        return lax.dot_general(
            jn[rows, cols], wv[slot, tall, cols], (((1,), (1,)), ((), ())),
            preferred_element_type=jnp.float32,
        )

    every = pl.ds(0, WIDE)

    def fill(target, step, plane, rows, extra=None):
        slot = slot_of(step, plane)

        @pl.loop(0, FEAT // 256)
        def _(tile):
            cols = pl.ds(pl.multiple_of(tile * 256, 256), 256)
            value = product(slot, tile, rows, every)
            if extra is not None:
                value += extra[:, cols].astype(jnp.float32)
            target[rows, cols] = value.astype(jnp.bfloat16)

    low, high = pl.ds(0, HALF), pl.ds(HALF, HALF)
    both = pl.ds(0, TOK)

    loads[2, 1].wait()

    @pl.loop(0, FEAT // 256)
    def _(tile):
        acc[tile] = product(slot_of(2, 1), tile, both, pl.ds(0, FEAT))

    for i in range(2):
        got(side_got.at[1 - i], ds.at[i], dr.at[i])
    jn[:, FEAT:] = (
        mid_in[...] + side_got[0].astype(jnp.float32) + side_got[1].astype(jnp.float32)
    ).astype(jnp.bfloat16)

    @pl.loop(0, FEAT // 256)
    def _(tile):
        cols = pl.ds(pl.multiple_of(tile * 256, 256), 256)
        value = acc[tile] + product(slot_of(2, 1), tile, both, pl.ds(FEAT, KV))
        pb[1, 0, :, cols] = value.astype(jnp.bfloat16)

    def send_far(plane):
        i = plane * 2
        send(pb.at[plane, 0, low], far.at[plane, 0], fs.at[i], fr.at[i], row, z_next)
        send(pb.at[plane, 0, high], far.at[plane, 1], fs.at[i + 1], fr.at[i + 1], row, z_prev)

    def near_half(plane, way, half, extra=None):
        step = 1 if way == 0 else 3
        rows = low if half == 0 else high
        fill(pb.at[plane, 1 + way], step, plane, rows, extra)
        i = (plane * 2 + way) * 2 + half
        send(
            pb.at[plane, 1 + way, rows], near.at[plane, way, rows], ns.at[i], nr.at[i],
            row, z_next if way == 0 else z_prev,
        )

    def near_free(plane):
        near_half(plane, 0, 1)
        near_half(plane, 1, 0)

    def near_joined(plane):
        i = plane * 2
        got(far.at[plane, 0], fs.at[i], fr.at[i])
        near_half(plane, 0, 0, far.at[plane, 0])
        got(far.at[plane, 1], fs.at[i + 1], fr.at[i + 1])
        near_half(plane, 1, 1, far.at[plane, 1])

    send_far(1)
    loads[1, 1].wait()
    loads[3, 1].wait()
    near_free(1)
    loads[2, 0].wait()
    fill(pb.at[0, 0], 2, 0, both)
    send_far(0)
    near_joined(1)
    loads[1, 0].wait()
    loads[3, 0].wait()
    near_free(0)
    near_joined(0)

    def own(plane):
        loads[0, plane].wait()

        @pl.loop(0, FEAT // 256)
        def _(tile):
            acc[tile] = product(slot_of(0, plane), tile, both, every)

    def near_wait(plane, half):
        rows = low if half == 0 else high
        for way in range(2):
            i = (plane * 2 + way) * 2 + half
            got(near.at[plane, way, rows], ns.at[i], nr.at[i])

    own(1)
    for half in range(2):
        near_wait(1, half)
        rows = low if half == 0 else high

        @pl.loop(0, FEAT // 256)
        def _(tile):
            cols = pl.ds(pl.multiple_of(tile * 256, 256), 256)
            value = acc[tile, rows] + near[1, 0, rows, cols].astype(jnp.float32)
            value += near[1, 1, rows, cols].astype(jnp.float32)
            pair_out[rows, cols] = value.astype(jnp.bfloat16)

        send(pair_out.at[rows], pair_in.at[rows], ps.at[half], pr.at[half], row, l_pair)
    own(0)
    for half in range(2):
        near_wait(0, half)
        rows = low if half == 0 else high
        got(pair_in.at[rows], ps.at[half], pr.at[half])

        @pl.loop(0, FEAT // 256)
        def _(tile):
            cols = pl.ds(pl.multiple_of(tile * 256, 256), 256)
            value = acc[tile, rows] + near[0, 0, rows, cols].astype(jnp.float32)
            value += near[0, 1, rows, cols].astype(jnp.float32)
            value += pair_in[rows, cols].astype(jnp.float32)
            out[rows, cols] = value.astype(jnp.bfloat16)

    for copy in started:
        copy.wait_send()


def scatter(grad_query, side, mid, full_wide):
    dma = pltpu.SemaphoreType.DMA
    vmem = pl.BlockSpec(memory_space=pltpu.VMEM)
    low = jnp.bfloat16
    return pl.pallas_call(
        scatter_kernel,
        name="project_scatter",
        out_shape=jax.ShapeDtypeStruct((TOK, FEAT), low),
        in_specs=[vmem, vmem, vmem, pl.BlockSpec(memory_space=pl.ANY)],
        out_specs=vmem,
        scratch_shapes=[
            pltpu.VMEM((TOK, WIDE), low),
            pltpu.VMEM((COLS, FEAT, WIDE), low),
            pltpu.VMEM((FEAT // 256, TOK, 256), jnp.float32),
            pltpu.VMEM((2, 3, TOK, FEAT), low),
            pltpu.VMEM((2, 2, HALF, FEAT), low),
            pltpu.VMEM((2, 2, TOK, FEAT), low),
            pltpu.VMEM((TOK, FEAT), low),
            pltpu.VMEM((TOK, FEAT), low),
            pltpu.VMEM((2, TOK, KV), low),
            dma((COLS,)),
            dma((2,)), dma((2,)),
            dma((4,)), dma((4,)),
            dma((8,)), dma((8,)),
            dma((2,)), dma((2,)),
        ],
        compiler_params=pltpu.CompilerParams(
            collective_id=1, has_side_effects=True, vmem_limit_bytes=56 * MIB
        ),
        cost_estimate=pl.CostEstimate(
            flops=2 * TOK * 8192 * WIDE, bytes_accessed=24 * MIB, transcendentals=0
        ),
    )(grad_query, side, mid, full_wide)


def attend_kernel(
    pattern, counts, q_in, cot_in, kv_in,
    out, dq_out, side_out, mid_out,
    owed,
):
    block = pl.program_id(0)
    per_dev = TOK // BLOCK
    block_count = ROWS * per_dev
    first = lax.axis_index("row") * per_dev
    scale = HEAD_DIM ** (-0.5)
    pair = 2 * HEAD_DIM

    @pl.when(block == 0)
    def _():
        owed[...] = jnp.zeros_like(owed)

    chosen = [pattern[block, i] for i in range(4)]
    local = [(b - first + per_dev + block_count) % block_count for b in chosen]
    keys = jnp.concatenate([kv_in[i, :, :HEAD_DIM] for i in local], axis=0)
    values = jnp.concatenate([kv_in[i, :, HEAD_DIM:] for i in local], axis=0)
    keys_t, values_t = keys.T, values.T
    spot = lax.broadcasted_iota(jnp.int32, (BLOCK, pair), 0)
    live = jnp.concatenate([spot < counts[b] for b in chosen], axis=0)
    own_count = counts[first + block]
    lane = lax.broadcasted_iota(jnp.int32, (HEAD_DIM, pair), 1)
    query_live = jnp.where(lane % BLOCK < own_count, 1.0, 0.0)
    row_live = lax.broadcasted_iota(jnp.int32, (BLOCK, HEAD_DIM), 0) < own_count
    row_live = jnp.where(row_live, 1.0, 0.0).astype(jnp.bfloat16)

    def heads(ref, start, mask=None):
        parts = [ref[:, start + i * HEAD_DIM : start + (i + 1) * HEAD_DIM] for i in range(2)]
        if mask is not None:
            parts = [part * mask for part in parts]
        return jnp.concatenate(parts, axis=0)

    def dot(a, b, dims):
        return lax.dot_general(a, b, (dims, ((), ())), preferred_element_type=jnp.float32)

    def put(ref, start, both):
        low = both.astype(jnp.bfloat16)
        for i in range(2):
            cols = slice(start + i * HEAD_DIM, start + (i + 1) * HEAD_DIM)
            ref[:, cols] = low[:, i * HEAD_DIM : (i + 1) * HEAD_DIM].T

    grad_keys = grad_values = None
    for start in range(0, FEAT, pair):
        query = heads(q_in, start)
        grad_out = heads(cot_in, start, row_live)
        raw = jnp.where(live, dot(keys, query, ((1,), (1,))), -1e30)
        top = jnp.max(raw, axis=0, keepdims=True)
        power = jnp.exp((raw - top) * scale)
        probs = power * (1.0 / jnp.sum(power, axis=0, keepdims=True))
        probs_low = probs.astype(jnp.bfloat16)
        put(out, start, dot(values_t, probs_low, ((1,), (0,))) * query_live)
        grad_probs = dot(values, grad_out, ((1,), (1,)))
        delta = jnp.sum(probs_low.astype(jnp.float32) * grad_probs, axis=0, keepdims=True)
        grad_scores = (probs * (grad_probs - delta) * scale).astype(jnp.bfloat16)
        put(dq_out, start, dot(keys_t, grad_scores, ((1,), (0,))))
        key_part = dot(grad_scores, query, ((1,), (0,)))
        value_part = dot(probs_low, grad_out, ((1,), (0,)))
        grad_keys = key_part if grad_keys is None else grad_keys + key_part
        grad_values = value_part if grad_values is None else grad_values + value_part

    for i, spot in enumerate(local):
        rows = slice(i * BLOCK, (i + 1) * BLOCK)
        owed[spot, :, :HEAD_DIM] += grad_keys[rows]
        owed[spot, :, HEAD_DIM:] += grad_values[rows]

    @pl.when(block == per_dev - 1)
    def _():
        for i in range(per_dev):
            rows = slice(i * BLOCK, (i + 1) * BLOCK)
            side_out[0, rows] = owed[i].astype(jnp.bfloat16)
            mid_out[rows] = owed[per_dev + i]
            side_out[1, rows] = owed[2 * per_dev + i].astype(jnp.bfloat16)


def attend(pattern, counts, query, cotangent, source):
    per_dev = TOK // BLOCK
    tokens = pl.BlockSpec((BLOCK, FEAT), lambda b: (b, 0))
    smem = pl.BlockSpec(memory_space=pltpu.SMEM)
    low = jnp.bfloat16
    return pl.pallas_call(
        attend_kernel,
        name="attend",
        grid=(per_dev,),
        out_shape=(
            jax.ShapeDtypeStruct((TOK, FEAT), low),
            jax.ShapeDtypeStruct((TOK, FEAT), low),
            jax.ShapeDtypeStruct((2, TOK, KV), low),
            jax.ShapeDtypeStruct((TOK, KV), jnp.float32),
        ),
        in_specs=[
            smem, smem, tokens, tokens,
            pl.BlockSpec((3 * per_dev, BLOCK, KV), lambda b: (0, 0, 0)),
        ],
        out_specs=(
            tokens, tokens,
            pl.BlockSpec((2, TOK, KV), lambda b: (0, 0, 0)),
            pl.BlockSpec((TOK, KV), lambda b: (0, 0)),
        ),
        scratch_shapes=[pltpu.VMEM((3 * per_dev, BLOCK, KV), jnp.float32)],
        compiler_params=pltpu.CompilerParams(vmem_limit_bytes=40 * MIB),
    )(pattern, counts, query, cotangent, source.reshape(3 * per_dev, BLOCK, KV))


def body(layer_input, w_query, w_key, w_value, counts, pattern, cotangent):
    query, source, full_wide = gather(layer_input, w_query, w_key, w_value)
    attended, grad_query, side, mid = attend(pattern, counts, query, cotangent, source)
    input_grad = scatter(grad_query, side, mid, full_wide)
    return attended, input_grad


def solution(mesh):
    placed = (
        P("row", "col"),
        P("row", "col"),
        P("row", "col"),
        P("row", "col"),
        P(),
        P("row", None),
        P("row", "col"),
    )
    return jax.shard_map(
        body,
        mesh=mesh,
        in_specs=placed,
        out_specs=(P("row", "col"), P("row", "col")),
        check_vma=False,
    )
```

```python
import functools

import jax
import jax.numpy as jnp
from jax import lax
from jax.experimental import pallas as pl
from jax.experimental.pallas import tpu as pltpu
from jax.sharding import PartitionSpec as P

HEADS = 64
KV_HEADS = 8
HEAD_DIM = 128
BLOCK = 128
GROUP = HEADS // KV_HEADS
ROWS = 16
COLS = 8
TOK = 512
HALF = 256
FEAT = 1024
KV = 256
WIDE = FEAT + KV
MESH = pl.DeviceIdType.MESH
MIB = 1024 * 1024


def place():
    row, col = lax.axis_index("row"), lax.axis_index("col")
    return row, col, row // 4, (row // 2) % 2, row % 2, col // 2, col % 2


def remote(src, dst, send, recv, row, col):
    return pltpu.make_async_remote_copy(
        src_ref=src,
        dst_ref=dst,
        send_sem=send,
        recv_sem=recv,
        device_id=(row, col),
        device_id_type=MESH,
    )


FAR = 64
NEAR_KINDS = {
    0: (1, 0, 0, HALF), 1: (1, 0, HALF, HALF), 2: (3, 0, HALF, HALF), 3: (3, 0, 0, HALF),
    4: (1, 3, 0, HALF), 5: (3, 1, HALF, HALF),
}
FEW_KINDS = {
    **NEAR_KINDS, 4: (1, 3, 0, FAR), 5: (3, 1, FAR, FAR), 6: (1, 0, 0, TOK), 7: (3, 0, 0, TOK),
}
ALL_COLS, Q_COLS, KV_COLS = (0, WIDE), (0, FEAT), (FEAT, KV)


def w_cols(plane, kind):
    return ALL_COLS if plane == 0 else KV_COLS if kind > 5 else Q_COLS


X_KINDS = (NEAR_KINDS, NEAR_KINDS)
W_KINDS = (NEAR_KINDS, FEW_KINDS)


def gather_kernel(
    x_in, wq_in, wk_in, wv_in,
    q_out, kv_out, w_out,
    xf, wf, acc, kv_buf,
    load_sem, send_sems, recv_sems, out_sem, kv_sem,
):
    row, col, y, h, k, z, l = place()
    prev_row, next_row = (row + ROWS - 1) % ROWS, (row + 1) % ROWS

    def row_of(yy, hh, kk):
        return (yy * 2 + hh) * 2 + kk

    y_to = {1: (row_of((y + 1) % 4, h, k), col), 3: (row_of((y + 3) % 4, h, k), col)}
    z_to = {1: (row, ((z + 1) % 4) * 2 + l), 3: (row, ((z + 3) % 4) * 2 + l)}
    h_pair, sibling = (row_of(y, 1 - h, k), col), (row_of(y, h, 1 - k), col)
    l_pair = (row, z * 2 + 1 - l)

    own_x, own_w = col, row // 2
    own_rows = pl.ds(k * TOK, TOK)
    loads = [
        pltpu.make_async_copy(x_in, xf.at[own_x], load_sem.at[0]),
        pltpu.make_async_copy(wq_in, wf.at[own_w, own_rows, pl.ds(0, FEAT)], load_sem.at[1]),
        pltpu.make_async_copy(wk_in, wf.at[own_w, own_rows, pl.ds(FEAT, 128)], load_sem.at[2]),
        pltpu.make_async_copy(
            wv_in, wf.at[own_w, own_rows, pl.ds(FEAT + 128, 128)], load_sem.at[3]
        ),
    ]
    for load in loads:
        load.start()

    barrier = pltpu.get_barrier_semaphore()
    peers = [
        z_to[1], z_to[3], l_pair, y_to[1], y_to[3], h_pair, sibling,
        (prev_row, col), (next_row, col),
    ]
    for peer in peers:
        pl.semaphore_signal(barrier, inc=1, device_id=peer, device_id_type=MESH)
    pl.semaphore_wait(barrier, len(peers))
    for load in loads:
        load.wait()

    index, started = {}, []

    def move(name, src, dst, peer):
        i = index.setdefault(name, len(index))
        return remote(src, dst, send_sems.at[i], recv_sems.at[i], *peer)

    def send(name, ref, peer):
        copy = move(name, ref, ref, peer)
        copy.start()
        started.append(copy)

    def got(name, ref):
        move(name, ref, ref, sibling).wait_recv()

    def x_part(step, plane, first, count):
        slot = ((z + step) % 4) * 2 + (l + plane) % 2
        return xf.at[slot, pl.ds(first, count)]

    def w_part(step, plane, first, count, cols=ALL_COLS, core=None):
        slot = ((y + step) % 4) * 2 + (h + plane) % 2
        core = k if core is None else core
        return wf.at[slot, pl.ds(core * TOK + first, count), pl.ds(*cols)]

    shared = []

    def share(step, plane, first, count, cols=ALL_COLS):
        part = (step, plane, first, count, cols)
        send(("s", *part), w_part(*part), sibling)
        shared.append(part)

    def take_shared():
        for part in shared:
            got(("s", *part), w_part(*part, 1 - k))
        shared.clear()

    def x_ring(plane, *kinds):
        for kind in kinds:
            way, step, first, count = X_KINDS[plane][kind]
            send(("x", plane, kind), x_part(step, plane, first, count), z_to[way])

    def x_got(plane, *kinds):
        for kind in kinds:
            way, step, first, count = X_KINDS[plane][kind]
            got(("x", plane, kind), x_part((step - way) % 4, plane, first, count))

    def w_ring(plane, *kinds):
        for kind in kinds:
            way, step, first, count = W_KINDS[plane][kind]
            part = (step, plane, first, count, w_cols(plane, kind))
            send(("w", plane, kind), w_part(*part), y_to[way])

    def w_got(plane, kind, *then):
        way, step, first, count = W_KINDS[plane][kind]
        part = ((step - way) % 4, plane, first, count, w_cols(plane, kind))
        got(("w", plane, kind), w_part(*part))
        w_ring(plane, *then)
        share(*part)

    def w_lend(name, step, first, count, cols):
        send((name, first, cols), w_part(step, 0, first, count, cols), h_pair)

    def w_lent(name, step, first, count, cols, *then):
        part = (step, 1, first, count, cols)
        got((name, first, cols), w_part(*part))
        w_ring(1, *then)
        share(*part)

    for kind in (0, 2, 1, 3):
        x_ring(0, kind)
        w_ring(0, kind)
    for half in range(2):
        send(("xp", half), x_part(0, 0, half * HALF, HALF), l_pair)
        share(0, 0, half * HALF, HALF)

    x_got(0, 0)
    x_ring(0, 4)
    x_got(0, 2)
    x_ring(0, 5)
    got(("xp", 0), x_part(0, 1, 0, HALF))
    x_ring(1, 0, 3)
    w_got(0, 0, 4)
    w_got(0, 2, 5)
    got(("xp", 1), x_part(0, 1, HALF, HALF))
    x_ring(1, 2, 1)
    w_lend("wp", 0, 0, TOK, KV_COLS)
    w_lend("wp", 0, 0, HALF, Q_COLS)
    x_got(0, 1, 3)
    w_got(0, 1)
    w_got(0, 3)
    w_lent("wp", 0, 0, TOK, KV_COLS, 6, 7)
    x_got(0, 4, 5)
    w_lent("wp", 0, 0, HALF, Q_COLS, 0, 3)
    w_lend("wp", 0, HALF, HALF, Q_COLS)
    w_got(0, 4)
    w_got(0, 5)
    x_got(1, 0)
    x_ring(1, 4)
    w_lent("wp", 0, HALF, HALF, Q_COLS, 1, 2)
    w_lend("wf", 2, 0, TOK, KV_COLS)
    w_lend("wf", 2, 2 * FAR, HALF - 2 * FAR, Q_COLS)
    w_lend("wf", 2, HALF, HALF, Q_COLS)
    x_got(1, 2)
    x_ring(1, 5)
    w_got(1, 6)
    w_got(1, 7)
    x_got(1, 1, 3)
    take_shared()

    late_x = ((z + 2) % 4) * 2 + 1 - l
    late_w = ((y + 2) % 4) * 2 + 1 - h

    def multiply(slot, tile):
        cols = pl.ds(pl.multiple_of(tile * 256, 256), 256)
        return jnp.dot(xf[slot], wf[slot, :, cols], preferred_element_type=jnp.float32)

    tiles = FEAT // 256

    @pl.loop(0, tiles)
    def _(tile):
        acc[tile] = jnp.zeros((TOK, 256), jnp.float32)

    def add_slots(wanted):
        @pl.loop(0, COLS)
        def _(slot):
            @pl.when(wanted(slot))
            def _():
                @pl.loop(0, tiles)
                def _(tile):
                    acc[tile] += multiply(slot, tile)

                pltpu.make_async_copy(wf.at[slot], w_out.at[slot], out_sem.at[slot]).start()

    def early(slot):
        here = (slot % 2 == h) | (slot // 2 == y)
        return here & (slot != late_x)

    add_slots(early)

    w_got(1, 0, 4)
    w_got(1, 3, 5)
    w_lent("wf", 2, 0, TOK, KV_COLS)
    x_got(1, 4, 5)
    take_shared()

    acc[tiles] = jnp.zeros((TOK, 256), jnp.float32)

    @pl.loop(0, COLS)
    def _(slot):
        acc[tiles] += multiply(slot, tiles)

    kv_buf[...] = acc[tiles].astype(jnp.bfloat16)
    halo = [
        move("up", kv_buf, kv_out.at[0], (next_row, col)),
        move("down", kv_buf, kv_out.at[2], (prev_row, col)),
    ]
    for copy in halo:
        copy.start()
    own_kv = pltpu.make_async_copy(kv_buf, kv_out.at[1], kv_sem)
    own_kv.start()

    w_lent("wf", 2, 2 * FAR, HALF - 2 * FAR, Q_COLS)
    w_got(1, 1)
    w_got(1, 2)
    take_shared()
    add_slots(lambda slot: jnp.logical_not(early(slot)) & (slot != late_w))
    w_lent("wf", 2, HALF, HALF, Q_COLS)
    w_got(1, 4)
    w_got(1, 5)
    take_shared()
    pltpu.make_async_copy(wf.at[late_w], w_out.at[late_w], out_sem.at[late_w]).start()

    @pl.loop(0, tiles)
    def _(tile):
        cols = pl.ds(pl.multiple_of(tile * 256, 256), 256)
        q_out[:, cols] = (acc[tile] + multiply(late_w, tile)).astype(jnp.bfloat16)

    for copy in started:
        copy.wait_send()
    for copy in halo:
        copy.wait()
    own_kv.wait()
    for slot in range(COLS):
        pltpu.make_async_copy(wf.at[slot], w_out.at[slot], out_sem.at[slot]).wait()
    assert len(index) <= SEMS


SEMS = 60


def gather(layer_input, w_query, w_key, w_value):
    dma = pltpu.SemaphoreType.DMA
    return pl.pallas_call(
        gather_kernel,
        name="gather_project",
        out_shape=(
            jax.ShapeDtypeStruct((TOK, FEAT), jnp.bfloat16),
            jax.ShapeDtypeStruct((3, TOK, KV), jnp.bfloat16),
            jax.ShapeDtypeStruct((COLS, FEAT, WIDE), jnp.bfloat16),
        ),
        in_specs=[pl.BlockSpec(memory_space=pl.ANY)] * 4,
        out_specs=(
            pl.BlockSpec(memory_space=pltpu.VMEM),
            pl.BlockSpec(memory_space=pl.ANY),
            pl.BlockSpec(memory_space=pl.ANY),
        ),
        scratch_shapes=[
            pltpu.VMEM((COLS, TOK, FEAT), jnp.bfloat16),
            pltpu.VMEM((COLS, FEAT, WIDE), jnp.bfloat16),
            pltpu.VMEM((WIDE // 256, TOK, 256), jnp.float32),
            pltpu.VMEM((TOK, KV), jnp.bfloat16),
            dma((4,)),
            dma((SEMS,)), dma((SEMS,)),
            dma((COLS,)), dma,
        ],
        compiler_params=pltpu.CompilerParams(
            collective_id=0, has_side_effects=True, vmem_limit_bytes=56 * MIB
        ),
        cost_estimate=pl.CostEstimate(
            flops=2 * TOK * 8192 * WIDE, bytes_accessed=40 * MIB, transcendentals=0
        ),
    )(layer_input, w_query, w_key, w_value)


def scatter_kernel(
    dq_in, side_in, mid_in, w_in,
    out,
    jn, wv, acc, pb, lent, far, near, pair_out, pair_in, side_got,
    w_sem, send_sems, recv_sems,
):
    row, col, y, h, k, z, l = place()
    prev_row, next_row = (row + ROWS - 1) % ROWS, (row + 1) % ROWS
    z_next, z_prev = (row, ((z + 1) % 4) * 2 + l), (row, ((z + 3) % 4) * 2 + l)
    l_pair = (row, z * 2 + 1 - l)

    def slot_of(step, plane):
        return ((z + step) % 4) * 2 + (l + plane) % 2

    order = [(2, 1), (1, 1), (3, 1), (2, 0), (1, 0), (3, 0), (0, 1), (0, 0)]
    loads = {}
    for i, (step, plane) in enumerate(order):
        slot = slot_of(step, plane)
        loads[step, plane] = pltpu.make_async_copy(w_in.at[slot], wv.at[slot], w_sem.at[i])
        loads[step, plane].start()

    barrier = pltpu.get_barrier_semaphore()
    peers = [z_next, z_prev, l_pair, (prev_row, col), (next_row, col)]
    for peer in peers:
        pl.semaphore_signal(barrier, inc=1, device_id=peer, device_id_type=MESH)
    jn[:, :FEAT] = dq_in[...]
    pl.semaphore_wait(barrier, len(peers))

    index, started = {}, []

    def send(name, src, dst, peer):
        i = index.setdefault(name, len(index))
        copy = remote(src, dst, send_sems.at[i], recv_sems.at[i], *peer)
        copy.start()
        started.append(copy)

    def got(name, ref):
        i = index[name]
        remote(ref, ref, send_sems.at[i], recv_sems.at[i], *l_pair).wait_recv()

    send("down", side_in.at[0], side_got.at[1], (prev_row, col))
    send("up", side_in.at[1], side_got.at[0], (next_row, col))

    tiles = FEAT // 256
    low, high, both = pl.ds(0, HALF), pl.ds(HALF, HALF), pl.ds(0, TOK)
    halves = (low, high)

    def product(slot, tile, rows, cols):
        tall = pl.ds(pl.multiple_of(tile * 256, 256), 256)
        return lax.dot_general(
            jn[rows, cols], wv[slot, tall, cols], (((1,), (1,)), ((), ())),
            preferred_element_type=jnp.float32,
        )

    def each_tile(step):
        @pl.loop(0, tiles)
        def _(tile):
            step(tile, pl.ds(pl.multiple_of(tile * 256, 256), 256))

    every = pl.ds(0, WIDE)

    def fill(target, step, plane, rows, extra=None):
        slot = slot_of(step, plane)

        def one(tile, cols):
            value = product(slot, tile, rows, every)
            if extra is not None:
                value += extra[:, cols].astype(jnp.float32)
            target[rows, cols] = value.astype(jnp.bfloat16)

        each_tile(one)

    first = [(2, 1), (1, 1), (3, 1)]
    for i, (step, plane) in enumerate(first):
        loads[step, plane].wait()
        slot = slot_of(step, plane)

        def query_part(tile, cols):
            acc[i, tile] = product(slot, tile, both, pl.ds(0, FEAT))

        each_tile(query_part)

    got("down", side_got.at[1])
    got("up", side_got.at[0])
    jn[:, FEAT:] = (
        mid_in[...] + side_got[0].astype(jnp.float32) + side_got[1].astype(jnp.float32)
    ).astype(jnp.bfloat16)

    for half, rows in enumerate(halves):
        for i, (step, plane) in enumerate(first):
            slot = slot_of(step, plane)

            def whole(tile, cols):
                value = acc[i, tile, rows] + product(slot, tile, rows, pl.ds(FEAT, KV))
                pb[1, i, rows, cols] = value.astype(jnp.bfloat16)

            each_tile(whole)
            source = pb.at[1, i, rows]
            if i == 0:
                send(("lend", half), source, lent.at[rows], l_pair)
            else:
                target = near.at[1, i - 1, rows]
                send(("near", 1, i - 1, half), source, target, z_next if i == 1 else z_prev)

    def near_half(way, half, extra=None):
        rows = halves[half]
        fill(pb.at[0, 1 + way], 1 if way == 0 else 3, 0, rows, extra)
        send(
            ("near", 0, way, half), pb.at[0, 1 + way, rows], near.at[0, way, rows],
            z_next if way == 0 else z_prev,
        )

    loads[2, 0].wait()
    for half, rows in enumerate(halves):
        got(("lend", half), lent.at[rows])
        fill(pb.at[0, 0], 2, 0, rows, lent.at[rows])
        send(("far", half), pb.at[0, 0, rows], far.at[half], z_prev if half else z_next)
    loads[1, 0].wait()
    loads[3, 0].wait()
    near_half(0, 1)
    near_half(1, 0)

    def own(plane):
        loads[0, plane].wait()

        def one(tile, cols):
            acc[plane, tile] = product(slot_of(0, plane), tile, both, every)

        each_tile(one)

    def add_near(plane, way, half):
        rows = halves[half]
        got(("near", plane, way, half), near.at[plane, way, rows])

        def one(tile, cols):
            acc[plane, tile, rows] += near[plane, way, rows, cols].astype(jnp.float32)

        each_tile(one)

    own(1)
    for half, rows in enumerate(halves):
        for way in range(2):
            got(("near", 1, way, half), near.at[1, way, rows])

        def pair_sum(tile, cols):
            value = acc[1, tile, rows] + near[1, 0, rows, cols].astype(jnp.float32)
            value += near[1, 1, rows, cols].astype(jnp.float32)
            pair_out[rows, cols] = value.astype(jnp.bfloat16)

        each_tile(pair_sum)
        send(("pair", half), pair_out.at[rows], pair_in.at[rows], l_pair)
    got(("far", 0), far.at[0])
    near_half(0, 0, far.at[0])
    got(("far", 1), far.at[1])
    near_half(1, 1, far.at[1])
    own(0)
    add_near(0, 0, 1)
    add_near(0, 1, 0)
    for half, rows in enumerate(halves):
        got(("pair", half), pair_in.at[rows])

        def add_pair(tile, cols):
            acc[0, tile, rows] += pair_in[rows, cols].astype(jnp.float32)

        each_tile(add_pair)
    for half, rows in enumerate(halves):
        got(("near", 0, half, half), near.at[0, half, rows])

        def last(tile, cols):
            value = acc[0, tile, rows] + near[0, half, rows, cols].astype(jnp.float32)
            out[rows, cols] = value.astype(jnp.bfloat16)

        each_tile(last)

    for copy in started:
        copy.wait_send()


def scatter(grad_query, side, mid, full_wide):
    dma = pltpu.SemaphoreType.DMA
    vmem = pl.BlockSpec(memory_space=pltpu.VMEM)
    low = jnp.bfloat16
    return pl.pallas_call(
        scatter_kernel,
        name="project_scatter",
        out_shape=jax.ShapeDtypeStruct((TOK, FEAT), low),
        in_specs=[vmem, vmem, vmem, pl.BlockSpec(memory_space=pl.ANY)],
        out_specs=vmem,
        scratch_shapes=[
            pltpu.VMEM((TOK, WIDE), low),
            pltpu.VMEM((COLS, FEAT, WIDE), low),
            pltpu.VMEM((3, FEAT // 256, TOK, 256), jnp.float32),
            pltpu.VMEM((2, 3, TOK, FEAT), low),
            pltpu.VMEM((TOK, FEAT), low),
            pltpu.VMEM((2, HALF, FEAT), low),
            pltpu.VMEM((2, 2, TOK, FEAT), low),
            pltpu.VMEM((TOK, FEAT), low),
            pltpu.VMEM((TOK, FEAT), low),
            pltpu.VMEM((2, TOK, KV), low),
            dma((COLS,)),
            dma((16,)), dma((16,)),
        ],
        compiler_params=pltpu.CompilerParams(
            collective_id=1, has_side_effects=True, vmem_limit_bytes=56 * MIB
        ),
        cost_estimate=pl.CostEstimate(
            flops=2 * TOK * 8192 * WIDE, bytes_accessed=24 * MIB, transcendentals=0
        ),
    )(grad_query, side, mid, full_wide)


def attend_kernel(
    pattern, counts, q_in, cot_in, kv_in,
    out, dq_out, side_out, mid_out,
    owed,
):
    block = pl.program_id(0)
    per_dev = TOK // BLOCK
    block_count = ROWS * per_dev
    first = lax.axis_index("row") * per_dev
    scale = HEAD_DIM ** (-0.5)
    pair = 2 * HEAD_DIM

    @pl.when(block == 0)
    def _():
        owed[...] = jnp.zeros_like(owed)

    chosen = [pattern[block, i] for i in range(4)]
    local = [(b - first + per_dev + block_count) % block_count for b in chosen]
    keys = jnp.concatenate([kv_in[i, :, :HEAD_DIM] for i in local], axis=0)
    values = jnp.concatenate([kv_in[i, :, HEAD_DIM:] for i in local], axis=0)
    keys_t, values_t = keys.T, values.T
    spot = lax.broadcasted_iota(jnp.int32, (BLOCK, pair), 0)
    live = jnp.concatenate([spot < counts[b] for b in chosen], axis=0)
    own_count = counts[first + block]
    lane = lax.broadcasted_iota(jnp.int32, (HEAD_DIM, pair), 1)
    query_live = jnp.where(lane % BLOCK < own_count, 1.0, 0.0)
    row_live = lax.broadcasted_iota(jnp.int32, (BLOCK, HEAD_DIM), 0) < own_count
    row_live = jnp.where(row_live, 1.0, 0.0).astype(jnp.bfloat16)

    def heads(ref, start, mask=None):
        parts = [ref[:, start + i * HEAD_DIM : start + (i + 1) * HEAD_DIM] for i in range(2)]
        if mask is not None:
            parts = [part * mask for part in parts]
        return jnp.concatenate(parts, axis=0)

    def dot(a, b, dims):
        return lax.dot_general(a, b, (dims, ((), ())), preferred_element_type=jnp.float32)

    def put(ref, start, both):
        low = both.astype(jnp.bfloat16)
        for i in range(2):
            cols = slice(start + i * HEAD_DIM, start + (i + 1) * HEAD_DIM)
            ref[:, cols] = low[:, i * HEAD_DIM : (i + 1) * HEAD_DIM].T

    grad_keys = grad_values = None
    for start in range(0, FEAT, pair):
        query = heads(q_in, start)
        grad_out = heads(cot_in, start, row_live)
        raw = jnp.where(live, dot(keys, query, ((1,), (1,))), -1e30)
        top = jnp.max(raw, axis=0, keepdims=True)
        power = jnp.exp((raw - top) * scale)
        probs = power * (1.0 / jnp.sum(power, axis=0, keepdims=True))
        probs_low = probs.astype(jnp.bfloat16)
        put(out, start, dot(values_t, probs_low, ((1,), (0,))) * query_live)
        grad_probs = dot(values, grad_out, ((1,), (1,)))
        delta = jnp.sum(probs_low.astype(jnp.float32) * grad_probs, axis=0, keepdims=True)
        grad_scores = (probs * (grad_probs - delta) * scale).astype(jnp.bfloat16)
        put(dq_out, start, dot(keys_t, grad_scores, ((1,), (0,))))
        key_part = dot(grad_scores, query, ((1,), (0,)))
        value_part = dot(probs_low, grad_out, ((1,), (0,)))
        grad_keys = key_part if grad_keys is None else grad_keys + key_part
        grad_values = value_part if grad_values is None else grad_values + value_part

    for i, spot in enumerate(local):
        rows = slice(i * BLOCK, (i + 1) * BLOCK)
        owed[spot, :, :HEAD_DIM] += grad_keys[rows]
        owed[spot, :, HEAD_DIM:] += grad_values[rows]

    @pl.when(block == per_dev - 1)
    def _():
        for i in range(per_dev):
            rows = slice(i * BLOCK, (i + 1) * BLOCK)
            side_out[0, rows] = owed[i].astype(jnp.bfloat16)
            mid_out[rows] = owed[per_dev + i]
            side_out[1, rows] = owed[2 * per_dev + i].astype(jnp.bfloat16)


def attend(pattern, counts, query, cotangent, source):
    per_dev = TOK // BLOCK
    tokens = pl.BlockSpec((BLOCK, FEAT), lambda b: (b, 0))
    smem = pl.BlockSpec(memory_space=pltpu.SMEM)
    low = jnp.bfloat16
    return pl.pallas_call(
        attend_kernel,
        name="attend",
        grid=(per_dev,),
        out_shape=(
            jax.ShapeDtypeStruct((TOK, FEAT), low),
            jax.ShapeDtypeStruct((TOK, FEAT), low),
            jax.ShapeDtypeStruct((2, TOK, KV), low),
            jax.ShapeDtypeStruct((TOK, KV), jnp.float32),
        ),
        in_specs=[
            smem, smem, tokens, tokens,
            pl.BlockSpec((3 * per_dev, BLOCK, KV), lambda b: (0, 0, 0)),
        ],
        out_specs=(
            tokens, tokens,
            pl.BlockSpec((2, TOK, KV), lambda b: (0, 0, 0)),
            pl.BlockSpec((TOK, KV), lambda b: (0, 0)),
        ),
        scratch_shapes=[pltpu.VMEM((3 * per_dev, BLOCK, KV), jnp.float32)],
        compiler_params=pltpu.CompilerParams(vmem_limit_bytes=62 * MIB),
    )(pattern, counts, query, cotangent, source.reshape(3 * per_dev, BLOCK, KV))


def body(layer_input, w_query, w_key, w_value, counts, pattern, cotangent):
    query, source, full_wide = gather(layer_input, w_query, w_key, w_value)
    attended, grad_query, side, mid = attend(pattern, counts, query, cotangent, source)
    input_grad = scatter(grad_query, side, mid, full_wide)
    return attended, input_grad


def solution(mesh):
    placed = (
        P("row", "col"),
        P("row", "col"),
        P("row", "col"),
        P("row", "col"),
        P(),
        P("row", None),
        P("row", "col"),
    )
    return jax.shard_map(
        body,
        mesh=mesh,
        in_specs=placed,
        out_specs=(P("row", "col"), P("row", "col")),
        check_vma=False,
    )
```

```python
import functools

import jax
import jax.numpy as jnp
from jax import lax
from jax.experimental import pallas as pl
from jax.experimental.pallas import tpu as pltpu
from jax.sharding import PartitionSpec as P

HEADS = 64
KV_HEADS = 8
HEAD_DIM = 128
BLOCK = 128
GROUP = HEADS // KV_HEADS
ROWS = 16
COLS = 8
TOK = 512
HALF = 256
FEAT = 1024
KV = 256
WIDE = FEAT + KV
MESH = pl.DeviceIdType.MESH
MIB = 1024 * 1024
LOG2E = 1.4426950408889634


def place():
    row, col = lax.axis_index("row"), lax.axis_index("col")
    return row, col, row // 4, (row // 2) % 2, row % 2, col // 2, col % 2


def remote(src, dst, send, recv, row, col):
    return pltpu.make_async_remote_copy(
        src_ref=src,
        dst_ref=dst,
        send_sem=send,
        recv_sem=recv,
        device_id=(row, col),
        device_id_type=MESH,
    )


FAR = 96
NEAR_KINDS = {
    0: (1, 0, 0, HALF), 1: (1, 0, HALF, HALF), 2: (3, 0, HALF, HALF), 3: (3, 0, 0, HALF),
    4: (1, 3, 0, HALF), 5: (3, 1, HALF, HALF),
}
FEW_KINDS = {
    **NEAR_KINDS, 4: (1, 3, 0, FAR), 5: (3, 1, FAR, FAR), 6: (1, 0, 0, TOK), 7: (3, 0, 0, TOK),
}
ALL_COLS, Q_COLS, KV_COLS = (0, WIDE), (0, FEAT), (FEAT, KV)


def w_cols(plane, kind):
    return ALL_COLS if plane == 0 else KV_COLS if kind > 5 else Q_COLS


X_KINDS = (NEAR_KINDS, NEAR_KINDS)
W_KINDS = (NEAR_KINDS, FEW_KINDS)


def gather_kernel(
    x_in, wq_in, wk_in, wv_in,
    q_out, kv_out, w_out,
    xf, wf, acc, kv_buf, q_buf,
    load_sem, send_sems, recv_sems, out_sem, kv_sem, q_sem,
):
    row, col, y, h, k, z, l = place()
    prev_row, next_row = (row + ROWS - 1) % ROWS, (row + 1) % ROWS

    def row_of(yy, hh, kk):
        return (yy * 2 + hh) * 2 + kk

    y_to = {1: (row_of((y + 1) % 4, h, k), col), 3: (row_of((y + 3) % 4, h, k), col)}
    z_to = {1: (row, ((z + 1) % 4) * 2 + l), 3: (row, ((z + 3) % 4) * 2 + l)}
    h_pair, sibling = (row_of(y, 1 - h, k), col), (row_of(y, h, 1 - k), col)
    l_pair = (row, z * 2 + 1 - l)

    own_x, own_w = col, row // 2
    own_rows = pl.ds(k * TOK, TOK)
    loads = [
        pltpu.make_async_copy(x_in, xf.at[own_x], load_sem.at[0]),
        pltpu.make_async_copy(wq_in, wf.at[own_w, own_rows, pl.ds(0, FEAT)], load_sem.at[1]),
        pltpu.make_async_copy(wk_in, wf.at[own_w, own_rows, pl.ds(FEAT, 128)], load_sem.at[2]),
        pltpu.make_async_copy(
            wv_in, wf.at[own_w, own_rows, pl.ds(FEAT + 128, 128)], load_sem.at[3]
        ),
    ]
    for load in loads:
        load.start()

    barrier = pltpu.get_barrier_semaphore()
    peers = [
        z_to[1], z_to[3], l_pair, y_to[1], y_to[3], h_pair, sibling,
        (prev_row, col), (next_row, col),
    ]
    for peer in peers:
        pl.semaphore_signal(barrier, inc=1, device_id=peer, device_id_type=MESH)
    pl.semaphore_wait(barrier, len(peers))
    for load in loads:
        load.wait()

    index, started = {}, []

    def move(name, src, dst, peer):
        i = index.setdefault(name, len(index))
        return remote(src, dst, send_sems.at[i], recv_sems.at[i], *peer)

    def send(name, ref, peer):
        copy = move(name, ref, ref, peer)
        copy.start()
        started.append(copy)

    def got(name, ref):
        move(name, ref, ref, sibling).wait_recv()

    def x_part(step, plane, first, count):
        slot = ((z + step) % 4) * 2 + (l + plane) % 2
        return xf.at[slot, pl.ds(first, count)]

    def w_part(step, plane, first, count, cols=ALL_COLS, core=None):
        slot = ((y + step) % 4) * 2 + (h + plane) % 2
        core = k if core is None else core
        return wf.at[slot, pl.ds(core * TOK + first, count), pl.ds(*cols)]

    shared = []

    def share(step, plane, first, count, cols=ALL_COLS):
        part = (step, plane, first, count, cols)
        send(("s", *part), w_part(*part), sibling)
        shared.append(part)

    def take_shared():
        for part in shared:
            got(("s", *part), w_part(*part, 1 - k))
        shared.clear()

    def x_ring(plane, *kinds):
        for kind in kinds:
            way, step, first, count = X_KINDS[plane][kind]
            send(("x", plane, kind), x_part(step, plane, first, count), z_to[way])

    def x_got(plane, *kinds):
        for kind in kinds:
            way, step, first, count = X_KINDS[plane][kind]
            got(("x", plane, kind), x_part((step - way) % 4, plane, first, count))

    def w_ring(plane, *kinds):
        for kind in kinds:
            way, step, first, count = W_KINDS[plane][kind]
            part = (step, plane, first, count, w_cols(plane, kind))
            send(("w", plane, kind), w_part(*part), y_to[way])

    def w_got(plane, kind, *then):
        way, step, first, count = W_KINDS[plane][kind]
        part = ((step - way) % 4, plane, first, count, w_cols(plane, kind))
        got(("w", plane, kind), w_part(*part))
        w_ring(plane, *then)
        share(*part)

    def w_lend(name, step, first, count, cols):
        send((name, first, cols), w_part(step, 0, first, count, cols), h_pair)

    def w_lent(name, step, first, count, cols, *then):
        part = (step, 1, first, count, cols)
        got((name, first, cols), w_part(*part))
        w_ring(1, *then)
        share(*part)

    for kind in (0, 2, 1, 3):
        x_ring(0, kind)
        w_ring(0, kind)
    for half in range(2):
        send(("xp", half), x_part(0, 0, half * HALF, HALF), l_pair)
        share(0, 0, half * HALF, HALF)

    x_got(0, 0)
    x_ring(0, 4)
    x_got(0, 2)
    x_ring(0, 5)
    got(("xp", 0), x_part(0, 1, 0, HALF))
    x_ring(1, 0, 3)
    w_got(0, 0, 4)
    w_got(0, 2, 5)
    got(("xp", 1), x_part(0, 1, HALF, HALF))
    x_ring(1, 2, 1)
    w_lend("wp", 0, 0, TOK, KV_COLS)
    w_lend("wp", 0, 0, HALF, Q_COLS)
    x_got(0, 1, 3)
    w_got(0, 1)
    w_got(0, 3)
    w_lent("wp", 0, 0, TOK, KV_COLS, 6, 7)
    x_got(0, 4, 5)
    w_lent("wp", 0, 0, HALF, Q_COLS, 0, 3)
    w_lend("wp", 0, HALF, HALF, Q_COLS)
    w_got(0, 4)
    w_got(0, 5)
    x_got(1, 0)
    x_ring(1, 4)
    w_lent("wp", 0, HALF, HALF, Q_COLS, 1, 2)
    w_lend("wf", 2, 0, TOK, KV_COLS)
    w_lend("wf", 2, 2 * FAR, HALF - 2 * FAR, Q_COLS)
    w_lend("wf", 2, HALF, HALF, Q_COLS)
    x_got(1, 2)
    x_ring(1, 5)
    w_got(1, 6)
    w_got(1, 7)
    x_got(1, 1, 3)
    take_shared()

    late_x = ((z + 2) % 4) * 2 + 1 - l
    late_w = ((y + 2) % 4) * 2 + 1 - h

    def multiply(slot, tile):
        cols = pl.ds(pl.multiple_of(tile * 256, 256), 256)
        return jnp.dot(xf[slot], wf[slot, :, cols], preferred_element_type=jnp.float32)

    tiles = FEAT // 256

    @pl.loop(0, tiles)
    def _(tile):
        acc[tile] = jnp.zeros((TOK, 256), jnp.float32)

    def add_slots(wanted):
        @pl.loop(0, COLS)
        def _(slot):
            @pl.when(wanted(slot))
            def _():
                @pl.loop(0, tiles)
                def _(tile):
                    acc[tile] += multiply(slot, tile)

                pltpu.make_async_copy(wf.at[slot], w_out.at[slot], out_sem.at[slot]).start()

    def early(slot):
        here = (slot % 2 == h) | (slot // 2 == y)
        return here & (slot != late_x)

    add_slots(early)

    w_got(1, 0, 4)
    w_got(1, 3, 5)
    w_lent("wf", 2, 0, TOK, KV_COLS)
    x_got(1, 4, 5)
    take_shared()

    acc[tiles] = jnp.zeros((TOK, 256), jnp.float32)

    @pl.loop(0, COLS)
    def _(slot):
        acc[tiles] += multiply(slot, tiles)

    kv_buf[...] = acc[tiles].astype(jnp.bfloat16)
    halo = [
        move("up", kv_buf, kv_out.at[0], (next_row, col)),
        move("down", kv_buf, kv_out.at[2], (prev_row, col)),
    ]
    for copy in halo:
        copy.start()
    own_kv = pltpu.make_async_copy(kv_buf, kv_out.at[1], kv_sem)
    own_kv.start()

    w_lent("wf", 2, 2 * FAR, HALF - 2 * FAR, Q_COLS)
    w_got(1, 1)
    w_got(1, 2)
    take_shared()
    add_slots(lambda slot: jnp.logical_not(early(slot)) & (slot != late_w))
    w_lent("wf", 2, HALF, HALF, Q_COLS)
    w_got(1, 4)
    w_got(1, 5)
    take_shared()
    pltpu.make_async_copy(wf.at[late_w], w_out.at[late_w], out_sem.at[late_w]).start()

    @pl.loop(0, tiles)
    def _(tile):
        cols = pl.ds(pl.multiple_of(tile * 256, 256), 256)
        q_buf[:, cols] = (acc[tile] + multiply(late_w, tile)).astype(jnp.bfloat16)
        pltpu.make_async_copy(q_buf.at[:, cols], q_out.at[:, cols], q_sem.at[tile]).start()

    for copy in started:
        copy.wait_send()
    for copy in halo:
        copy.wait()
    own_kv.wait()
    for tile in range(tiles):
        cols = pl.ds(tile * 256, 256)
        pltpu.make_async_copy(q_buf.at[:, cols], q_out.at[:, cols], q_sem.at[tile]).wait()
    for slot in range(COLS):
        pltpu.make_async_copy(wf.at[slot], w_out.at[slot], out_sem.at[slot]).wait()
    assert len(index) <= SEMS


SEMS = 60


def gather(layer_input, w_query, w_key, w_value):
    dma = pltpu.SemaphoreType.DMA
    return pl.pallas_call(
        gather_kernel,
        name="gather_project",
        out_shape=(
            jax.ShapeDtypeStruct((TOK, FEAT), jnp.bfloat16),
            jax.ShapeDtypeStruct((3, TOK, KV), jnp.bfloat16),
            jax.ShapeDtypeStruct((COLS, FEAT, WIDE), jnp.bfloat16),
        ),
        in_specs=[pl.BlockSpec(memory_space=pl.ANY)] * 4,
        out_specs=(
            pl.BlockSpec(memory_space=pl.ANY),
            pl.BlockSpec(memory_space=pl.ANY),
            pl.BlockSpec(memory_space=pl.ANY),
        ),
        scratch_shapes=[
            pltpu.VMEM((COLS, TOK, FEAT), jnp.bfloat16),
            pltpu.VMEM((COLS, FEAT, WIDE), jnp.bfloat16),
            pltpu.VMEM((WIDE // 256, TOK, 256), jnp.float32),
            pltpu.VMEM((TOK, KV), jnp.bfloat16),
            pltpu.VMEM((TOK, FEAT), jnp.bfloat16),
            dma((4,)),
            dma((SEMS,)), dma((SEMS,)),
            dma((COLS,)), dma, dma((FEAT // 256,)),
        ],
        compiler_params=pltpu.CompilerParams(
            collective_id=0, has_side_effects=True, vmem_limit_bytes=56 * MIB
        ),
        cost_estimate=pl.CostEstimate(
            flops=2 * TOK * 8192 * WIDE, bytes_accessed=40 * MIB, transcendentals=0
        ),
    )(layer_input, w_query, w_key, w_value)


def scatter_kernel(
    dq_in, side_in, mid_in, w_in,
    out,
    jn, wv, acc, pb, lent, far, near, pair_out, pair_in, side_got, mid, result,
    w_sem, load_sem, out_sem, send_sems, recv_sems,
):
    row, col, y, h, k, z, l = place()
    prev_row, next_row = (row + ROWS - 1) % ROWS, (row + 1) % ROWS
    z_next, z_prev = (row, ((z + 1) % 4) * 2 + l), (row, ((z + 3) % 4) * 2 + l)
    l_pair = (row, z * 2 + 1 - l)

    def slot_of(step, plane):
        return ((z + step) % 4) * 2 + (l + plane) % 2

    order = [(2, 1), (1, 1), (3, 1), (2, 0), (1, 0), (3, 0), (0, 1), (0, 0)]
    load_query = pltpu.make_async_copy(dq_in, jn.at[:, pl.ds(0, FEAT)], load_sem.at[0])
    load_mid = pltpu.make_async_copy(mid_in, mid, load_sem.at[1])
    load_query.start()
    loads = {}
    for i, (step, plane) in enumerate(order):
        slot = slot_of(step, plane)
        loads[step, plane] = pltpu.make_async_copy(w_in.at[slot], wv.at[slot], w_sem.at[i])
        loads[step, plane].start()
    load_mid.start()

    barrier = pltpu.get_barrier_semaphore()
    peers = [z_next, z_prev, l_pair, (prev_row, col), (next_row, col)]
    for peer in peers:
        pl.semaphore_signal(barrier, inc=1, device_id=peer, device_id_type=MESH)
    pl.semaphore_wait(barrier, len(peers))

    index, started = {}, []

    def send(name, src, dst, peer):
        i = index.setdefault(name, len(index))
        copy = remote(src, dst, send_sems.at[i], recv_sems.at[i], *peer)
        copy.start()
        started.append(copy)

    def got(name, ref):
        i = index[name]
        remote(ref, ref, send_sems.at[i], recv_sems.at[i], *l_pair).wait_recv()

    send("down", side_in.at[0], side_got.at[1], (prev_row, col))
    send("up", side_in.at[1], side_got.at[0], (next_row, col))

    tiles = FEAT // 256
    low, high, both = pl.ds(0, HALF), pl.ds(HALF, HALF), pl.ds(0, TOK)
    halves = (low, high)

    def product(slot, tile, rows, cols):
        tall = pl.ds(pl.multiple_of(tile * 256, 256), 256)
        return lax.dot_general(
            jn[rows, cols], wv[slot, tall, cols], (((1,), (1,)), ((), ())),
            preferred_element_type=jnp.float32,
        )

    def each_tile(step):
        @pl.loop(0, tiles)
        def _(tile):
            step(tile, pl.ds(pl.multiple_of(tile * 256, 256), 256))

    every = pl.ds(0, WIDE)

    def fill(target, step, plane, rows, extra=None):
        slot = slot_of(step, plane)

        def one(tile, cols):
            value = product(slot, tile, rows, every)
            if extra is not None:
                value += extra[:, cols].astype(jnp.float32)
            target[rows, cols] = value.astype(jnp.bfloat16)

        each_tile(one)

    first = [(2, 1), (1, 1), (3, 1)]
    load_query.wait()
    for i, (step, plane) in enumerate(first):
        loads[step, plane].wait()

    def query_part(rows):
        for i, (step, plane) in enumerate(first):
            slot = slot_of(step, plane)

            def one(tile, cols):
                acc[i, tile, rows] = product(slot, tile, rows, pl.ds(0, FEAT))

            each_tile(one)

    def whole_part(half):
        rows = halves[half]
        for i, (step, plane) in enumerate(first):
            slot = slot_of(step, plane)

            def one(tile, cols):
                value = acc[i, tile, rows] + product(slot, tile, rows, pl.ds(FEAT, KV))
                pb[1, i, rows, cols] = value.astype(jnp.bfloat16)

            each_tile(one)
            source = pb.at[1, i, rows]
            if i == 0:
                send(("lend", half), source, lent.at[rows], l_pair)
            else:
                target = near.at[1, i - 1, rows]
                send(("near", 1, i - 1, half), source, target, z_next if i == 1 else z_prev)

    query_part(low)
    load_mid.wait()
    got("down", side_got.at[1])
    got("up", side_got.at[0])
    jn[:, FEAT:] = (
        mid[...] + side_got[0].astype(jnp.float32) + side_got[1].astype(jnp.float32)
    ).astype(jnp.bfloat16)
    whole_part(0)
    query_part(high)
    whole_part(1)

    def near_half(way, half, extra=None):
        rows = halves[half]
        fill(pb.at[0, 1 + way], 1 if way == 0 else 3, 0, rows, extra)
        send(
            ("near", 0, way, half), pb.at[0, 1 + way, rows], near.at[0, way, rows],
            z_next if way == 0 else z_prev,
        )

    loads[2, 0].wait()
    for half, rows in enumerate(halves):
        got(("lend", half), lent.at[rows])
        fill(pb.at[0, 0], 2, 0, rows, lent.at[rows])
        send(("far", half), pb.at[0, 0, rows], far.at[half], z_prev if half else z_next)
    loads[1, 0].wait()
    loads[3, 0].wait()
    near_half(0, 1)
    near_half(1, 0)

    def own(plane):
        loads[0, plane].wait()

        def one(tile, cols):
            acc[plane, tile] = product(slot_of(0, plane), tile, both, every)

        each_tile(one)

    def add_near(plane, way, half):
        rows = halves[half]
        got(("near", plane, way, half), near.at[plane, way, rows])

        def one(tile, cols):
            acc[plane, tile, rows] += near[plane, way, rows, cols].astype(jnp.float32)

        each_tile(one)

    own(1)
    for half, rows in enumerate(halves):
        for way in range(2):
            got(("near", 1, way, half), near.at[1, way, rows])

        def pair_sum(tile, cols):
            value = acc[1, tile, rows] + near[1, 0, rows, cols].astype(jnp.float32)
            value += near[1, 1, rows, cols].astype(jnp.float32)
            pair_out[rows, cols] = value.astype(jnp.bfloat16)

        each_tile(pair_sum)
        send(("pair", half), pair_out.at[rows], pair_in.at[rows], l_pair)
    got(("far", 0), far.at[0])
    near_half(0, 0, far.at[0])
    got(("far", 1), far.at[1])
    near_half(1, 1, far.at[1])
    own(0)
    add_near(0, 0, 1)
    add_near(0, 1, 0)
    for half, rows in enumerate(halves):
        got(("pair", half), pair_in.at[rows])

        def add_pair(tile, cols):
            acc[0, tile, rows] += pair_in[rows, cols].astype(jnp.float32)

        each_tile(add_pair)
    for half, rows in enumerate(halves):
        got(("near", 0, half, half), near.at[0, half, rows])

        def last(tile, cols):
            value = acc[0, tile, rows] + near[0, half, rows, cols].astype(jnp.float32)
            result[rows, cols] = value.astype(jnp.bfloat16)

        each_tile(last)
        pltpu.make_async_copy(result.at[rows], out.at[rows], out_sem.at[half]).start()

    for copy in started:
        copy.wait_send()
    for half, rows in enumerate(halves):
        pltpu.make_async_copy(result.at[rows], out.at[rows], out_sem.at[half]).wait()


def scatter(grad_query, side, mid, full_wide):
    dma = pltpu.SemaphoreType.DMA
    anywhere = pl.BlockSpec(memory_space=pl.ANY)
    low = jnp.bfloat16
    return pl.pallas_call(
        scatter_kernel,
        name="project_scatter",
        out_shape=jax.ShapeDtypeStruct((TOK, FEAT), low),
        in_specs=[anywhere] * 4,
        out_specs=anywhere,
        scratch_shapes=[
            pltpu.VMEM((TOK, WIDE), low),
            pltpu.VMEM((COLS, FEAT, WIDE), low),
            pltpu.VMEM((3, FEAT // 256, TOK, 256), jnp.float32),
            pltpu.VMEM((2, 3, TOK, FEAT), low),
            pltpu.VMEM((TOK, FEAT), low),
            pltpu.VMEM((2, HALF, FEAT), low),
            pltpu.VMEM((2, 2, TOK, FEAT), low),
            pltpu.VMEM((TOK, FEAT), low),
            pltpu.VMEM((TOK, FEAT), low),
            pltpu.VMEM((2, TOK, KV), low),
            pltpu.VMEM((TOK, KV), jnp.float32),
            pltpu.VMEM((TOK, FEAT), low),
            dma((COLS,)), dma((2,)), dma((2,)),
            dma((16,)), dma((16,)),
        ],
        compiler_params=pltpu.CompilerParams(
            collective_id=1, has_side_effects=True, vmem_limit_bytes=56 * MIB
        ),
        cost_estimate=pl.CostEstimate(
            flops=2 * TOK * 8192 * WIDE, bytes_accessed=24 * MIB, transcendentals=0
        ),
    )(grad_query, side, mid, full_wide)


def attend_kernel(
    pattern, counts, q_in, cot_in, kv_in,
    out, dq_out, side_out, mid_out,
    owed,
):
    block = pl.program_id(0)
    per_dev = TOK // BLOCK
    block_count = ROWS * per_dev
    first = lax.axis_index("row") * per_dev
    scale = HEAD_DIM ** (-0.5)
    exponent_scale = scale * LOG2E
    pair = 2 * HEAD_DIM

    @pl.when(block == 0)
    def _():
        owed[...] = jnp.zeros_like(owed)

    chosen = [pattern[block, i] for i in range(4)]
    local = [(b - first + per_dev + block_count) % block_count for b in chosen]
    keys = jnp.concatenate([kv_in[i, :, :HEAD_DIM] for i in local], axis=0)
    values = jnp.concatenate([kv_in[i, :, HEAD_DIM:] for i in local], axis=0)
    keys_t, values_t = keys.T, values.T
    spot = lax.broadcasted_iota(jnp.int32, (BLOCK, pair), 0)
    live = jnp.concatenate([spot < counts[b] for b in chosen], axis=0)
    own_count = counts[first + block]
    lane = lax.broadcasted_iota(jnp.int32, (1, pair), 1)
    query_live = jnp.where(lane % BLOCK < own_count, 1.0, 0.0)
    row_live = lax.broadcasted_iota(jnp.int32, (BLOCK, HEAD_DIM), 0) < own_count
    row_live = jnp.where(row_live, 1.0, 0.0).astype(jnp.bfloat16)

    def heads(ref, start, mask=None):
        parts = [ref[:, start + i * HEAD_DIM : start + (i + 1) * HEAD_DIM] for i in range(2)]
        if mask is not None:
            parts = [part * mask for part in parts]
        return jnp.concatenate(parts, axis=0)

    def dot(a, b, dims):
        return lax.dot_general(a, b, (dims, ((), ())), preferred_element_type=jnp.float32)

    def put(ref, start, both):
        low = both.astype(jnp.bfloat16)
        for i in range(2):
            cols = slice(start + i * HEAD_DIM, start + (i + 1) * HEAD_DIM)
            ref[:, cols] = low[:, i * HEAD_DIM : (i + 1) * HEAD_DIM].T

    def begin(start):
        query = heads(q_in, start)
        grad_out = heads(cot_in, start, row_live)
        raw = dot(keys, query, ((1,), (1,)))
        return start, query, grad_out, raw, dot(values, grad_out, ((1,), (1,)))

    def middle(start, query, grad_out, raw, grad_probs):
        raw = jnp.where(live, raw, -1e30)
        top = jnp.max(raw, axis=0, keepdims=True)
        power = jnp.exp2((raw - top) * exponent_scale)
        probs = power * (1.0 / jnp.sum(power, axis=0, keepdims=True))
        probs_low = probs.astype(jnp.bfloat16)
        delta = jnp.sum(probs_low.astype(jnp.float32) * grad_probs, axis=0, keepdims=True)
        grad_scores = (probs * (grad_probs - delta) * scale).astype(jnp.bfloat16)
        return start, query, grad_out, probs_low, grad_scores

    def end(start, query, grad_out, probs_low, grad_scores):
        put(out, start, dot(values_t, probs_low, ((1,), (0,))) * query_live)
        put(dq_out, start, dot(keys_t, grad_scores, ((1,), (0,))))
        key_part = dot(grad_scores, query, ((1,), (0,)))
        value_part = dot(probs_low, grad_out, ((1,), (0,)))
        return key_part, value_part

    starts = range(0, FEAT, pair)
    parts = []
    coming, going = begin(starts[0]), None
    for i in range(len(starts)):
        now = coming
        if i + 1 < len(starts):
            coming = begin(starts[i + 1])
        done = middle(*now)
        if going is not None:
            parts.append(end(*going))
        going = done
    parts.append(end(*going))
    grad_keys = sum(part[0] for part in parts[1:]) + parts[0][0]
    grad_values = sum(part[1] for part in parts[1:]) + parts[0][1]

    for i, spot in enumerate(local):
        rows = slice(i * BLOCK, (i + 1) * BLOCK)
        owed[spot, :, :HEAD_DIM] += grad_keys[rows]
        owed[spot, :, HEAD_DIM:] += grad_values[rows]

    @pl.when(block == per_dev - 1)
    def _():
        for i in range(per_dev):
            rows = slice(i * BLOCK, (i + 1) * BLOCK)
            side_out[0, rows] = owed[i].astype(jnp.bfloat16)
            mid_out[rows] = owed[per_dev + i]
            side_out[1, rows] = owed[2 * per_dev + i].astype(jnp.bfloat16)


def attend(pattern, counts, query, cotangent, source):
    per_dev = TOK // BLOCK
    tokens = pl.BlockSpec((BLOCK, FEAT), lambda b: (b, 0))
    smem = pl.BlockSpec(memory_space=pltpu.SMEM)
    low = jnp.bfloat16
    return pl.pallas_call(
        attend_kernel,
        name="attend",
        grid=(per_dev,),
        out_shape=(
            jax.ShapeDtypeStruct((TOK, FEAT), low),
            jax.ShapeDtypeStruct((TOK, FEAT), low),
            jax.ShapeDtypeStruct((2, TOK, KV), low),
            jax.ShapeDtypeStruct((TOK, KV), jnp.float32),
        ),
        in_specs=[
            smem, smem, tokens, tokens,
            pl.BlockSpec((3 * per_dev, BLOCK, KV), lambda b: (0, 0, 0)),
        ],
        out_specs=(
            tokens, tokens,
            pl.BlockSpec((2, TOK, KV), lambda b: (0, 0, 0)),
            pl.BlockSpec((TOK, KV), lambda b: (0, 0)),
        ),
        scratch_shapes=[pltpu.VMEM((3 * per_dev, BLOCK, KV), jnp.float32)],
        compiler_params=pltpu.CompilerParams(vmem_limit_bytes=62 * MIB),
    )(pattern, counts, query, cotangent, source.reshape(3 * per_dev, BLOCK, KV))


def body(layer_input, w_query, w_key, w_value, counts, pattern, cotangent):
    query, source, full_wide = gather(layer_input, w_query, w_key, w_value)
    attended, grad_query, side, mid = attend(pattern, counts, query, cotangent, source)
    input_grad = scatter(grad_query, side, mid, full_wide)
    return attended, input_grad


def solution(mesh):
    placed = (
        P("row", "col"),
        P("row", "col"),
        P("row", "col"),
        P("row", "col"),
        P(),
        P("row", None),
        P("row", "col"),
    )
    return jax.shard_map(
        body,
        mesh=mesh,
        in_specs=placed,
        out_specs=(P("row", "col"), P("row", "col")),
        check_vma=False,
    )
```

```python
import functools

import jax
import jax.numpy as jnp
from jax import lax
from jax.experimental import pallas as pl
from jax.experimental.pallas import tpu as pltpu
from jax.sharding import PartitionSpec as P

HEADS = 64
KV_HEADS = 8
HEAD_DIM = 128
BLOCK = 128
GROUP = HEADS // KV_HEADS
ROWS = 16
COLS = 8
TOK = 512
HALF = 256
FEAT = 1024
KV = 256
WIDE = FEAT + KV
MESH = pl.DeviceIdType.MESH
SPAN = 1024
LAST = 2
LEND = 64
OUT_SPAN = 1024
MIB = 1024 * 1024
LOG2E = 1.4426950408889634


def place():
    row, col = lax.axis_index("row"), lax.axis_index("col")
    return row, col, row // 4, (row // 2) % 2, row % 2, col // 2, col % 2


def remote(src, dst, send, recv, row, col):
    return pltpu.make_async_remote_copy(
        src_ref=src,
        dst_ref=dst,
        send_sem=send,
        recv_sem=recv,
        device_id=(row, col),
        device_id_type=MESH,
    )


FAR = 96
NEAR_KINDS = {
    0: (1, 0, 0, HALF), 1: (1, 0, HALF, HALF), 2: (3, 0, HALF, HALF), 3: (3, 0, 0, HALF),
    4: (1, 3, 0, HALF), 5: (3, 1, HALF, HALF),
}
FEW_KINDS = {
    **NEAR_KINDS, 4: (1, 3, 0, FAR), 5: (3, 1, FAR, FAR), 6: (1, 0, 0, TOK), 7: (3, 0, 0, TOK),
}
ALL_COLS, Q_COLS, KV_COLS = (0, WIDE), (0, FEAT), (FEAT, KV)


def w_cols(plane, kind):
    return ALL_COLS if plane == 0 else KV_COLS if kind > 5 else Q_COLS


X_KINDS = (NEAR_KINDS, NEAR_KINDS)
W_KINDS = (NEAR_KINDS, FEW_KINDS)


def gather_kernel(
    x_in, wq_in, wk_in, wv_in,
    q_out, kv_out, w_out,
    xf, wf, acc, kv_acc, kv_buf, q_buf,
    load_sem, send_sems, recv_sems, out_sem, kv_sem, q_sem,
):
    row, col, y, h, k, z, l = place()
    prev_row, next_row = (row + ROWS - 1) % ROWS, (row + 1) % ROWS

    def row_of(yy, hh, kk):
        return (yy * 2 + hh) * 2 + kk

    y_to = {1: (row_of((y + 1) % 4, h, k), col), 3: (row_of((y + 3) % 4, h, k), col)}
    z_to = {1: (row, ((z + 1) % 4) * 2 + l), 3: (row, ((z + 3) % 4) * 2 + l)}
    h_pair, sibling = (row_of(y, 1 - h, k), col), (row_of(y, h, 1 - k), col)
    l_pair = (row, z * 2 + 1 - l)

    own_x, own_w = col, row // 2
    own_rows = pl.ds(k * TOK, TOK)
    loads = [
        pltpu.make_async_copy(x_in, xf.at[own_x], load_sem.at[0]),
        pltpu.make_async_copy(wq_in, wf.at[own_w, own_rows, pl.ds(0, FEAT)], load_sem.at[1]),
        pltpu.make_async_copy(wk_in, wf.at[own_w, own_rows, pl.ds(FEAT, 128)], load_sem.at[2]),
        pltpu.make_async_copy(
            wv_in, wf.at[own_w, own_rows, pl.ds(FEAT + 128, 128)], load_sem.at[3]
        ),
    ]
    for load in loads:
        load.start()

    barrier = pltpu.get_barrier_semaphore()
    peers = [
        z_to[1], z_to[3], l_pair, y_to[1], y_to[3], h_pair, sibling,
        (prev_row, col), (next_row, col),
    ]
    for peer in peers:
        pl.semaphore_signal(barrier, inc=1, device_id=peer, device_id_type=MESH)
    pl.semaphore_wait(barrier, len(peers))
    for load in loads:
        load.wait()

    index, started = {}, []

    def move(name, src, dst, peer):
        i = index.setdefault(name, len(index))
        return remote(src, dst, send_sems.at[i], recv_sems.at[i], *peer)

    def send(name, ref, peer):
        copy = move(name, ref, ref, peer)
        copy.start()
        started.append(copy)

    def got(name, ref):
        move(name, ref, ref, sibling).wait_recv()

    def x_part(step, plane, first, count):
        slot = ((z + step) % 4) * 2 + (l + plane) % 2
        return xf.at[slot, pl.ds(first, count)]

    def w_part(step, plane, first, count, cols=ALL_COLS, core=None):
        slot = ((y + step) % 4) * 2 + (h + plane) % 2
        core = k if core is None else core
        return wf.at[slot, pl.ds(core * TOK + first, count), pl.ds(*cols)]

    shared = []

    def share(step, plane, first, count, cols=ALL_COLS):
        part = (step, plane, first, count, cols)
        send(("s", *part), w_part(*part), sibling)
        shared.append(part)

    def take_shared():
        for part in shared:
            got(("s", *part), w_part(*part, 1 - k))
        shared.clear()

    def x_ring(plane, *kinds):
        for kind in kinds:
            way, step, first, count = X_KINDS[plane][kind]
            send(("x", plane, kind), x_part(step, plane, first, count), z_to[way])

    def x_got(plane, *kinds):
        for kind in kinds:
            way, step, first, count = X_KINDS[plane][kind]
            got(("x", plane, kind), x_part((step - way) % 4, plane, first, count))

    def w_ring(plane, *kinds):
        for kind in kinds:
            way, step, first, count = W_KINDS[plane][kind]
            part = (step, plane, first, count, w_cols(plane, kind))
            send(("w", plane, kind), w_part(*part), y_to[way])

    def w_got(plane, kind, *then):
        way, step, first, count = W_KINDS[plane][kind]
        part = ((step - way) % 4, plane, first, count, w_cols(plane, kind))
        got(("w", plane, kind), w_part(*part))
        w_ring(plane, *then)
        share(*part)

    def w_lend(name, step, first, count, cols):
        send((name, first, cols), w_part(step, 0, first, count, cols), h_pair)

    def w_lent(name, step, first, count, cols, *then):
        part = (step, 1, first, count, cols)
        got((name, first, cols), w_part(*part))
        w_ring(1, *then)
        share(*part)

    for kind in (0, 2, 1, 3):
        x_ring(0, kind)
        w_ring(0, kind)
    for half in range(2):
        send(("xp", half), x_part(0, 0, half * HALF, HALF), l_pair)
        share(0, 0, half * HALF, HALF)

    x_got(0, 0)
    x_ring(0, 4)
    x_got(0, 2)
    x_ring(0, 5)
    got(("xp", 0), x_part(0, 1, 0, HALF))
    x_ring(1, 0, 3)
    w_got(0, 0, 4)
    w_got(0, 2, 5)
    got(("xp", 1), x_part(0, 1, HALF, HALF))
    x_ring(1, 2, 1)
    w_lend("wp", 0, 0, TOK, KV_COLS)
    w_lend("wp", 0, 0, HALF, Q_COLS)
    x_got(0, 1, 3)
    w_got(0, 1)
    w_got(0, 3)
    w_lent("wp", 0, 0, TOK, KV_COLS, 6, 7)
    x_got(0, 4, 5)
    w_lent("wp", 0, 0, HALF, Q_COLS, 0, 3)
    w_lend("wp", 0, HALF, HALF, Q_COLS)
    w_got(0, 4)
    w_got(0, 5)
    x_got(1, 0)
    x_ring(1, 4)
    w_lent("wp", 0, HALF, HALF, Q_COLS, 1, 2)
    w_lend("wf", 2, 0, TOK, KV_COLS)
    w_lend("wf", 2, 2 * FAR, HALF - 2 * FAR, Q_COLS)
    w_lend("wf", 2, HALF, HALF, Q_COLS)
    x_got(1, 2)
    x_ring(1, 5)
    w_got(1, 6)
    w_got(1, 7)
    x_got(1, 1, 3)
    take_shared()

    late_x = ((z + 2) % 4) * 2 + 1 - l
    late_w = ((y + 2) % 4) * 2 + 1 - h

    def multiply(slot, first, count):
        cols = pl.ds(first, count)
        return jnp.dot(xf[slot], wf[slot, :, cols], preferred_element_type=jnp.float32)

    def multiply_tile(slot, tile):
        return multiply(slot, pl.multiple_of(tile * SPAN, SPAN), SPAN)

    tiles = FEAT // SPAN

    @pl.loop(0, tiles)
    def _(tile):
        acc[tile] = jnp.zeros((TOK, SPAN), jnp.float32)

    def add_slots(wanted):
        @pl.loop(0, COLS)
        def _(slot):
            @pl.when(wanted(slot))
            def _():
                @pl.loop(0, tiles)
                def _(tile):
                    acc[tile] += multiply_tile(slot, tile)

                pltpu.make_async_copy(wf.at[slot], w_out.at[slot], out_sem.at[slot]).start()

    def early(slot):
        here = (slot % 2 == h) | (slot // 2 == y)
        return here & (slot != late_x)

    add_slots(early)

    w_got(1, 0, 4)
    w_got(1, 3, 5)
    w_lent("wf", 2, 0, TOK, KV_COLS)
    x_got(1, 4, 5)
    take_shared()

    kv_acc[...] = multiply(0, FEAT, KV)

    @pl.loop(1, COLS)
    def _(slot):
        kv_acc[...] += multiply(slot, FEAT, KV)

    kv_buf[...] = kv_acc[...].astype(jnp.bfloat16)
    halo = [
        move("up", kv_buf, kv_out.at[0], (next_row, col)),
        move("down", kv_buf, kv_out.at[2], (prev_row, col)),
    ]
    for copy in halo:
        copy.start()
    own_kv = pltpu.make_async_copy(kv_buf, kv_out.at[1], kv_sem)
    own_kv.start()

    w_lent("wf", 2, 2 * FAR, HALF - 2 * FAR, Q_COLS)
    w_got(1, 1)
    w_got(1, 2)
    take_shared()
    add_slots(lambda slot: jnp.logical_not(early(slot)) & (slot != late_w))
    w_lent("wf", 2, HALF, HALF, Q_COLS)
    w_got(1, 4)
    w_got(1, 5)
    take_shared()
    pltpu.make_async_copy(wf.at[late_w], w_out.at[late_w], out_sem.at[late_w]).start()

    for i in range(LAST):
        cols = pl.ds(i * (FEAT // LAST), FEAT // LAST)
        total = acc[0, :, cols] + multiply(late_w, i * (FEAT // LAST), FEAT // LAST)
        q_buf[:, cols] = total.astype(jnp.bfloat16)
        pltpu.make_async_copy(q_buf.at[:, cols], q_out.at[:, cols], q_sem.at[i]).start()

    for copy in started:
        copy.wait_send()
    for copy in halo:
        copy.wait()
    own_kv.wait()
    for i in range(LAST):
        cols = pl.ds(i * (FEAT // LAST), FEAT // LAST)
        pltpu.make_async_copy(q_buf.at[:, cols], q_out.at[:, cols], q_sem.at[i]).wait()
    for slot in range(COLS):
        pltpu.make_async_copy(wf.at[slot], w_out.at[slot], out_sem.at[slot]).wait()
    assert len(index) <= SEMS


SEMS = 60


def gather(layer_input, w_query, w_key, w_value):
    dma = pltpu.SemaphoreType.DMA
    return pl.pallas_call(
        gather_kernel,
        name="gather_project",
        out_shape=(
            jax.ShapeDtypeStruct((TOK, FEAT), jnp.bfloat16),
            jax.ShapeDtypeStruct((3, TOK, KV), jnp.bfloat16),
            jax.ShapeDtypeStruct((COLS, FEAT, WIDE), jnp.bfloat16),
        ),
        in_specs=[pl.BlockSpec(memory_space=pl.ANY)] * 4,
        out_specs=(
            pl.BlockSpec(memory_space=pl.ANY),
            pl.BlockSpec(memory_space=pl.ANY),
            pl.BlockSpec(memory_space=pl.ANY),
        ),
        scratch_shapes=[
            pltpu.VMEM((COLS, TOK, FEAT), jnp.bfloat16),
            pltpu.VMEM((COLS, FEAT, WIDE), jnp.bfloat16),
            pltpu.VMEM((FEAT // SPAN, TOK, SPAN), jnp.float32),
            pltpu.VMEM((TOK, KV), jnp.float32),
            pltpu.VMEM((TOK, KV), jnp.bfloat16),
            pltpu.VMEM((TOK, FEAT), jnp.bfloat16),
            dma((4,)),
            dma((SEMS,)), dma((SEMS,)),
            dma((COLS,)), dma, dma((LAST,)),
        ],
        compiler_params=pltpu.CompilerParams(
            collective_id=0, has_side_effects=True, vmem_limit_bytes=56 * MIB
        ),
        cost_estimate=pl.CostEstimate(
            flops=2 * TOK * 8192 * WIDE, bytes_accessed=40 * MIB, transcendentals=0
        ),
    )(layer_input, w_query, w_key, w_value)


def scatter_kernel(
    dq_in, side_in, mid_in, w_in,
    out,
    jn, wv, acc, pb, lent, far, near, pair_out, pair_in, side_got, taken, mid, result,
    w_sem, load_sem, out_sem, send_sems, recv_sems,
):
    row, col, y, h, k, z, l = place()
    prev_row, next_row = (row + ROWS - 1) % ROWS, (row + 1) % ROWS
    z_next, z_prev = (row, ((z + 1) % 4) * 2 + l), (row, ((z + 3) % 4) * 2 + l)
    l_pair = (row, z * 2 + 1 - l)

    def slot_of(step, plane):
        return ((z + step) % 4) * 2 + (l + plane) % 2

    order = [(2, 1), (1, 1), (3, 1), (2, 0), (1, 0), (3, 0), (0, 1), (0, 0)]
    load_query = pltpu.make_async_copy(dq_in, jn.at[:, pl.ds(0, FEAT)], load_sem.at[0])
    load_mid = pltpu.make_async_copy(mid_in, mid, load_sem.at[1])
    load_query.start()
    loads = {}
    for i, (step, plane) in enumerate(order):
        slot = slot_of(step, plane)
        loads[step, plane] = pltpu.make_async_copy(w_in.at[slot], wv.at[slot], w_sem.at[i])
        loads[step, plane].start()
    load_mid.start()

    barrier = pltpu.get_barrier_semaphore()
    peers = [z_next, z_prev, l_pair, (prev_row, col), (next_row, col)]
    for peer in peers:
        pl.semaphore_signal(barrier, inc=1, device_id=peer, device_id_type=MESH)
    pl.semaphore_wait(barrier, len(peers))

    index, started = {}, []

    def send(name, src, dst, peer):
        i = index.setdefault(name, len(index))
        copy = remote(src, dst, send_sems.at[i], recv_sems.at[i], *peer)
        copy.start()
        started.append(copy)

    def got(name, ref):
        i = index[name]
        remote(ref, ref, send_sems.at[i], recv_sems.at[i], *l_pair).wait_recv()

    tiles = FEAT // OUT_SPAN
    low, high, both = pl.ds(0, HALF), pl.ds(HALF, HALF), pl.ds(0, TOK)
    halves = (low, high)
    for half, rows in enumerate(halves):
        send(("down", half), side_in.at[0, rows], side_got.at[1, rows], (prev_row, col))
        send(("up", half), side_in.at[1, rows], side_got.at[0, rows], (next_row, col))

    def product(slot, tile, rows, cols):
        tall = pl.ds(pl.multiple_of(tile * OUT_SPAN, OUT_SPAN), OUT_SPAN)
        return lax.dot_general(
            jn[rows, cols], wv[slot, tall, cols], (((1,), (1,)), ((), ())),
            preferred_element_type=jnp.float32,
        )

    def each_tile(step):
        @pl.loop(0, tiles)
        def _(tile):
            step(tile, pl.ds(pl.multiple_of(tile * OUT_SPAN, OUT_SPAN), OUT_SPAN))

    every = pl.ds(0, WIDE)

    def fill(target, step, plane, rows, extra=None, last=None):
        slot = slot_of(step, plane)

        def one(tile, cols):
            value = product(slot, tile, rows, every)
            if extra is not None:
                value += extra[:, cols].astype(jnp.float32)
            if last is not None:
                zeros = jnp.zeros((HALF - LEND, OUT_SPAN), jnp.float32)
                value += jnp.concatenate([zeros, last[:, cols].astype(jnp.float32)], axis=0)
            target[rows, cols] = value.astype(jnp.bfloat16)

        each_tile(one)

    first = [(2, 1), (1, 1), (3, 1)]
    load_query.wait()
    for i, (step, plane) in enumerate(first):
        loads[step, plane].wait()

    def query_part(rows):
        for i, (step, plane) in enumerate(first):
            slot = slot_of(step, plane)

            def one(tile, cols):
                acc[i, tile, rows] = product(slot, tile, rows, pl.ds(0, FEAT))

            each_tile(one)

    def settle(half):
        rows = halves[half]
        got(("down", half), side_got.at[1, rows])
        got(("up", half), side_got.at[0, rows])
        value = mid[rows] + side_got[0, rows].astype(jnp.float32)
        value += side_got[1, rows].astype(jnp.float32)
        jn[rows, FEAT:] = value.astype(jnp.bfloat16)

    kept, given = pl.ds(HALF, HALF - LEND), pl.ds(TOK - LEND, LEND)

    def whole_part(half):
        rows = halves[half]
        for i, (step, plane) in enumerate(first):
            slot = slot_of(step, plane)

            def one(tile, cols):
                value = acc[i, tile, rows] + product(slot, tile, rows, pl.ds(FEAT, KV))
                pb[1, i, rows, cols] = value.astype(jnp.bfloat16)

            each_tile(one)
            if i == 0:
                send(("lend", half), pb.at[1, i, rows], lent.at[rows], l_pair)
                continue
            rows_out = kept if half else rows
            source, target = pb.at[1, i, rows_out], near.at[1, i - 1, rows_out]
            send(("near", 1, i - 1, half), source, target, z_next if i == 1 else z_prev)
        if half:
            for way in range(2):
                send(("give", way), pb.at[1, 1 + way, given], taken.at[way], l_pair)

    query_part(low)
    load_mid.wait()
    settle(0)
    whole_part(0)
    query_part(high)
    settle(1)
    whole_part(1)

    def near_half(way, half, extra=None):
        rows = halves[half]
        if half:
            got(("give", way), taken.at[way])
        fill(pb.at[0, 1 + way], 1 if way == 0 else 3, 0, rows, extra, taken.at[way] if half else None)
        send(
            ("near", 0, way, half), pb.at[0, 1 + way, rows], near.at[0, way, rows],
            z_next if way == 0 else z_prev,
        )

    loads[2, 0].wait()
    for half, rows in enumerate(halves):
        got(("lend", half), lent.at[rows])
        fill(pb.at[0, 0], 2, 0, rows, lent.at[rows])
        send(("far", half), pb.at[0, 0, rows], far.at[half], z_prev if half else z_next)
    loads[1, 0].wait()
    loads[3, 0].wait()
    near_half(0, 1)
    near_half(1, 0)

    def own(plane):
        loads[0, plane].wait()

        def one(tile, cols):
            acc[plane, tile] = product(slot_of(0, plane), tile, both, every)

        each_tile(one)

    def add_near(plane, way, half):
        rows = halves[half]
        got(("near", plane, way, half), near.at[plane, way, rows])

        def one(tile, cols):
            acc[plane, tile, rows] += near[plane, way, rows, cols].astype(jnp.float32)

        each_tile(one)

    own(1)
    for half, rows in enumerate(halves):
        rows_in = kept if half else rows
        for way in range(2):
            got(("near", 1, way, half), near.at[1, way, rows_in])

        def pair_sum(tile, cols):
            value = acc[1, tile, rows_in] + near[1, 0, rows_in, cols].astype(jnp.float32)
            value += near[1, 1, rows_in, cols].astype(jnp.float32)
            pair_out[rows_in, cols] = value.astype(jnp.bfloat16)
            if half:
                pair_out[given, cols] = acc[1, tile, given].astype(jnp.bfloat16)

        each_tile(pair_sum)
        send(("pair", half), pair_out.at[rows], pair_in.at[rows], l_pair)
    got(("far", 0), far.at[0])
    near_half(0, 0, far.at[0])
    got(("far", 1), far.at[1])
    near_half(1, 1, far.at[1])
    own(0)
    add_near(0, 0, 1)
    add_near(0, 1, 0)
    for half, rows in enumerate(halves):
        got(("pair", half), pair_in.at[rows])

        def add_pair(tile, cols):
            acc[0, tile, rows] += pair_in[rows, cols].astype(jnp.float32)

        each_tile(add_pair)
    for half, rows in enumerate(halves):
        got(("near", 0, half, half), near.at[0, half, rows])

        def last(tile, cols):
            value = acc[0, tile, rows] + near[0, half, rows, cols].astype(jnp.float32)
            result[rows, cols] = value.astype(jnp.bfloat16)

        each_tile(last)
        pltpu.make_async_copy(result.at[rows], out.at[rows], out_sem.at[half]).start()

    for copy in started:
        copy.wait_send()
    for half, rows in enumerate(halves):
        pltpu.make_async_copy(result.at[rows], out.at[rows], out_sem.at[half]).wait()


def scatter(grad_query, side, mid, full_wide):
    dma = pltpu.SemaphoreType.DMA
    anywhere = pl.BlockSpec(memory_space=pl.ANY)
    low = jnp.bfloat16
    return pl.pallas_call(
        scatter_kernel,
        name="project_scatter",
        out_shape=jax.ShapeDtypeStruct((TOK, FEAT), low),
        in_specs=[anywhere] * 4,
        out_specs=anywhere,
        scratch_shapes=[
            pltpu.VMEM((TOK, WIDE), low),
            pltpu.VMEM((COLS, FEAT, WIDE), low),
            pltpu.VMEM((3, FEAT // OUT_SPAN, TOK, OUT_SPAN), jnp.float32),
            pltpu.VMEM((2, 3, TOK, FEAT), low),
            pltpu.VMEM((TOK, FEAT), low),
            pltpu.VMEM((2, HALF, FEAT), low),
            pltpu.VMEM((2, 2, TOK, FEAT), low),
            pltpu.VMEM((TOK, FEAT), low),
            pltpu.VMEM((TOK, FEAT), low),
            pltpu.VMEM((2, TOK, KV), low),
            pltpu.VMEM((2, LEND, FEAT), low),
            pltpu.VMEM((TOK, KV), jnp.float32),
            pltpu.VMEM((TOK, FEAT), low),
            dma((COLS,)), dma((2,)), dma((2,)),
            dma((20,)), dma((20,)),
        ],
        compiler_params=pltpu.CompilerParams(
            collective_id=1, has_side_effects=True, vmem_limit_bytes=56 * MIB
        ),
        cost_estimate=pl.CostEstimate(
            flops=2 * TOK * 8192 * WIDE, bytes_accessed=24 * MIB, transcendentals=0
        ),
    )(grad_query, side, mid, full_wide)


def attend_kernel(
    pattern, counts, q_in, cot_in, kv_in,
    out, dq_out, side_out, mid_out,
    owed,
):
    block = pl.program_id(0)
    per_dev = TOK // BLOCK
    block_count = ROWS * per_dev
    first = lax.axis_index("row") * per_dev
    scale = HEAD_DIM ** (-0.5)
    exponent_scale = scale * LOG2E
    pair = 2 * HEAD_DIM

    @pl.when(block == 0)
    def _():
        owed[...] = jnp.zeros_like(owed)

    chosen = [pattern[block, i] for i in range(4)]
    local = [(b - first + per_dev + block_count) % block_count for b in chosen]
    keys = jnp.concatenate([kv_in[i, :, :HEAD_DIM] for i in local], axis=0)
    values = jnp.concatenate([kv_in[i, :, HEAD_DIM:] for i in local], axis=0)
    keys_t, values_t = keys.T, values.T
    spot = lax.broadcasted_iota(jnp.int32, (BLOCK, pair), 0)
    live = jnp.concatenate([spot < counts[b] for b in chosen], axis=0)
    own_count = counts[first + block]
    lane = lax.broadcasted_iota(jnp.int32, (1, pair), 1)
    query_live = jnp.where(lane % BLOCK < own_count, 1.0, 0.0)
    row_live = lax.broadcasted_iota(jnp.int32, (BLOCK, HEAD_DIM), 0) < own_count
    row_live = jnp.where(row_live, 1.0, 0.0).astype(jnp.bfloat16)

    def heads(ref, start, mask=None):
        parts = [ref[:, start + i * HEAD_DIM : start + (i + 1) * HEAD_DIM] for i in range(2)]
        if mask is not None:
            parts = [part * mask for part in parts]
        return jnp.concatenate(parts, axis=0)

    def dot(a, b, dims):
        return lax.dot_general(a, b, (dims, ((), ())), preferred_element_type=jnp.float32)

    def put(ref, start, both):
        low = both.astype(jnp.bfloat16)
        for i in range(2):
            cols = slice(start + i * HEAD_DIM, start + (i + 1) * HEAD_DIM)
            ref[:, cols] = low[:, i * HEAD_DIM : (i + 1) * HEAD_DIM].T

    def begin(start):
        query = heads(q_in, start)
        grad_out = heads(cot_in, start, row_live)
        raw = dot(keys, query, ((1,), (1,)))
        return start, query, grad_out, raw, dot(values, grad_out, ((1,), (1,)))

    def middle(start, query, grad_out, raw, grad_probs):
        raw = jnp.where(live, raw, -1e30)
        top = jnp.max(raw, axis=0, keepdims=True)
        power = jnp.exp2((raw - top) * exponent_scale)
        probs = power * (1.0 / jnp.sum(power, axis=0, keepdims=True))
        probs_low = probs.astype(jnp.bfloat16)
        delta = jnp.sum(probs_low.astype(jnp.float32) * grad_probs, axis=0, keepdims=True)
        grad_scores = (probs * (grad_probs - delta) * scale).astype(jnp.bfloat16)
        return start, query, grad_out, probs_low, grad_scores

    def end(start, query, grad_out, probs_low, grad_scores):
        put(out, start, dot(values_t, probs_low, ((1,), (0,))) * query_live)
        put(dq_out, start, dot(keys_t, grad_scores, ((1,), (0,))))
        key_part = dot(grad_scores, query, ((1,), (0,)))
        value_part = dot(probs_low, grad_out, ((1,), (0,)))
        return key_part, value_part

    starts = range(0, FEAT, pair)
    parts = []
    coming, going = begin(starts[0]), None
    for i in range(len(starts)):
        now = coming
        if i + 1 < len(starts):
            coming = begin(starts[i + 1])
        done = middle(*now)
        if going is not None:
            parts.append(end(*going))
        going = done
    parts.append(end(*going))
    grad_keys = sum(part[0] for part in parts[1:]) + parts[0][0]
    grad_values = sum(part[1] for part in parts[1:]) + parts[0][1]

    for i, spot in enumerate(local):
        rows = slice(i * BLOCK, (i + 1) * BLOCK)
        owed[spot, :, :HEAD_DIM] += grad_keys[rows]
        owed[spot, :, HEAD_DIM:] += grad_values[rows]

    @pl.when(block == per_dev - 1)
    def _():
        for i in range(per_dev):
            rows = slice(i * BLOCK, (i + 1) * BLOCK)
            side_out[0, rows] = owed[i].astype(jnp.bfloat16)
            mid_out[rows] = owed[per_dev + i]
            side_out[1, rows] = owed[2 * per_dev + i].astype(jnp.bfloat16)


def attend(pattern, counts, query, cotangent, source):
    per_dev = TOK // BLOCK
    tokens = pl.BlockSpec((BLOCK, FEAT), lambda b: (b, 0))
    smem = pl.BlockSpec(memory_space=pltpu.SMEM)
    low = jnp.bfloat16
    return pl.pallas_call(
        attend_kernel,
        name="attend",
        grid=(per_dev,),
        out_shape=(
            jax.ShapeDtypeStruct((TOK, FEAT), low),
            jax.ShapeDtypeStruct((TOK, FEAT), low),
            jax.ShapeDtypeStruct((2, TOK, KV), low),
            jax.ShapeDtypeStruct((TOK, KV), jnp.float32),
        ),
        in_specs=[
            smem, smem, tokens, tokens,
            pl.BlockSpec((3 * per_dev, BLOCK, KV), lambda b: (0, 0, 0)),
        ],
        out_specs=(
            tokens, tokens,
            pl.BlockSpec((2, TOK, KV), lambda b: (0, 0, 0)),
            pl.BlockSpec((TOK, KV), lambda b: (0, 0)),
        ),
        scratch_shapes=[pltpu.VMEM((3 * per_dev, BLOCK, KV), jnp.float32)],
        compiler_params=pltpu.CompilerParams(vmem_limit_bytes=62 * MIB),
    )(pattern, counts, query, cotangent, source.reshape(3 * per_dev, BLOCK, KV))


def body(layer_input, w_query, w_key, w_value, counts, pattern, cotangent):
    query, source, full_wide = gather(layer_input, w_query, w_key, w_value)
    attended, grad_query, side, mid = attend(pattern, counts, query, cotangent, source)
    input_grad = scatter(grad_query, side, mid, full_wide)
    return attended, input_grad


def solution(mesh):
    placed = (
        P("row", "col"),
        P("row", "col"),
        P("row", "col"),
        P("row", "col"),
        P(),
        P("row", None),
        P("row", "col"),
    )
    return jax.shard_map(
        body,
        mesh=mesh,
        in_specs=placed,
        out_specs=(P("row", "col"), P("row", "col")),
        check_vma=False,
    )
```

```python
import functools

import jax
import jax.numpy as jnp
from jax import lax
from jax.experimental import pallas as pl
from jax.experimental.pallas import tpu as pltpu
from jax.sharding import PartitionSpec as P

HEADS = 64
KV_HEADS = 8
HEAD_DIM = 128
BLOCK = 128
GROUP = HEADS // KV_HEADS
ROWS = 16
COLS = 8
TOK = 512
HALF = 256
FEAT = 1024
KV = 256
WIDE = FEAT + KV
MESH = pl.DeviceIdType.MESH
SPAN = 1024
LAST = 2
LEND = 64
OUT_SPAN = 1024
MIB = 1024 * 1024
LOG2E = 1.4426950408889634


def place():
    row, col = lax.axis_index("row"), lax.axis_index("col")
    return row, col, row // 4, (row // 2) % 2, row % 2, col // 2, col % 2


def remote(src, dst, send, recv, row, col):
    return pltpu.make_async_remote_copy(
        src_ref=src,
        dst_ref=dst,
        send_sem=send,
        recv_sem=recv,
        device_id=(row, col),
        device_id_type=MESH,
    )


FAR = 96
NEAR_KINDS = {
    0: (1, 0, 0, HALF), 1: (1, 0, HALF, HALF), 2: (3, 0, HALF, HALF), 3: (3, 0, 0, HALF),
    4: (1, 3, 0, HALF), 5: (3, 1, HALF, HALF),
}
FEW_KINDS = {
    **NEAR_KINDS, 4: (1, 3, 0, FAR), 5: (3, 1, FAR, FAR), 6: (1, 0, 0, TOK), 7: (3, 0, 0, TOK),
}
ALL_COLS, Q_COLS, KV_COLS = (0, WIDE), (0, FEAT), (FEAT, KV)


def w_cols(plane, kind):
    return ALL_COLS if plane == 0 else KV_COLS if kind > 5 else Q_COLS


X_KINDS = (NEAR_KINDS, NEAR_KINDS)
W_KINDS = (NEAR_KINDS, FEW_KINDS)


def gather_kernel(
    x_in, wq_in, wk_in, wv_in,
    q_out, kv_out, w_out,
    xf, wf, acc, kv_acc, kv_buf, q_buf,
    load_sem, send_sems, recv_sems, out_sem, kv_sem, q_sem,
):
    row, col, y, h, k, z, l = place()
    prev_row, next_row = (row + ROWS - 1) % ROWS, (row + 1) % ROWS

    def row_of(yy, hh, kk):
        return (yy * 2 + hh) * 2 + kk

    y_to = {1: (row_of((y + 1) % 4, h, k), col), 3: (row_of((y + 3) % 4, h, k), col)}
    z_to = {1: (row, ((z + 1) % 4) * 2 + l), 3: (row, ((z + 3) % 4) * 2 + l)}
    h_pair, sibling = (row_of(y, 1 - h, k), col), (row_of(y, h, 1 - k), col)
    l_pair = (row, z * 2 + 1 - l)

    own_x, own_w = col, row // 2
    own_rows = pl.ds(k * TOK, TOK)
    loads = [
        pltpu.make_async_copy(x_in, xf.at[own_x], load_sem.at[0]),
        pltpu.make_async_copy(wq_in, wf.at[own_w, own_rows, pl.ds(0, FEAT)], load_sem.at[1]),
        pltpu.make_async_copy(wk_in, wf.at[own_w, own_rows, pl.ds(FEAT, 128)], load_sem.at[2]),
        pltpu.make_async_copy(
            wv_in, wf.at[own_w, own_rows, pl.ds(FEAT + 128, 128)], load_sem.at[3]
        ),
    ]
    for load in loads:
        load.start()

    barrier = pltpu.get_barrier_semaphore()
    peers = [
        z_to[1], z_to[3], l_pair, y_to[1], y_to[3], h_pair, sibling,
        (prev_row, col), (next_row, col),
    ]
    for peer in peers:
        pl.semaphore_signal(barrier, inc=1, device_id=peer, device_id_type=MESH)
    pl.semaphore_wait(barrier, len(peers))
    for load in loads:
        load.wait()

    index, started = {}, []

    def move(name, src, dst, peer):
        i = index.setdefault(name, len(index))
        return remote(src, dst, send_sems.at[i], recv_sems.at[i], *peer)

    def send(name, ref, peer):
        copy = move(name, ref, ref, peer)
        copy.start()
        started.append(copy)

    def got(name, ref):
        move(name, ref, ref, sibling).wait_recv()

    def x_part(step, plane, first, count):
        slot = ((z + step) % 4) * 2 + (l + plane) % 2
        return xf.at[slot, pl.ds(first, count)]

    def w_part(step, plane, first, count, cols=ALL_COLS, core=None):
        slot = ((y + step) % 4) * 2 + (h + plane) % 2
        core = k if core is None else core
        return wf.at[slot, pl.ds(core * TOK + first, count), pl.ds(*cols)]

    shared = []

    def share(step, plane, first, count, cols=ALL_COLS):
        part = (step, plane, first, count, cols)
        send(("s", *part), w_part(*part), sibling)
        shared.append(part)

    def take_shared():
        for part in shared:
            got(("s", *part), w_part(*part, 1 - k))
        shared.clear()

    def x_ring(plane, *kinds):
        for kind in kinds:
            way, step, first, count = X_KINDS[plane][kind]
            send(("x", plane, kind), x_part(step, plane, first, count), z_to[way])

    def x_got(plane, *kinds):
        for kind in kinds:
            way, step, first, count = X_KINDS[plane][kind]
            got(("x", plane, kind), x_part((step - way) % 4, plane, first, count))

    def w_ring(plane, *kinds):
        for kind in kinds:
            way, step, first, count = W_KINDS[plane][kind]
            part = (step, plane, first, count, w_cols(plane, kind))
            send(("w", plane, kind), w_part(*part), y_to[way])

    def w_got(plane, kind, *then):
        way, step, first, count = W_KINDS[plane][kind]
        part = ((step - way) % 4, plane, first, count, w_cols(plane, kind))
        got(("w", plane, kind), w_part(*part))
        w_ring(plane, *then)
        share(*part)

    def w_lend(name, step, first, count, cols):
        send((name, first, cols), w_part(step, 0, first, count, cols), h_pair)

    def w_lent(name, step, first, count, cols, *then):
        part = (step, 1, first, count, cols)
        got((name, first, cols), w_part(*part))
        w_ring(1, *then)
        share(*part)

    for kind in (0, 2, 1, 3):
        x_ring(0, kind)
        w_ring(0, kind)
    for half in range(2):
        send(("xp", half), x_part(0, 0, half * HALF, HALF), l_pair)
        share(0, 0, half * HALF, HALF)

    x_got(0, 0)
    x_ring(0, 4)
    x_got(0, 2)
    x_ring(0, 5)
    got(("xp", 0), x_part(0, 1, 0, HALF))
    x_ring(1, 0, 3)
    w_got(0, 0, 4)
    w_got(0, 2, 5)
    got(("xp", 1), x_part(0, 1, HALF, HALF))
    x_ring(1, 2, 1)
    w_lend("wp", 0, 0, TOK, KV_COLS)
    w_lend("wp", 0, 0, HALF, Q_COLS)
    x_got(0, 1, 3)
    w_got(0, 1)
    w_got(0, 3)
    w_lent("wp", 0, 0, TOK, KV_COLS, 6, 7)
    x_got(0, 4, 5)
    w_lent("wp", 0, 0, HALF, Q_COLS, 0, 3)
    w_lend("wp", 0, HALF, HALF, Q_COLS)
    w_got(0, 4)
    w_got(0, 5)
    x_got(1, 0)
    x_ring(1, 4)
    w_lent("wp", 0, HALF, HALF, Q_COLS, 1, 2)
    w_lend("wf", 2, 0, TOK, KV_COLS)
    w_lend("wf", 2, 2 * FAR, HALF - 2 * FAR, Q_COLS)
    w_lend("wf", 2, HALF, HALF, Q_COLS)
    x_got(1, 2)
    x_ring(1, 5)
    w_got(1, 6)
    w_got(1, 7)
    x_got(1, 1, 3)
    take_shared()

    late_x = ((z + 2) % 4) * 2 + 1 - l
    late_w = ((y + 2) % 4) * 2 + 1 - h

    def multiply(slot, first, count):
        cols = pl.ds(first, count)
        return jnp.dot(xf[slot], wf[slot, :, cols], preferred_element_type=jnp.float32)

    def multiply_tile(slot, tile):
        return multiply(slot, pl.multiple_of(tile * SPAN, SPAN), SPAN)

    tiles = FEAT // SPAN

    @pl.loop(0, tiles)
    def _(tile):
        acc[tile] = jnp.zeros((TOK, SPAN), jnp.float32)

    def add_slots(wanted):
        @pl.loop(0, COLS)
        def _(slot):
            @pl.when(wanted(slot))
            def _():
                @pl.loop(0, tiles)
                def _(tile):
                    acc[tile] += multiply_tile(slot, tile)

                pltpu.make_async_copy(wf.at[slot], w_out.at[slot], out_sem.at[slot]).start()

    def early(slot):
        here = (slot % 2 == h) | (slot // 2 == y)
        return here & (slot != late_x)

    add_slots(early)

    w_got(1, 0, 4)
    w_got(1, 3, 5)
    w_lent("wf", 2, 0, TOK, KV_COLS)
    x_got(1, 4, 5)
    take_shared()

    kv_acc[...] = multiply(0, FEAT, KV)

    @pl.loop(1, COLS)
    def _(slot):
        kv_acc[...] += multiply(slot, FEAT, KV)

    kv_buf[...] = kv_acc[...].astype(jnp.bfloat16)
    halo = [
        move("up", kv_buf, kv_out.at[0], (next_row, col)),
        move("down", kv_buf, kv_out.at[2], (prev_row, col)),
    ]
    for copy in halo:
        copy.start()
    own_kv = pltpu.make_async_copy(kv_buf, kv_out.at[1], kv_sem)
    own_kv.start()

    w_lent("wf", 2, 2 * FAR, HALF - 2 * FAR, Q_COLS)
    w_got(1, 1)
    w_got(1, 2)
    take_shared()
    add_slots(lambda slot: jnp.logical_not(early(slot)) & (slot != late_w))
    w_lent("wf", 2, HALF, HALF, Q_COLS)
    w_got(1, 4)
    w_got(1, 5)
    take_shared()
    pltpu.make_async_copy(wf.at[late_w], w_out.at[late_w], out_sem.at[late_w]).start()

    for i in range(LAST):
        cols = pl.ds(i * (FEAT // LAST), FEAT // LAST)
        total = acc[0, :, cols] + multiply(late_w, i * (FEAT // LAST), FEAT // LAST)
        q_buf[:, cols] = total.astype(jnp.bfloat16)
        pltpu.make_async_copy(q_buf.at[:, cols], q_out.at[:, cols], q_sem.at[i]).start()

    for copy in started:
        copy.wait_send()
    for copy in halo:
        copy.wait()
    own_kv.wait()
    for i in range(LAST):
        cols = pl.ds(i * (FEAT // LAST), FEAT // LAST)
        pltpu.make_async_copy(q_buf.at[:, cols], q_out.at[:, cols], q_sem.at[i]).wait()
    for slot in range(COLS):
        pltpu.make_async_copy(wf.at[slot], w_out.at[slot], out_sem.at[slot]).wait()
    assert len(index) <= SEMS


SEMS = 60


def gather(*inputs):
    dma = pltpu.SemaphoreType.DMA
    return pl.pallas_call(
        gather_kernel,
        name="gather_project",
        out_shape=(
            jax.ShapeDtypeStruct((TOK, FEAT), jnp.bfloat16),
            jax.ShapeDtypeStruct((3, TOK, KV), jnp.bfloat16),
            jax.ShapeDtypeStruct((COLS, FEAT, WIDE), jnp.bfloat16),
        ),
        in_specs=[pl.BlockSpec(memory_space=pl.ANY)] * 4,
        out_specs=(
            pl.BlockSpec(memory_space=pl.ANY),
            pl.BlockSpec(memory_space=pl.ANY),
            pl.BlockSpec(memory_space=pl.ANY),
        ),
        scratch_shapes=[
            pltpu.VMEM((COLS, TOK, FEAT), jnp.bfloat16),
            pltpu.VMEM((COLS, FEAT, WIDE), jnp.bfloat16),
            pltpu.VMEM((FEAT // SPAN, TOK, SPAN), jnp.float32),
            pltpu.VMEM((TOK, KV), jnp.float32),
            pltpu.VMEM((TOK, KV), jnp.bfloat16),
            pltpu.VMEM((TOK, FEAT), jnp.bfloat16),
            dma((4,)),
            dma((SEMS,)), dma((SEMS,)),
            dma((COLS,)), dma, dma((LAST,)),
        ],
        compiler_params=pltpu.CompilerParams(
            collective_id=0, has_side_effects=True, vmem_limit_bytes=40 * MIB
        ),
        cost_estimate=pl.CostEstimate(
            flops=2 * TOK * 8192 * WIDE, bytes_accessed=40 * MIB, transcendentals=0
        ),
    )(*(pltpu.with_memory_space_constraint(a, pltpu.HBM) for a in inputs))


def scatter_kernel(
    dq_in, side_in, mid_in, w_in,
    out,
    jn, wv, acc, pb, lent, far, near, pair_out, pair_in, side_got, taken, mid, result,
    w_sem, load_sem, out_sem, send_sems, recv_sems,
):
    row, col, y, h, k, z, l = place()
    prev_row, next_row = (row + ROWS - 1) % ROWS, (row + 1) % ROWS
    z_next, z_prev = (row, ((z + 1) % 4) * 2 + l), (row, ((z + 3) % 4) * 2 + l)
    l_pair = (row, z * 2 + 1 - l)

    def slot_of(step, plane):
        return ((z + step) % 4) * 2 + (l + plane) % 2

    order = [(2, 1), (1, 1), (3, 1), (2, 0), (1, 0), (3, 0), (0, 1), (0, 0)]
    load_query = pltpu.make_async_copy(dq_in, jn.at[:, pl.ds(0, FEAT)], load_sem.at[0])
    load_mid = pltpu.make_async_copy(mid_in, mid, load_sem.at[1])
    load_query.start()
    loads = {}
    for i, (step, plane) in enumerate(order):
        slot = slot_of(step, plane)
        loads[step, plane] = pltpu.make_async_copy(w_in.at[slot], wv.at[slot], w_sem.at[i])
        loads[step, plane].start()
    load_mid.start()

    barrier = pltpu.get_barrier_semaphore()
    peers = [z_next, z_prev, l_pair, (prev_row, col), (next_row, col)]
    for peer in peers:
        pl.semaphore_signal(barrier, inc=1, device_id=peer, device_id_type=MESH)
    pl.semaphore_wait(barrier, len(peers))

    index, started = {}, []

    def send(name, src, dst, peer):
        i = index.setdefault(name, len(index))
        copy = remote(src, dst, send_sems.at[i], recv_sems.at[i], *peer)
        copy.start()
        started.append(copy)

    def got(name, ref):
        i = index[name]
        remote(ref, ref, send_sems.at[i], recv_sems.at[i], *l_pair).wait_recv()

    tiles = FEAT // OUT_SPAN
    low, high, both = pl.ds(0, HALF), pl.ds(HALF, HALF), pl.ds(0, TOK)
    halves = (low, high)
    for half, rows in enumerate(halves):
        send(("down", half), side_in.at[0, rows], side_got.at[1, rows], (prev_row, col))
        send(("up", half), side_in.at[1, rows], side_got.at[0, rows], (next_row, col))

    def product(slot, tile, rows, cols):
        tall = pl.ds(pl.multiple_of(tile * OUT_SPAN, OUT_SPAN), OUT_SPAN)
        return lax.dot_general(
            jn[rows, cols], wv[slot, tall, cols], (((1,), (1,)), ((), ())),
            preferred_element_type=jnp.float32,
        )

    def each_tile(step):
        @pl.loop(0, tiles)
        def _(tile):
            step(tile, pl.ds(pl.multiple_of(tile * OUT_SPAN, OUT_SPAN), OUT_SPAN))

    every = pl.ds(0, WIDE)

    def fill(target, step, plane, rows, extra=None, last=None):
        slot = slot_of(step, plane)

        def one(tile, cols):
            value = product(slot, tile, rows, every)
            if extra is not None:
                value += extra[:, cols].astype(jnp.float32)
            if last is not None:
                zeros = jnp.zeros((HALF - LEND, OUT_SPAN), jnp.float32)
                value += jnp.concatenate([zeros, last[:, cols].astype(jnp.float32)], axis=0)
            target[rows, cols] = value.astype(jnp.bfloat16)

        each_tile(one)

    first = [(2, 1), (1, 1), (3, 1)]
    load_query.wait()
    for i, (step, plane) in enumerate(first):
        loads[step, plane].wait()

    def query_part(rows):
        for i, (step, plane) in enumerate(first):
            slot = slot_of(step, plane)

            def one(tile, cols):
                acc[i, tile, rows] = product(slot, tile, rows, pl.ds(0, FEAT))

            each_tile(one)

    def settle(half):
        rows = halves[half]
        got(("down", half), side_got.at[1, rows])
        got(("up", half), side_got.at[0, rows])
        value = mid[rows] + side_got[0, rows].astype(jnp.float32)
        value += side_got[1, rows].astype(jnp.float32)
        jn[rows, FEAT:] = value.astype(jnp.bfloat16)

    kept, given = pl.ds(HALF, HALF - LEND), pl.ds(TOK - LEND, LEND)

    def whole_part(half):
        rows = halves[half]
        for i, (step, plane) in enumerate(first):
            slot = slot_of(step, plane)

            def one(tile, cols):
                value = acc[i, tile, rows] + product(slot, tile, rows, pl.ds(FEAT, KV))
                pb[1, i, rows, cols] = value.astype(jnp.bfloat16)

            each_tile(one)
            if i == 0:
                send(("lend", half), pb.at[1, i, rows], lent.at[rows], l_pair)
                continue
            rows_out = kept if half else rows
            source, target = pb.at[1, i, rows_out], near.at[1, i - 1, rows_out]
            send(("near", 1, i - 1, half), source, target, z_next if i == 1 else z_prev)
        if half:
            for way in range(2):
                send(("give", way), pb.at[1, 1 + way, given], taken.at[way], l_pair)

    query_part(low)
    load_mid.wait()
    settle(0)
    whole_part(0)
    query_part(high)
    settle(1)
    whole_part(1)

    def near_half(way, half, extra=None):
        rows = halves[half]
        if half:
            got(("give", way), taken.at[way])
        fill(pb.at[0, 1 + way], 1 if way == 0 else 3, 0, rows, extra, taken.at[way] if half else None)
        send(
            ("near", 0, way, half), pb.at[0, 1 + way, rows], near.at[0, way, rows],
            z_next if way == 0 else z_prev,
        )

    loads[2, 0].wait()
    for half, rows in enumerate(halves):
        got(("lend", half), lent.at[rows])
        fill(pb.at[0, 0], 2, 0, rows, lent.at[rows])
        send(("far", half), pb.at[0, 0, rows], far.at[half], z_prev if half else z_next)
    loads[1, 0].wait()
    loads[3, 0].wait()
    near_half(0, 1)
    near_half(1, 0)

    def own(plane):
        loads[0, plane].wait()

        def one(tile, cols):
            acc[plane, tile] = product(slot_of(0, plane), tile, both, every)

        each_tile(one)

    def add_near(plane, way, half):
        rows = halves[half]
        got(("near", plane, way, half), near.at[plane, way, rows])

        def one(tile, cols):
            acc[plane, tile, rows] += near[plane, way, rows, cols].astype(jnp.float32)

        each_tile(one)

    own(1)
    for half, rows in enumerate(halves):
        rows_in = kept if half else rows
        for way in range(2):
            got(("near", 1, way, half), near.at[1, way, rows_in])

        def pair_sum(tile, cols):
            value = acc[1, tile, rows_in] + near[1, 0, rows_in, cols].astype(jnp.float32)
            value += near[1, 1, rows_in, cols].astype(jnp.float32)
            pair_out[rows_in, cols] = value.astype(jnp.bfloat16)
            if half:
                pair_out[given, cols] = acc[1, tile, given].astype(jnp.bfloat16)

        each_tile(pair_sum)
        send(("pair", half), pair_out.at[rows], pair_in.at[rows], l_pair)
    got(("far", 0), far.at[0])
    near_half(0, 0, far.at[0])
    got(("far", 1), far.at[1])
    near_half(1, 1, far.at[1])
    own(0)
    add_near(0, 0, 1)
    add_near(0, 1, 0)
    for half, rows in enumerate(halves):
        got(("pair", half), pair_in.at[rows])

        def add_pair(tile, cols):
            acc[0, tile, rows] += pair_in[rows, cols].astype(jnp.float32)

        each_tile(add_pair)
    for half, rows in enumerate(halves):
        got(("near", 0, half, half), near.at[0, half, rows])

        def last(tile, cols):
            value = acc[0, tile, rows] + near[0, half, rows, cols].astype(jnp.float32)
            result[rows, cols] = value.astype(jnp.bfloat16)

        each_tile(last)
        pltpu.make_async_copy(result.at[rows], out.at[rows], out_sem.at[half]).start()

    for copy in started:
        copy.wait_send()
    for half, rows in enumerate(halves):
        pltpu.make_async_copy(result.at[rows], out.at[rows], out_sem.at[half]).wait()


def scatter(grad_query, side, mid, full_wide):
    dma = pltpu.SemaphoreType.DMA
    anywhere = pl.BlockSpec(memory_space=pl.ANY)
    low = jnp.bfloat16
    return pl.pallas_call(
        scatter_kernel,
        name="project_scatter",
        out_shape=jax.ShapeDtypeStruct((TOK, FEAT), low),
        in_specs=[anywhere] * 4,
        out_specs=anywhere,
        scratch_shapes=[
            pltpu.VMEM((TOK, WIDE), low),
            pltpu.VMEM((COLS, FEAT, WIDE), low),
            pltpu.VMEM((3, FEAT // OUT_SPAN, TOK, OUT_SPAN), jnp.float32),
            pltpu.VMEM((2, 3, TOK, FEAT), low),
            pltpu.VMEM((TOK, FEAT), low),
            pltpu.VMEM((2, HALF, FEAT), low),
            pltpu.VMEM((2, 2, TOK, FEAT), low),
            pltpu.VMEM((TOK, FEAT), low),
            pltpu.VMEM((TOK, FEAT), low),
            pltpu.VMEM((2, TOK, KV), low),
            pltpu.VMEM((2, LEND, FEAT), low),
            pltpu.VMEM((TOK, KV), jnp.float32),
            pltpu.VMEM((TOK, FEAT), low),
            dma((COLS,)), dma((2,)), dma((2,)),
            dma((20,)), dma((20,)),
        ],
        compiler_params=pltpu.CompilerParams(
            collective_id=1, has_side_effects=True, vmem_limit_bytes=48 * MIB
        ),
        cost_estimate=pl.CostEstimate(
            flops=2 * TOK * 8192 * WIDE, bytes_accessed=24 * MIB, transcendentals=0
        ),
    )(grad_query, side, mid, full_wide)


def attend_kernel(
    pattern, counts, q_in, cot_in, kv_in,
    out, dq_out, side_out, mid_out,
    owed,
):
    block = pl.program_id(0)
    per_dev = TOK // BLOCK
    block_count = ROWS * per_dev
    first = lax.axis_index("row") * per_dev
    scale = HEAD_DIM ** (-0.5)
    exponent_scale = scale * LOG2E
    pair = 2 * HEAD_DIM

    @pl.when(block == 0)
    def _():
        owed[...] = jnp.zeros_like(owed)

    chosen = [pattern[block, i] for i in range(4)]
    local = [(b - first + per_dev + block_count) % block_count for b in chosen]
    keys = jnp.concatenate([kv_in[i, :, :HEAD_DIM] for i in local], axis=0)
    values = jnp.concatenate([kv_in[i, :, HEAD_DIM:] for i in local], axis=0)
    keys_t, values_t = keys.T, values.T
    spot = lax.broadcasted_iota(jnp.int32, (BLOCK, pair), 0)
    live = jnp.concatenate([spot < counts[b] for b in chosen], axis=0)
    own_count = counts[first + block]
    lane = lax.broadcasted_iota(jnp.int32, (1, pair), 1)
    query_live = jnp.where(lane % BLOCK < own_count, 1.0, 0.0)
    row_live = lax.broadcasted_iota(jnp.int32, (BLOCK, HEAD_DIM), 0) < own_count
    row_live = jnp.where(row_live, 1.0, 0.0).astype(jnp.bfloat16)

    def heads(ref, start, mask=None):
        parts = [ref[:, start + i * HEAD_DIM : start + (i + 1) * HEAD_DIM] for i in range(2)]
        if mask is not None:
            parts = [part * mask for part in parts]
        return jnp.concatenate(parts, axis=0)

    def dot(a, b, dims):
        return lax.dot_general(a, b, (dims, ((), ())), preferred_element_type=jnp.float32)

    def put(ref, start, both):
        low = both.astype(jnp.bfloat16)
        for i in range(2):
            cols = slice(start + i * HEAD_DIM, start + (i + 1) * HEAD_DIM)
            ref[:, cols] = low[:, i * HEAD_DIM : (i + 1) * HEAD_DIM].T

    def begin(start):
        query = heads(q_in, start)
        grad_out = heads(cot_in, start, row_live)
        raw = dot(keys, query, ((1,), (1,)))
        return start, query, grad_out, raw, dot(values, grad_out, ((1,), (1,)))

    def middle(start, query, grad_out, raw, grad_probs):
        raw = jnp.where(live, raw, -1e30)
        top = jnp.max(raw, axis=0, keepdims=True)
        power = jnp.exp2((raw - top) * exponent_scale)
        probs = power * (1.0 / jnp.sum(power, axis=0, keepdims=True))
        probs_low = probs.astype(jnp.bfloat16)
        delta = jnp.sum(probs_low.astype(jnp.float32) * grad_probs, axis=0, keepdims=True)
        grad_scores = (probs * (grad_probs - delta) * scale).astype(jnp.bfloat16)
        return start, query, grad_out, probs_low, grad_scores

    def end(start, query, grad_out, probs_low, grad_scores):
        put(out, start, dot(values_t, probs_low, ((1,), (0,))) * query_live)
        put(dq_out, start, dot(keys_t, grad_scores, ((1,), (0,))))
        key_part = dot(grad_scores, query, ((1,), (0,)))
        value_part = dot(probs_low, grad_out, ((1,), (0,)))
        return key_part, value_part

    starts = range(0, FEAT, pair)
    parts = []
    coming, going = begin(starts[0]), None
    for i in range(len(starts)):
        now = coming
        if i + 1 < len(starts):
            coming = begin(starts[i + 1])
        done = middle(*now)
        if going is not None:
            parts.append(end(*going))
        going = done
    parts.append(end(*going))
    grad_keys = sum(part[0] for part in parts[1:]) + parts[0][0]
    grad_values = sum(part[1] for part in parts[1:]) + parts[0][1]

    for i, spot in enumerate(local):
        rows = slice(i * BLOCK, (i + 1) * BLOCK)
        owed[spot, :, :HEAD_DIM] += grad_keys[rows]
        owed[spot, :, HEAD_DIM:] += grad_values[rows]

    @pl.when(block == per_dev - 1)
    def _():
        for i in range(per_dev):
            rows = slice(i * BLOCK, (i + 1) * BLOCK)
            side_out[0, rows] = owed[i].astype(jnp.bfloat16)
            mid_out[rows] = owed[per_dev + i]
            side_out[1, rows] = owed[2 * per_dev + i].astype(jnp.bfloat16)


def attend(pattern, counts, query, cotangent, source):
    per_dev = TOK // BLOCK
    tokens = pl.BlockSpec((BLOCK, FEAT), lambda b: (b, 0))
    smem = pl.BlockSpec(memory_space=pltpu.SMEM)
    low = jnp.bfloat16
    return pl.pallas_call(
        attend_kernel,
        name="attend",
        grid=(per_dev,),
        out_shape=(
            jax.ShapeDtypeStruct((TOK, FEAT), low),
            jax.ShapeDtypeStruct((TOK, FEAT), low),
            jax.ShapeDtypeStruct((2, TOK, KV), low),
            jax.ShapeDtypeStruct((TOK, KV), jnp.float32),
        ),
        in_specs=[
            smem, smem, tokens, tokens,
            pl.BlockSpec((3 * per_dev, BLOCK, KV), lambda b: (0, 0, 0)),
        ],
        out_specs=(
            tokens, tokens,
            pl.BlockSpec((2, TOK, KV), lambda b: (0, 0, 0)),
            pl.BlockSpec((TOK, KV), lambda b: (0, 0)),
        ),
        scratch_shapes=[pltpu.VMEM((3 * per_dev, BLOCK, KV), jnp.float32)],
        compiler_params=pltpu.CompilerParams(vmem_limit_bytes=24 * MIB),
    )(pattern, counts, query, cotangent, source.reshape(3 * per_dev, BLOCK, KV))


def body(layer_input, w_query, w_key, w_value, counts, pattern, cotangent):
    query, source, full_wide = gather(layer_input, w_query, w_key, w_value)
    attended, grad_query, side, mid = attend(pattern, counts, query, cotangent, source)
    input_grad = scatter(grad_query, side, mid, full_wide)
    return attended, input_grad


def solution(mesh):
    placed = (
        P("row", "col"),
        P("row", "col"),
        P("row", "col"),
        P("row", "col"),
        P(),
        P("row", None),
        P("row", "col"),
    )
    return jax.shard_map(
        body,
        mesh=mesh,
        in_specs=placed,
        out_specs=(P("row", "col"), P("row", "col")),
        check_vma=False,
    )
```

```python
import functools

import jax
import jax.numpy as jnp
from jax import lax
from jax.experimental import pallas as pl
from jax.experimental.pallas import tpu as pltpu
from jax.sharding import PartitionSpec as P

HEADS = 64
KV_HEADS = 8
HEAD_DIM = 128
BLOCK = 128
GROUP = HEADS // KV_HEADS
ROWS = 16
COLS = 8
TOK = 512
HALF = 256
FEAT = 1024
KV = 256
WIDE = FEAT + KV
MESH = pl.DeviceIdType.MESH
SPAN = 1024
LAST = 2
LEND = 96
OUT_SPAN = 1024
MIB = 1024 * 1024
LOG2E = 1.4426950408889634


def place():
    row, col = lax.axis_index("row"), lax.axis_index("col")
    return row, col, row // 4, (row // 2) % 2, row % 2, col // 2, col % 2


def remote(src, dst, send, recv, row, col):
    return pltpu.make_async_remote_copy(
        src_ref=src,
        dst_ref=dst,
        send_sem=send,
        recv_sem=recv,
        device_id=(row, col),
        device_id_type=MESH,
    )


FAR = 96
NEAR_KINDS = {
    0: (1, 0, 0, HALF), 1: (1, 0, HALF, HALF), 2: (3, 0, HALF, HALF), 3: (3, 0, 0, HALF),
    4: (1, 3, 0, HALF), 5: (3, 1, HALF, HALF),
}
FEW_KINDS = {
    **NEAR_KINDS, 4: (1, 3, 0, FAR), 5: (3, 1, FAR, FAR), 6: (1, 0, 0, TOK), 7: (3, 0, 0, TOK),
}
ALL_COLS, Q_COLS, KV_COLS = (0, WIDE), (0, FEAT), (FEAT, KV)


def w_cols(plane, kind):
    return ALL_COLS if plane == 0 else KV_COLS if kind > 5 else Q_COLS


X_KINDS = (NEAR_KINDS, NEAR_KINDS)
W_KINDS = (NEAR_KINDS, FEW_KINDS)


def gather_kernel(
    x_in, wq_in, wk_in, wv_in,
    q_out, kv_out, w_out,
    xf, wf, acc, kv_acc, kv_buf, q_buf,
    load_sem, send_sems, recv_sems, out_sem, kv_sem, q_sem,
):
    row, col, y, h, k, z, l = place()
    prev_row, next_row = (row + ROWS - 1) % ROWS, (row + 1) % ROWS

    def row_of(yy, hh, kk):
        return (yy * 2 + hh) * 2 + kk

    y_to = {1: (row_of((y + 1) % 4, h, k), col), 3: (row_of((y + 3) % 4, h, k), col)}
    z_to = {1: (row, ((z + 1) % 4) * 2 + l), 3: (row, ((z + 3) % 4) * 2 + l)}
    h_pair, sibling = (row_of(y, 1 - h, k), col), (row_of(y, h, 1 - k), col)
    l_pair = (row, z * 2 + 1 - l)

    own_x, own_w = col, row // 2
    own_rows = pl.ds(k * TOK, TOK)
    loads = [
        pltpu.make_async_copy(x_in, xf.at[own_x], load_sem.at[0]),
        pltpu.make_async_copy(wq_in, wf.at[own_w, own_rows, pl.ds(0, FEAT)], load_sem.at[1]),
        pltpu.make_async_copy(wk_in, wf.at[own_w, own_rows, pl.ds(FEAT, 128)], load_sem.at[2]),
        pltpu.make_async_copy(
            wv_in, wf.at[own_w, own_rows, pl.ds(FEAT + 128, 128)], load_sem.at[3]
        ),
    ]
    for load in loads:
        load.start()

    barrier = pltpu.get_barrier_semaphore()
    peers = [
        z_to[1], z_to[3], l_pair, y_to[1], y_to[3], h_pair, sibling,
        (prev_row, col), (next_row, col),
    ]
    for peer in peers:
        pl.semaphore_signal(barrier, inc=1, device_id=peer, device_id_type=MESH)
    pl.semaphore_wait(barrier, len(peers))
    for load in loads:
        load.wait()

    index, started = {}, []

    def move(name, src, dst, peer):
        i = index.setdefault(name, len(index))
        return remote(src, dst, send_sems.at[i], recv_sems.at[i], *peer)

    def send(name, ref, peer):
        copy = move(name, ref, ref, peer)
        copy.start()
        started.append(copy)

    def got(name, ref):
        move(name, ref, ref, sibling).wait_recv()

    def x_part(step, plane, first, count):
        slot = ((z + step) % 4) * 2 + (l + plane) % 2
        return xf.at[slot, pl.ds(first, count)]

    def w_part(step, plane, first, count, cols=ALL_COLS, core=None):
        slot = ((y + step) % 4) * 2 + (h + plane) % 2
        core = k if core is None else core
        return wf.at[slot, pl.ds(core * TOK + first, count), pl.ds(*cols)]

    shared = []

    def share(step, plane, first, count, cols=ALL_COLS):
        part = (step, plane, first, count, cols)
        send(("s", *part), w_part(*part), sibling)
        shared.append(part)

    def take_shared():
        for part in shared:
            got(("s", *part), w_part(*part, 1 - k))
        shared.clear()

    def x_ring(plane, *kinds):
        for kind in kinds:
            way, step, first, count = X_KINDS[plane][kind]
            send(("x", plane, kind), x_part(step, plane, first, count), z_to[way])

    def x_got(plane, *kinds):
        for kind in kinds:
            way, step, first, count = X_KINDS[plane][kind]
            got(("x", plane, kind), x_part((step - way) % 4, plane, first, count))

    def w_ring(plane, *kinds):
        for kind in kinds:
            way, step, first, count = W_KINDS[plane][kind]
            part = (step, plane, first, count, w_cols(plane, kind))
            send(("w", plane, kind), w_part(*part), y_to[way])

    def w_got(plane, kind, *then):
        way, step, first, count = W_KINDS[plane][kind]
        part = ((step - way) % 4, plane, first, count, w_cols(plane, kind))
        got(("w", plane, kind), w_part(*part))
        w_ring(plane, *then)
        share(*part)

    def w_lend(name, step, first, count, cols):
        send((name, first, cols), w_part(step, 0, first, count, cols), h_pair)

    def w_lent(name, step, first, count, cols, *then):
        part = (step, 1, first, count, cols)
        got((name, first, cols), w_part(*part))
        w_ring(1, *then)
        share(*part)

    for kind in (0, 2, 1, 3):
        x_ring(0, kind)
        w_ring(0, kind)
    for half in range(2):
        send(("xp", half), x_part(0, 0, half * HALF, HALF), l_pair)
        share(0, 0, half * HALF, HALF)

    x_got(0, 0)
    x_ring(0, 4)
    x_got(0, 2)
    x_ring(0, 5)
    got(("xp", 0), x_part(0, 1, 0, HALF))
    x_ring(1, 0, 3)
    w_got(0, 0, 4)
    w_got(0, 2, 5)
    got(("xp", 1), x_part(0, 1, HALF, HALF))
    x_ring(1, 2, 1)
    w_lend("wp", 0, 0, TOK, KV_COLS)
    w_lend("wp", 0, 0, HALF, Q_COLS)
    x_got(0, 1, 3)
    w_got(0, 1)
    w_got(0, 3)
    w_lent("wp", 0, 0, TOK, KV_COLS, 6, 7)
    x_got(0, 4, 5)
    w_lent("wp", 0, 0, HALF, Q_COLS, 0, 3)
    w_lend("wp", 0, HALF, HALF, Q_COLS)
    w_got(0, 4)
    w_got(0, 5)
    x_got(1, 0)
    x_ring(1, 4)
    w_lent("wp", 0, HALF, HALF, Q_COLS, 1, 2)
    w_lend("wf", 2, 0, TOK, KV_COLS)
    w_lend("wf", 2, 2 * FAR, HALF - 2 * FAR, Q_COLS)
    w_lend("wf", 2, HALF, HALF, Q_COLS)
    x_got(1, 2)
    x_ring(1, 5)
    w_got(1, 6)
    w_got(1, 7)
    x_got(1, 1, 3)
    take_shared()

    late_x = ((z + 2) % 4) * 2 + 1 - l
    late_w = ((y + 2) % 4) * 2 + 1 - h

    def multiply(slot, first, count):
        cols = pl.ds(first, count)
        return jnp.dot(xf[slot], wf[slot, :, cols], preferred_element_type=jnp.float32)

    def multiply_tile(slot, tile):
        return multiply(slot, pl.multiple_of(tile * SPAN, SPAN), SPAN)

    tiles = FEAT // SPAN

    @pl.loop(0, tiles)
    def _(tile):
        acc[tile] = jnp.zeros((TOK, SPAN), jnp.float32)

    def add_slots(wanted):
        @pl.loop(0, COLS)
        def _(slot):
            @pl.when(wanted(slot))
            def _():
                @pl.loop(0, tiles)
                def _(tile):
                    acc[tile] += multiply_tile(slot, tile)

                pltpu.make_async_copy(wf.at[slot], w_out.at[slot], out_sem.at[slot]).start()

    def early(slot):
        here = (slot % 2 == h) | (slot // 2 == y)
        return here & (slot != late_x)

    add_slots(early)

    w_got(1, 0, 4)
    w_got(1, 3, 5)
    w_lent("wf", 2, 0, TOK, KV_COLS)
    x_got(1, 4, 5)
    take_shared()

    kv_acc[...] = multiply(0, FEAT, KV)

    @pl.loop(1, COLS)
    def _(slot):
        kv_acc[...] += multiply(slot, FEAT, KV)

    kv_buf[...] = kv_acc[...].astype(jnp.bfloat16)
    halo = [
        move("up", kv_buf, kv_out.at[0], (next_row, col)),
        move("down", kv_buf, kv_out.at[2], (prev_row, col)),
    ]
    for copy in halo:
        copy.start()
    own_kv = pltpu.make_async_copy(kv_buf, kv_out.at[1], kv_sem)
    own_kv.start()

    w_lent("wf", 2, 2 * FAR, HALF - 2 * FAR, Q_COLS)
    w_got(1, 1)
    w_got(1, 2)
    take_shared()
    add_slots(lambda slot: jnp.logical_not(early(slot)) & (slot != late_w))
    w_lent("wf", 2, HALF, HALF, Q_COLS)
    w_got(1, 4)
    w_got(1, 5)
    take_shared()
    pltpu.make_async_copy(wf.at[late_w], w_out.at[late_w], out_sem.at[late_w]).start()

    for i in range(LAST):
        cols = pl.ds(i * (FEAT // LAST), FEAT // LAST)
        total = acc[0, :, cols] + multiply(late_w, i * (FEAT // LAST), FEAT // LAST)
        q_buf[:, cols] = total.astype(jnp.bfloat16)
        pltpu.make_async_copy(q_buf.at[:, cols], q_out.at[:, cols], q_sem.at[i]).start()

    for copy in started:
        copy.wait_send()
    for copy in halo:
        copy.wait()
    own_kv.wait()
    for i in range(LAST):
        cols = pl.ds(i * (FEAT // LAST), FEAT // LAST)
        pltpu.make_async_copy(q_buf.at[:, cols], q_out.at[:, cols], q_sem.at[i]).wait()
    for slot in range(COLS):
        pltpu.make_async_copy(wf.at[slot], w_out.at[slot], out_sem.at[slot]).wait()
    assert len(index) <= SEMS


SEMS = 60


def gather(*inputs):
    dma = pltpu.SemaphoreType.DMA
    return pl.pallas_call(
        gather_kernel,
        name="gather_project",
        out_shape=(
            jax.ShapeDtypeStruct((TOK, FEAT), jnp.bfloat16),
            jax.ShapeDtypeStruct((3, TOK, KV), jnp.bfloat16),
            jax.ShapeDtypeStruct((COLS, FEAT, WIDE), jnp.bfloat16),
        ),
        in_specs=[pl.BlockSpec(memory_space=pl.ANY)] * 4,
        out_specs=(
            pl.BlockSpec(memory_space=pl.ANY),
            pl.BlockSpec(memory_space=pl.ANY),
            pl.BlockSpec(memory_space=pl.ANY),
        ),
        scratch_shapes=[
            pltpu.VMEM((COLS, TOK, FEAT), jnp.bfloat16),
            pltpu.VMEM((COLS, FEAT, WIDE), jnp.bfloat16),
            pltpu.VMEM((FEAT // SPAN, TOK, SPAN), jnp.float32),
            pltpu.VMEM((TOK, KV), jnp.float32),
            pltpu.VMEM((TOK, KV), jnp.bfloat16),
            pltpu.VMEM((TOK, FEAT), jnp.bfloat16),
            dma((4,)),
            dma((SEMS,)), dma((SEMS,)),
            dma((COLS,)), dma, dma((LAST,)),
        ],
        compiler_params=pltpu.CompilerParams(
            collective_id=0, has_side_effects=True, vmem_limit_bytes=40 * MIB
        ),
        cost_estimate=pl.CostEstimate(
            flops=2 * TOK * 8192 * WIDE, bytes_accessed=40 * MIB, transcendentals=0
        ),
    )(*(pltpu.with_memory_space_constraint(a, pltpu.HBM) for a in inputs))


def scatter_kernel(
    dq_in, side_in, mid_in, w_in,
    out,
    jn, wv, acc, pb, lent, far, near, pair_out, pair_in, side_got, taken, mid, result,
    w_sem, load_sem, out_sem, send_sems, recv_sems,
):
    row, col, y, h, k, z, l = place()
    prev_row, next_row = (row + ROWS - 1) % ROWS, (row + 1) % ROWS
    z_next, z_prev = (row, ((z + 1) % 4) * 2 + l), (row, ((z + 3) % 4) * 2 + l)
    l_pair = (row, z * 2 + 1 - l)

    def slot_of(step, plane):
        return ((z + step) % 4) * 2 + (l + plane) % 2

    order = [(2, 1), (1, 1), (3, 1), (2, 0), (1, 0), (3, 0), (0, 1), (0, 0)]
    load_query = pltpu.make_async_copy(dq_in, jn.at[:, pl.ds(0, FEAT)], load_sem.at[0])
    load_mid = pltpu.make_async_copy(mid_in, mid, load_sem.at[1])
    load_query.start()
    loads = {}
    for i, (step, plane) in enumerate(order):
        slot = slot_of(step, plane)
        loads[step, plane] = pltpu.make_async_copy(w_in.at[slot], wv.at[slot], w_sem.at[i])
        loads[step, plane].start()
    load_mid.start()

    barrier = pltpu.get_barrier_semaphore()
    peers = [z_next, z_prev, l_pair, (prev_row, col), (next_row, col)]
    for peer in peers:
        pl.semaphore_signal(barrier, inc=1, device_id=peer, device_id_type=MESH)
    pl.semaphore_wait(barrier, len(peers))

    index, started = {}, []

    def send(name, src, dst, peer):
        i = index.setdefault(name, len(index))
        copy = remote(src, dst, send_sems.at[i], recv_sems.at[i], *peer)
        copy.start()
        started.append(copy)

    def got(name, ref):
        i = index[name]
        remote(ref, ref, send_sems.at[i], recv_sems.at[i], *l_pair).wait_recv()

    tiles = FEAT // OUT_SPAN
    low, high, both = pl.ds(0, HALF), pl.ds(HALF, HALF), pl.ds(0, TOK)
    halves = (low, high)
    pieces = (pl.ds(0, HALF // 2), pl.ds(HALF // 2, HALF // 2), high)
    pieces_of = ((0, 1), (2,))
    for i, rows in enumerate(pieces):
        send(("down", i), side_in.at[0, rows], side_got.at[1, rows], (prev_row, col))
        send(("up", i), side_in.at[1, rows], side_got.at[0, rows], (next_row, col))

    def product(slot, tile, rows, cols):
        tall = pl.ds(pl.multiple_of(tile * OUT_SPAN, OUT_SPAN), OUT_SPAN)
        return lax.dot_general(
            jn[rows, cols], wv[slot, tall, cols], (((1,), (1,)), ((), ())),
            preferred_element_type=jnp.float32,
        )

    def each_tile(step):
        @pl.loop(0, tiles)
        def _(tile):
            step(tile, pl.ds(pl.multiple_of(tile * OUT_SPAN, OUT_SPAN), OUT_SPAN))

    every = pl.ds(0, WIDE)

    def fill(target, step, plane, rows, extra=None, last=None):
        slot = slot_of(step, plane)

        def one(tile, cols):
            value = product(slot, tile, rows, every)
            if extra is not None:
                value += extra[:, cols].astype(jnp.float32)
            if last is not None:
                zeros = jnp.zeros((HALF - LEND, OUT_SPAN), jnp.float32)
                value += jnp.concatenate([zeros, last[:, cols].astype(jnp.float32)], axis=0)
            target[rows, cols] = value.astype(jnp.bfloat16)

        each_tile(one)

    first = [(2, 1), (1, 1), (3, 1)]
    load_query.wait()
    for i, (step, plane) in enumerate(first):
        loads[step, plane].wait()

    def query_part(rows):
        for i, (step, plane) in enumerate(first):
            slot = slot_of(step, plane)

            def one(tile, cols):
                acc[i, tile, rows] = product(slot, tile, rows, pl.ds(0, FEAT))

            each_tile(one)

    def settle(piece):
        rows = pieces[piece]
        got(("down", piece), side_got.at[1, rows])
        got(("up", piece), side_got.at[0, rows])
        value = mid[rows] + side_got[0, rows].astype(jnp.float32)
        value += side_got[1, rows].astype(jnp.float32)
        jn[rows, FEAT:] = value.astype(jnp.bfloat16)

    kept, given = pl.ds(HALF, HALF - LEND), pl.ds(TOK - LEND, LEND)

    def whole_part(piece):
        rows = pieces[piece]
        for i in (1, 2, 0):
            slot = slot_of(*first[i])

            def one(tile, cols):
                value = acc[i, tile, rows] + product(slot, tile, rows, pl.ds(FEAT, KV))
                pb[1, i, rows, cols] = value.astype(jnp.bfloat16)

            each_tile(one)
            if i == 0:
                send(("lend", piece), pb.at[1, i, rows], lent.at[rows], l_pair)
                continue
            rows_out = kept if piece == 2 else rows
            source, target = pb.at[1, i, rows_out], near.at[1, i - 1, rows_out]
            send(("near", 1, i - 1, piece), source, target, z_next if i == 1 else z_prev)
        if piece == 2:
            for way in range(2):
                send(("give", way), pb.at[1, 1 + way, given], taken.at[way], l_pair)

    query_part(low)
    load_mid.wait()
    for piece in pieces_of[0]:
        settle(piece)
        whole_part(piece)
    query_part(high)
    for piece in pieces_of[1]:
        settle(piece)
        whole_part(piece)

    def near_half(way, half, extra=None):
        rows = halves[half]
        if half:
            got(("give", way), taken.at[way])
        fill(pb.at[0, 1 + way], 1 if way == 0 else 3, 0, rows, extra, taken.at[way] if half else None)
        send(
            ("near", 0, way, half), pb.at[0, 1 + way, rows], near.at[0, way, rows],
            z_next if way == 0 else z_prev,
        )

    loads[2, 0].wait()
    for half, rows in enumerate(halves):
        for piece in pieces_of[half]:
            got(("lend", piece), lent.at[pieces[piece]])
        fill(pb.at[0, 0], 2, 0, rows, lent.at[rows])
        send(("far", half), pb.at[0, 0, rows], far.at[half], z_prev if half else z_next)
    loads[1, 0].wait()
    loads[3, 0].wait()
    near_half(0, 1)
    near_half(1, 0)

    def own(plane):
        loads[0, plane].wait()

        def one(tile, cols):
            acc[plane, tile] = product(slot_of(0, plane), tile, both, every)

        each_tile(one)

    def add_near(plane, way, half):
        rows = halves[half]
        got(("near", plane, way, half), near.at[plane, way, rows])

        def one(tile, cols):
            acc[plane, tile, rows] += near[plane, way, rows, cols].astype(jnp.float32)

        each_tile(one)

    own(1)
    for half, rows in enumerate(halves):
        rows_in = kept if half else rows
        for way in range(2):
            for piece in pieces_of[half]:
                got(("near", 1, way, piece), near.at[1, way, rows_in if half else pieces[piece]])

        def pair_sum(tile, cols):
            value = acc[1, tile, rows_in] + near[1, 0, rows_in, cols].astype(jnp.float32)
            value += near[1, 1, rows_in, cols].astype(jnp.float32)
            pair_out[rows_in, cols] = value.astype(jnp.bfloat16)
            if half:
                pair_out[given, cols] = acc[1, tile, given].astype(jnp.bfloat16)

        each_tile(pair_sum)
        send(("pair", half), pair_out.at[rows], pair_in.at[rows], l_pair)
    got(("far", 0), far.at[0])
    near_half(0, 0, far.at[0])
    got(("far", 1), far.at[1])
    near_half(1, 1, far.at[1])
    own(0)
    add_near(0, 0, 1)
    add_near(0, 1, 0)
    for half, rows in enumerate(halves):
        got(("pair", half), pair_in.at[rows])

        def add_pair(tile, cols):
            acc[0, tile, rows] += pair_in[rows, cols].astype(jnp.float32)

        each_tile(add_pair)
    for half, rows in enumerate(halves):
        got(("near", 0, half, half), near.at[0, half, rows])

        def last(tile, cols):
            value = acc[0, tile, rows] + near[0, half, rows, cols].astype(jnp.float32)
            result[rows, cols] = value.astype(jnp.bfloat16)

        each_tile(last)
        pltpu.make_async_copy(result.at[rows], out.at[rows], out_sem.at[half]).start()

    for copy in started:
        copy.wait_send()
    for half, rows in enumerate(halves):
        pltpu.make_async_copy(result.at[rows], out.at[rows], out_sem.at[half]).wait()


def scatter(grad_query, side, mid, full_wide):
    dma = pltpu.SemaphoreType.DMA
    anywhere = pl.BlockSpec(memory_space=pl.ANY)
    low = jnp.bfloat16
    return pl.pallas_call(
        scatter_kernel,
        name="project_scatter",
        out_shape=jax.ShapeDtypeStruct((TOK, FEAT), low),
        in_specs=[anywhere] * 4,
        out_specs=anywhere,
        scratch_shapes=[
            pltpu.VMEM((TOK, WIDE), low),
            pltpu.VMEM((COLS, FEAT, WIDE), low),
            pltpu.VMEM((3, FEAT // OUT_SPAN, TOK, OUT_SPAN), jnp.float32),
            pltpu.VMEM((2, 3, TOK, FEAT), low),
            pltpu.VMEM((TOK, FEAT), low),
            pltpu.VMEM((2, HALF, FEAT), low),
            pltpu.VMEM((2, 2, TOK, FEAT), low),
            pltpu.VMEM((TOK, FEAT), low),
            pltpu.VMEM((TOK, FEAT), low),
            pltpu.VMEM((2, TOK, KV), low),
            pltpu.VMEM((2, LEND, FEAT), low),
            pltpu.VMEM((TOK, KV), jnp.float32),
            pltpu.VMEM((TOK, FEAT), low),
            dma((COLS,)), dma((2,)), dma((2,)),
            dma((25,)), dma((25,)),
        ],
        compiler_params=pltpu.CompilerParams(
            collective_id=1, has_side_effects=True, vmem_limit_bytes=48 * MIB
        ),
        cost_estimate=pl.CostEstimate(
            flops=2 * TOK * 8192 * WIDE, bytes_accessed=24 * MIB, transcendentals=0
        ),
    )(grad_query, side, mid, full_wide)


def attend_kernel(
    pattern, counts, q_in, cot_in, kv_in,
    out, dq_out, side_out, mid_out,
    owed, held, out_sem,
):
    per_dev = TOK // BLOCK
    block_count = ROWS * per_dev
    first = lax.axis_index("row") * per_dev
    scale = HEAD_DIM ** (-0.5)
    exponent_scale = scale * LOG2E
    pair = 2 * HEAD_DIM

    owed[...] = jnp.zeros_like(owed)

    def copy_out(block):
        rows = pl.ds(block * BLOCK, BLOCK)
        return pltpu.make_async_copy(held.at[rows], out.at[rows], out_sem.at[block])

    @pl.loop(0, per_dev)
    def _(block):
        block_rows = pl.ds(pl.multiple_of(block * BLOCK, BLOCK), BLOCK)
        chosen = [pattern[block, i] for i in range(4)]
        local = [(b - first + per_dev + block_count) % block_count for b in chosen]
        keys = jnp.concatenate([kv_in[i, :, :HEAD_DIM] for i in local], axis=0)
        values = jnp.concatenate([kv_in[i, :, HEAD_DIM:] for i in local], axis=0)
        keys_t, values_t = keys.T, values.T
        spot = lax.broadcasted_iota(jnp.int32, (BLOCK, pair), 0)
        live = jnp.concatenate([spot < counts[b] for b in chosen], axis=0)
        own_count = counts[first + block]
        lane = lax.broadcasted_iota(jnp.int32, (1, pair), 1)
        query_live = jnp.where(lane % BLOCK < own_count, 1.0, 0.0)
        row_live = lax.broadcasted_iota(jnp.int32, (BLOCK, HEAD_DIM), 0) < own_count
        row_live = jnp.where(row_live, 1.0, 0.0).astype(jnp.bfloat16)

        def heads(ref, start, mask=None):
            parts = [ref[block_rows, start + i * HEAD_DIM : start + (i + 1) * HEAD_DIM] for i in range(2)]
            if mask is not None:
                parts = [part * mask for part in parts]
            return jnp.concatenate(parts, axis=0)

        def dot(a, b, dims):
            return lax.dot_general(a, b, (dims, ((), ())), preferred_element_type=jnp.float32)

        def put(ref, start, both):
            low = both.astype(jnp.bfloat16)
            for i in range(2):
                cols = slice(start + i * HEAD_DIM, start + (i + 1) * HEAD_DIM)
                ref[block_rows, cols] = low[:, i * HEAD_DIM : (i + 1) * HEAD_DIM].T

        def begin(start):
            query = heads(q_in, start)
            grad_out = heads(cot_in, start, row_live)
            raw = dot(keys, query, ((1,), (1,)))
            return start, query, grad_out, raw, dot(values, grad_out, ((1,), (1,)))

        def middle(start, query, grad_out, raw, grad_probs):
            raw = jnp.where(live, raw, -1e30)
            top = jnp.max(raw, axis=0, keepdims=True)
            power = jnp.exp2((raw - top) * exponent_scale)
            probs = power * (1.0 / jnp.sum(power, axis=0, keepdims=True))
            probs_low = probs.astype(jnp.bfloat16)
            delta = jnp.sum(probs_low.astype(jnp.float32) * grad_probs, axis=0, keepdims=True)
            grad_scores = (probs * (grad_probs - delta) * scale).astype(jnp.bfloat16)
            return start, query, grad_out, probs_low, grad_scores

        def end(start, query, grad_out, probs_low, grad_scores):
            put(held, start, dot(values_t, probs_low, ((1,), (0,))) * query_live)
            put(dq_out, start, dot(keys_t, grad_scores, ((1,), (0,))))
            key_part = dot(grad_scores, query, ((1,), (0,)))
            value_part = dot(probs_low, grad_out, ((1,), (0,)))
            return key_part, value_part

        starts = range(0, FEAT, pair)
        parts = []
        coming, going = begin(starts[0]), None
        for i in range(len(starts)):
            now = coming
            if i + 1 < len(starts):
                coming = begin(starts[i + 1])
            done = middle(*now)
            if going is not None:
                parts.append(end(*going))
            going = done
        parts.append(end(*going))
        grad_keys = sum(part[0] for part in parts[1:]) + parts[0][0]
        grad_values = sum(part[1] for part in parts[1:]) + parts[0][1]

        for i, spot in enumerate(local):
            rows = slice(i * BLOCK, (i + 1) * BLOCK)
            owed[spot, :, :HEAD_DIM] += grad_keys[rows]
            owed[spot, :, HEAD_DIM:] += grad_values[rows]

        copy_out(block).start()

    for i in range(per_dev):
        rows = slice(i * BLOCK, (i + 1) * BLOCK)
        side_out[0, rows] = owed[i].astype(jnp.bfloat16)
        mid_out[rows] = owed[per_dev + i]
        side_out[1, rows] = owed[2 * per_dev + i].astype(jnp.bfloat16)
    for block in range(per_dev):
        copy_out(block).wait()


def attend(pattern, counts, query, cotangent, source):
    per_dev = TOK // BLOCK
    vmem = pl.BlockSpec(memory_space=pltpu.VMEM)
    smem = pl.BlockSpec(memory_space=pltpu.SMEM)
    low = jnp.bfloat16
    return pl.pallas_call(
        attend_kernel,
        name="attend",
        out_shape=(
            jax.ShapeDtypeStruct((TOK, FEAT), low),
            jax.ShapeDtypeStruct((TOK, FEAT), low),
            jax.ShapeDtypeStruct((2, TOK, KV), low),
            jax.ShapeDtypeStruct((TOK, KV), jnp.float32),
        ),
        in_specs=[smem, smem, vmem, vmem, vmem],
        out_specs=(pl.BlockSpec(memory_space=pl.ANY), vmem, vmem, vmem),
        scratch_shapes=[
            pltpu.VMEM((3 * per_dev, BLOCK, KV), jnp.float32),
            pltpu.VMEM((TOK, FEAT), low),
            pltpu.SemaphoreType.DMA((per_dev,)),
        ],
        compiler_params=pltpu.CompilerParams(vmem_limit_bytes=24 * MIB),
    )(pattern, counts, query, cotangent, source.reshape(3 * per_dev, BLOCK, KV))


def body(layer_input, w_query, w_key, w_value, counts, pattern, cotangent):
    query, source, full_wide = gather(layer_input, w_query, w_key, w_value)
    attended, grad_query, side, mid = attend(pattern, counts, query, cotangent, source)
    input_grad = scatter(grad_query, side, mid, full_wide)
    return attended, input_grad


def solution(mesh):
    placed = (
        P("row", "col"),
        P("row", "col"),
        P("row", "col"),
        P("row", "col"),
        P(),
        P("row", None),
        P("row", "col"),
    )
    return jax.shard_map(
        body,
        mesh=mesh,
        in_specs=placed,
        out_specs=(P("row", "col"), P("row", "col")),
        check_vma=False,
    )
```

```python
import functools

import jax
import jax.numpy as jnp
from jax import lax
from jax.experimental import pallas as pl
from jax.experimental.pallas import tpu as pltpu
from jax.sharding import PartitionSpec as P

HEADS = 64
KV_HEADS = 8
HEAD_DIM = 128
BLOCK = 128
GROUP = HEADS // KV_HEADS
ROWS = 16
COLS = 8
TOK = 512
HALF = 256
FEAT = 1024
KV = 256
WIDE = FEAT + KV
MESH = pl.DeviceIdType.MESH
SPAN = 1024
LAST = 2
LEND = 96
OUT_SPAN = 1024
MIB = 1024 * 1024
LOG2E = 1.4426950408889634


def place():
    row, col = lax.axis_index("row"), lax.axis_index("col")
    return row, col, row // 4, (row // 2) % 2, row % 2, col // 2, col % 2


def remote(src, dst, send, recv, row, col):
    return pltpu.make_async_remote_copy(
        src_ref=src,
        dst_ref=dst,
        send_sem=send,
        recv_sem=recv,
        device_id=(row, col),
        device_id_type=MESH,
    )


FAR = 96
NEAR_KINDS = {
    0: (1, 0, 0, HALF), 1: (1, 0, HALF, HALF), 2: (3, 0, HALF, HALF), 3: (3, 0, 0, HALF),
    4: (1, 3, 0, HALF), 5: (3, 1, HALF, HALF),
}
FEW_KINDS = {
    **NEAR_KINDS, 4: (1, 3, 0, FAR), 5: (3, 1, FAR, FAR), 6: (1, 0, 0, TOK), 7: (3, 0, 0, TOK),
}
ALL_COLS, Q_COLS, KV_COLS = (0, WIDE), (0, FEAT), (FEAT, KV)


def w_cols(plane, kind):
    return ALL_COLS if plane == 0 else KV_COLS if kind > 5 else Q_COLS


X_KINDS = (NEAR_KINDS, NEAR_KINDS)
W_KINDS = (NEAR_KINDS, FEW_KINDS)


def gather_kernel(
    x_in, wq_in, wk_in, wv_in,
    q_out, kv_out, w_out,
    xf, wf, acc, kv_acc, kv_buf, q_buf,
    load_sem, send_sems, recv_sems, out_sem, kv_sem, q_sem,
):
    row, col, y, h, k, z, l = place()
    prev_row, next_row = (row + ROWS - 1) % ROWS, (row + 1) % ROWS

    def row_of(yy, hh, kk):
        return (yy * 2 + hh) * 2 + kk

    y_to = {1: (row_of((y + 1) % 4, h, k), col), 3: (row_of((y + 3) % 4, h, k), col)}
    z_to = {1: (row, ((z + 1) % 4) * 2 + l), 3: (row, ((z + 3) % 4) * 2 + l)}
    h_pair, sibling = (row_of(y, 1 - h, k), col), (row_of(y, h, 1 - k), col)
    l_pair = (row, z * 2 + 1 - l)

    own_x, own_w = col, row // 2
    own_rows = pl.ds(k * TOK, TOK)
    loads = [
        pltpu.make_async_copy(x_in, xf.at[own_x], load_sem.at[0]),
        pltpu.make_async_copy(wq_in, wf.at[own_w, own_rows, pl.ds(0, FEAT)], load_sem.at[1]),
        pltpu.make_async_copy(wk_in, wf.at[own_w, own_rows, pl.ds(FEAT, 128)], load_sem.at[2]),
        pltpu.make_async_copy(
            wv_in, wf.at[own_w, own_rows, pl.ds(FEAT + 128, 128)], load_sem.at[3]
        ),
    ]
    for load in loads:
        load.start()

    barrier = pltpu.get_barrier_semaphore()
    peers = [
        z_to[1], z_to[3], l_pair, y_to[1], y_to[3], h_pair, sibling,
        (prev_row, col), (next_row, col),
    ]
    for peer in peers:
        pl.semaphore_signal(barrier, inc=1, device_id=peer, device_id_type=MESH)
    pl.semaphore_wait(barrier, len(peers))
    for load in loads:
        load.wait()

    index, started = {}, []

    def move(name, src, dst, peer):
        i = index.setdefault(name, len(index))
        return remote(src, dst, send_sems.at[i], recv_sems.at[i], *peer)

    def send(name, ref, peer):
        copy = move(name, ref, ref, peer)
        copy.start()
        started.append(copy)

    def got(name, ref):
        move(name, ref, ref, sibling).wait_recv()

    def x_part(step, plane, first, count):
        slot = ((z + step) % 4) * 2 + (l + plane) % 2
        return xf.at[slot, pl.ds(first, count)]

    def w_part(step, plane, first, count, cols=ALL_COLS, core=None):
        slot = ((y + step) % 4) * 2 + (h + plane) % 2
        core = k if core is None else core
        return wf.at[slot, pl.ds(core * TOK + first, count), pl.ds(*cols)]

    shared = []

    def share(step, plane, first, count, cols=ALL_COLS):
        part = (step, plane, first, count, cols)
        send(("s", *part), w_part(*part), sibling)
        shared.append(part)

    def take_shared():
        for part in shared:
            got(("s", *part), w_part(*part, 1 - k))
        shared.clear()

    def x_ring(plane, *kinds):
        for kind in kinds:
            way, step, first, count = X_KINDS[plane][kind]
            send(("x", plane, kind), x_part(step, plane, first, count), z_to[way])

    def x_got(plane, *kinds):
        for kind in kinds:
            way, step, first, count = X_KINDS[plane][kind]
            got(("x", plane, kind), x_part((step - way) % 4, plane, first, count))

    def w_ring(plane, *kinds):
        for kind in kinds:
            way, step, first, count = W_KINDS[plane][kind]
            part = (step, plane, first, count, w_cols(plane, kind))
            send(("w", plane, kind), w_part(*part), y_to[way])

    def w_got(plane, kind, *then):
        way, step, first, count = W_KINDS[plane][kind]
        part = ((step - way) % 4, plane, first, count, w_cols(plane, kind))
        got(("w", plane, kind), w_part(*part))
        w_ring(plane, *then)
        share(*part)

    def w_lend(name, step, first, count, cols):
        send((name, first, cols), w_part(step, 0, first, count, cols), h_pair)

    def w_lent(name, step, first, count, cols, *then):
        part = (step, 1, first, count, cols)
        got((name, first, cols), w_part(*part))
        w_ring(1, *then)
        share(*part)

    for kind in (0, 2, 1, 3):
        x_ring(0, kind)
        w_ring(0, kind)
    for half in range(2):
        send(("xp", half), x_part(0, 0, half * HALF, HALF), l_pair)
        share(0, 0, half * HALF, HALF)

    x_got(0, 0)
    x_ring(0, 4)
    x_got(0, 2)
    x_ring(0, 5)
    got(("xp", 0), x_part(0, 1, 0, HALF))
    x_ring(1, 0, 3)
    w_got(0, 0, 4)
    w_got(0, 2, 5)
    got(("xp", 1), x_part(0, 1, HALF, HALF))
    x_ring(1, 2, 1)
    w_lend("wp", 0, 0, TOK, KV_COLS)
    w_lend("wp", 0, 0, HALF, Q_COLS)
    x_got(0, 1, 3)
    w_got(0, 1)
    w_got(0, 3)
    w_lent("wp", 0, 0, TOK, KV_COLS, 6, 7)
    x_got(0, 4, 5)
    w_lent("wp", 0, 0, HALF, Q_COLS, 0, 3)
    w_lend("wp", 0, HALF, HALF, Q_COLS)
    w_got(0, 4)
    w_got(0, 5)
    x_got(1, 0)
    x_ring(1, 4)
    w_lent("wp", 0, HALF, HALF, Q_COLS, 1, 2)
    w_lend("wf", 2, 0, TOK, KV_COLS)
    w_lend("wf", 2, 2 * FAR, HALF - 2 * FAR, Q_COLS)
    w_lend("wf", 2, HALF, HALF, Q_COLS)
    x_got(1, 2)
    x_ring(1, 5)
    w_got(1, 6)
    w_got(1, 7)
    x_got(1, 1, 3)
    take_shared()

    late_x = ((z + 2) % 4) * 2 + 1 - l
    late_w = ((y + 2) % 4) * 2 + 1 - h

    def multiply(slot, first, count):
        cols = pl.ds(first, count)
        return jnp.dot(xf[slot], wf[slot, :, cols], preferred_element_type=jnp.float32)

    def multiply_tile(slot, tile):
        return multiply(slot, pl.multiple_of(tile * SPAN, SPAN), SPAN)

    tiles = FEAT // SPAN

    @pl.loop(0, tiles)
    def _(tile):
        acc[tile] = jnp.zeros((TOK, SPAN), jnp.float32)

    def add_slots(wanted):
        @pl.loop(0, COLS)
        def _(slot):
            @pl.when(wanted(slot))
            def _():
                @pl.loop(0, tiles)
                def _(tile):
                    acc[tile] += multiply_tile(slot, tile)

                pltpu.make_async_copy(wf.at[slot], w_out.at[slot], out_sem.at[slot]).start()

    def early(slot):
        here = (slot % 2 == h) | (slot // 2 == y)
        return here & (slot != late_x)

    add_slots(early)

    w_got(1, 0, 4)
    w_got(1, 3, 5)
    w_lent("wf", 2, 0, TOK, KV_COLS)
    x_got(1, 4, 5)
    take_shared()

    kv_acc[...] = multiply(0, FEAT, KV)

    @pl.loop(1, COLS)
    def _(slot):
        kv_acc[...] += multiply(slot, FEAT, KV)

    kv_buf[...] = kv_acc[...].astype(jnp.bfloat16)
    halo = [
        move("up", kv_buf, kv_out.at[0], (next_row, col)),
        move("down", kv_buf, kv_out.at[2], (prev_row, col)),
    ]
    for copy in halo:
        copy.start()
    own_kv = pltpu.make_async_copy(kv_buf, kv_out.at[1], kv_sem)
    own_kv.start()

    w_lent("wf", 2, 2 * FAR, HALF - 2 * FAR, Q_COLS)
    w_got(1, 1)
    w_got(1, 2)
    take_shared()
    add_slots(lambda slot: jnp.logical_not(early(slot)) & (slot != late_w))
    w_lent("wf", 2, HALF, HALF, Q_COLS)
    w_got(1, 4)
    w_got(1, 5)
    take_shared()
    pltpu.make_async_copy(wf.at[late_w], w_out.at[late_w], out_sem.at[late_w]).start()

    for i in range(LAST):
        cols = pl.ds(i * (FEAT // LAST), FEAT // LAST)
        total = acc[0, :, cols] + multiply(late_w, i * (FEAT // LAST), FEAT // LAST)
        q_buf[:, cols] = total.astype(jnp.bfloat16)
        pltpu.make_async_copy(q_buf.at[:, cols], q_out.at[:, cols], q_sem.at[i]).start()

    for copy in started:
        copy.wait_send()
    for copy in halo:
        copy.wait()
    own_kv.wait()
    for i in range(LAST):
        cols = pl.ds(i * (FEAT // LAST), FEAT // LAST)
        pltpu.make_async_copy(q_buf.at[:, cols], q_out.at[:, cols], q_sem.at[i]).wait()
    for slot in range(COLS):
        pltpu.make_async_copy(wf.at[slot], w_out.at[slot], out_sem.at[slot]).wait()
    assert len(index) <= SEMS


SEMS = 60


def gather(*inputs):
    dma = pltpu.SemaphoreType.DMA
    return pl.pallas_call(
        gather_kernel,
        name="gather_project",
        out_shape=(
            jax.ShapeDtypeStruct((TOK, FEAT), jnp.bfloat16),
            jax.ShapeDtypeStruct((3, TOK, KV), jnp.bfloat16),
            jax.ShapeDtypeStruct((COLS, FEAT, WIDE), jnp.bfloat16),
        ),
        in_specs=[pl.BlockSpec(memory_space=pl.ANY)] * 4,
        out_specs=(
            pl.BlockSpec(memory_space=pl.ANY),
            pl.BlockSpec(memory_space=pl.ANY),
            pl.BlockSpec(memory_space=pl.ANY),
        ),
        scratch_shapes=[
            pltpu.VMEM((COLS, TOK, FEAT), jnp.bfloat16),
            pltpu.VMEM((COLS, FEAT, WIDE), jnp.bfloat16),
            pltpu.VMEM((FEAT // SPAN, TOK, SPAN), jnp.float32),
            pltpu.VMEM((TOK, KV), jnp.float32),
            pltpu.VMEM((TOK, KV), jnp.bfloat16),
            pltpu.VMEM((TOK, FEAT), jnp.bfloat16),
            dma((4,)),
            dma((SEMS,)), dma((SEMS,)),
            dma((COLS,)), dma, dma((LAST,)),
        ],
        compiler_params=pltpu.CompilerParams(
            collective_id=0, has_side_effects=True, vmem_limit_bytes=40 * MIB
        ),
        cost_estimate=pl.CostEstimate(
            flops=2 * TOK * 8192 * WIDE, bytes_accessed=40 * MIB, transcendentals=0
        ),
    )(*(pltpu.with_memory_space_constraint(a, pltpu.HBM) for a in inputs))


def scatter_kernel(
    dq_in, side_in, mid_in, w_in,
    out,
    jn, wv, acc, pb, lent, far, near, pair_out, pair_in, side_got, taken, mid, result,
    w_sem, load_sem, out_sem, send_sems, recv_sems,
):
    row, col, y, h, k, z, l = place()
    prev_row, next_row = (row + ROWS - 1) % ROWS, (row + 1) % ROWS
    z_next, z_prev = (row, ((z + 1) % 4) * 2 + l), (row, ((z + 3) % 4) * 2 + l)
    l_pair = (row, z * 2 + 1 - l)

    def slot_of(step, plane):
        return ((z + step) % 4) * 2 + (l + plane) % 2

    order = [(2, 1), (1, 1), (3, 1), (2, 0), (1, 0), (3, 0), (0, 1), (0, 0)]
    load_query = pltpu.make_async_copy(dq_in, jn.at[:, pl.ds(0, FEAT)], load_sem.at[0])
    load_mid = pltpu.make_async_copy(mid_in, mid, load_sem.at[1])
    load_query.start()
    loads = {}
    for i, (step, plane) in enumerate(order):
        slot = slot_of(step, plane)
        loads[step, plane] = pltpu.make_async_copy(w_in.at[slot], wv.at[slot], w_sem.at[i])
        loads[step, plane].start()
    load_mid.start()

    barrier = pltpu.get_barrier_semaphore()
    peers = [z_next, z_prev, l_pair, (prev_row, col), (next_row, col)]
    for peer in peers:
        pl.semaphore_signal(barrier, inc=1, device_id=peer, device_id_type=MESH)
    pl.semaphore_wait(barrier, len(peers))

    index, started = {}, []

    def send(name, src, dst, peer):
        i = index.setdefault(name, len(index))
        copy = remote(src, dst, send_sems.at[i], recv_sems.at[i], *peer)
        copy.start()
        started.append(copy)

    def got(name, ref):
        i = index[name]
        remote(ref, ref, send_sems.at[i], recv_sems.at[i], *l_pair).wait_recv()

    tiles = FEAT // OUT_SPAN
    low, high, both = pl.ds(0, HALF), pl.ds(HALF, HALF), pl.ds(0, TOK)
    halves = (low, high)
    pieces = (pl.ds(0, HALF // 2), pl.ds(HALF // 2, HALF // 2), high)
    pieces_of = ((0, 1), (2,))
    for i, rows in enumerate(pieces):
        send(("down", i), side_in.at[0, rows], side_got.at[1, rows], (prev_row, col))
        send(("up", i), side_in.at[1, rows], side_got.at[0, rows], (next_row, col))

    def product(slot, tile, rows, cols):
        tall = pl.ds(pl.multiple_of(tile * OUT_SPAN, OUT_SPAN), OUT_SPAN)
        return lax.dot_general(
            jn[rows, cols], wv[slot, tall, cols], (((1,), (1,)), ((), ())),
            preferred_element_type=jnp.float32,
        )

    def each_tile(step):
        @pl.loop(0, tiles)
        def _(tile):
            step(tile, pl.ds(pl.multiple_of(tile * OUT_SPAN, OUT_SPAN), OUT_SPAN))

    every = pl.ds(0, WIDE)

    def fill(target, step, plane, rows, extra=None, last=None):
        slot = slot_of(step, plane)

        def one(tile, cols):
            value = product(slot, tile, rows, every)
            if extra is not None:
                value += extra[:, cols].astype(jnp.float32)
            if last is not None:
                zeros = jnp.zeros((HALF - LEND, OUT_SPAN), jnp.float32)
                value += jnp.concatenate([zeros, last[:, cols].astype(jnp.float32)], axis=0)
            target[rows, cols] = value.astype(jnp.bfloat16)

        each_tile(one)

    first = [(2, 1), (1, 1), (3, 1)]
    load_query.wait()
    for i, (step, plane) in enumerate(first):
        loads[step, plane].wait()

    def query_part(rows):
        for i, (step, plane) in enumerate(first):
            slot = slot_of(step, plane)

            def one(tile, cols):
                acc[i, tile, rows] = product(slot, tile, rows, pl.ds(0, FEAT))

            each_tile(one)

    def settle(piece):
        rows = pieces[piece]
        got(("down", piece), side_got.at[1, rows])
        got(("up", piece), side_got.at[0, rows])
        value = mid[rows] + side_got[0, rows].astype(jnp.float32)
        value += side_got[1, rows].astype(jnp.float32)
        jn[rows, FEAT:] = value.astype(jnp.bfloat16)

    kept, given = pl.ds(HALF, HALF - LEND), pl.ds(TOK - LEND, LEND)

    def whole_part(piece):
        rows = pieces[piece]
        for i in (1, 2, 0):
            slot = slot_of(*first[i])

            def one(tile, cols):
                value = acc[i, tile, rows] + product(slot, tile, rows, pl.ds(FEAT, KV))
                pb[1, i, rows, cols] = value.astype(jnp.bfloat16)

            each_tile(one)
            if i == 0:
                send(("lend", piece), pb.at[1, i, rows], lent.at[rows], l_pair)
                continue
            rows_out = kept if piece == 2 else rows
            source, target = pb.at[1, i, rows_out], near.at[1, i - 1, rows_out]
            send(("near", 1, i - 1, piece), source, target, z_next if i == 1 else z_prev)
        if piece == 2:
            for way in range(2):
                send(("give", way), pb.at[1, 1 + way, given], taken.at[way], l_pair)

    query_part(low)
    load_mid.wait()
    for piece in pieces_of[0]:
        settle(piece)
        whole_part(piece)
    query_part(high)
    for piece in pieces_of[1]:
        settle(piece)
        whole_part(piece)

    def near_half(way, half, extra=None):
        rows = halves[half]
        if half:
            got(("give", way), taken.at[way])
        fill(pb.at[0, 1 + way], 1 if way == 0 else 3, 0, rows, extra, taken.at[way] if half else None)
        send(
            ("near", 0, way, half), pb.at[0, 1 + way, rows], near.at[0, way, rows],
            z_next if way == 0 else z_prev,
        )

    loads[2, 0].wait()
    for half, rows in enumerate(halves):
        for piece in pieces_of[half]:
            got(("lend", piece), lent.at[pieces[piece]])
        fill(pb.at[0, 0], 2, 0, rows, lent.at[rows])
        send(("far", half), pb.at[0, 0, rows], far.at[half], z_prev if half else z_next)
    loads[1, 0].wait()
    loads[3, 0].wait()
    near_half(0, 1)
    near_half(1, 0)

    def own(plane):
        loads[0, plane].wait()

        def one(tile, cols):
            acc[plane, tile] = product(slot_of(0, plane), tile, both, every)

        each_tile(one)

    def add_near(plane, way, half):
        rows = halves[half]
        got(("near", plane, way, half), near.at[plane, way, rows])

        def one(tile, cols):
            acc[plane, tile, rows] += near[plane, way, rows, cols].astype(jnp.float32)

        each_tile(one)

    own(1)
    for half, rows in enumerate(halves):
        rows_in = kept if half else rows
        for way in range(2):
            for piece in pieces_of[half]:
                got(("near", 1, way, piece), near.at[1, way, rows_in if half else pieces[piece]])

        def pair_sum(tile, cols):
            value = acc[1, tile, rows_in] + near[1, 0, rows_in, cols].astype(jnp.float32)
            value += near[1, 1, rows_in, cols].astype(jnp.float32)
            pair_out[rows_in, cols] = value.astype(jnp.bfloat16)
            if half:
                pair_out[given, cols] = acc[1, tile, given].astype(jnp.bfloat16)

        each_tile(pair_sum)
        send(("pair", half), pair_out.at[rows], pair_in.at[rows], l_pair)
    got(("far", 0), far.at[0])
    near_half(0, 0, far.at[0])
    got(("far", 1), far.at[1])
    near_half(1, 1, far.at[1])
    own(0)
    add_near(0, 0, 1)
    add_near(0, 1, 0)
    for half, rows in enumerate(halves):
        got(("pair", half), pair_in.at[rows])

        def add_pair(tile, cols):
            acc[0, tile, rows] += pair_in[rows, cols].astype(jnp.float32)

        each_tile(add_pair)
    for half, rows in enumerate(halves):
        got(("near", 0, half, half), near.at[0, half, rows])

        def last(tile, cols):
            value = acc[0, tile, rows] + near[0, half, rows, cols].astype(jnp.float32)
            result[rows, cols] = value.astype(jnp.bfloat16)

        each_tile(last)
        pltpu.make_async_copy(result.at[rows], out.at[rows], out_sem.at[half]).start()

    for copy in started:
        copy.wait_send()
    for half, rows in enumerate(halves):
        pltpu.make_async_copy(result.at[rows], out.at[rows], out_sem.at[half]).wait()


def scatter(grad_query, side, mid, full_wide):
    dma = pltpu.SemaphoreType.DMA
    anywhere = pl.BlockSpec(memory_space=pl.ANY)
    low = jnp.bfloat16
    return pl.pallas_call(
        scatter_kernel,
        name="project_scatter",
        out_shape=jax.ShapeDtypeStruct((TOK, FEAT), low),
        in_specs=[anywhere] * 4,
        out_specs=anywhere,
        scratch_shapes=[
            pltpu.VMEM((TOK, WIDE), low),
            pltpu.VMEM((COLS, FEAT, WIDE), low),
            pltpu.VMEM((3, FEAT // OUT_SPAN, TOK, OUT_SPAN), jnp.float32),
            pltpu.VMEM((2, 3, TOK, FEAT), low),
            pltpu.VMEM((TOK, FEAT), low),
            pltpu.VMEM((2, HALF, FEAT), low),
            pltpu.VMEM((2, 2, TOK, FEAT), low),
            pltpu.VMEM((TOK, FEAT), low),
            pltpu.VMEM((TOK, FEAT), low),
            pltpu.VMEM((2, TOK, KV), low),
            pltpu.VMEM((2, LEND, FEAT), low),
            pltpu.VMEM((TOK, KV), jnp.float32),
            pltpu.VMEM((TOK, FEAT), low),
            dma((COLS,)), dma((2,)), dma((2,)),
            dma((25,)), dma((25,)),
        ],
        compiler_params=pltpu.CompilerParams(
            collective_id=1, has_side_effects=True, vmem_limit_bytes=48 * MIB
        ),
        cost_estimate=pl.CostEstimate(
            flops=2 * TOK * 8192 * WIDE, bytes_accessed=24 * MIB, transcendentals=0
        ),
    )(grad_query, side, mid, full_wide)


def attend_kernel(
    pattern, counts, q_in, cot_in, kv_in,
    out, dq_out, side_out, mid_out,
    owed, held, out_sem,
):
    per_dev = TOK // BLOCK
    block_count = ROWS * per_dev
    first = lax.axis_index("row") * per_dev
    scale = HEAD_DIM ** (-0.5)
    exponent_scale = scale * LOG2E
    pair = 2 * HEAD_DIM

    owed[...] = jnp.zeros_like(owed)

    def copy_out(block):
        rows = pl.ds(block * BLOCK, BLOCK)
        return pltpu.make_async_copy(held.at[rows], out.at[rows], out_sem.at[block])

    @pl.loop(0, per_dev, unroll=True)
    def _(block):
        block_rows = pl.ds(pl.multiple_of(block * BLOCK, BLOCK), BLOCK)
        chosen = [pattern[block, i] for i in range(4)]
        local = [(b - first + per_dev + block_count) % block_count for b in chosen]
        keys = jnp.concatenate([kv_in[i, :, :HEAD_DIM] for i in local], axis=0)
        values = jnp.concatenate([kv_in[i, :, HEAD_DIM:] for i in local], axis=0)
        keys_t, values_t = keys.T, values.T
        spot = lax.broadcasted_iota(jnp.int32, (BLOCK, pair), 0)
        live = jnp.concatenate([spot < counts[b] for b in chosen], axis=0)
        own_count = counts[first + block]
        lane = lax.broadcasted_iota(jnp.int32, (1, pair), 1)
        query_live = jnp.where(lane % BLOCK < own_count, 1.0, 0.0)
        row_live = lax.broadcasted_iota(jnp.int32, (BLOCK, HEAD_DIM), 0) < own_count
        row_live = jnp.where(row_live, 1.0, 0.0).astype(jnp.bfloat16)

        def heads(ref, start, mask=None):
            parts = [ref[block_rows, start + i * HEAD_DIM : start + (i + 1) * HEAD_DIM] for i in range(2)]
            if mask is not None:
                parts = [part * mask for part in parts]
            return jnp.concatenate(parts, axis=0)

        def dot(a, b, dims):
            return lax.dot_general(a, b, (dims, ((), ())), preferred_element_type=jnp.float32)

        def put(ref, start, both):
            low = both.astype(jnp.bfloat16)
            for i in range(2):
                cols = slice(start + i * HEAD_DIM, start + (i + 1) * HEAD_DIM)
                ref[block_rows, cols] = low[:, i * HEAD_DIM : (i + 1) * HEAD_DIM].T

        def begin(start):
            query = heads(q_in, start)
            grad_out = heads(cot_in, start, row_live)
            raw = dot(keys, query, ((1,), (1,)))
            return start, query, grad_out, raw, dot(values, grad_out, ((1,), (1,)))

        def middle(start, query, grad_out, raw, grad_probs):
            raw = jnp.where(live, raw, -1e30)
            top = jnp.max(raw, axis=0, keepdims=True)
            power = jnp.exp2((raw - top) * exponent_scale)
            probs = power * (1.0 / jnp.sum(power, axis=0, keepdims=True))
            probs_low = probs.astype(jnp.bfloat16)
            delta = jnp.sum(probs_low.astype(jnp.float32) * grad_probs, axis=0, keepdims=True)
            grad_scores = (probs * (grad_probs - delta) * scale).astype(jnp.bfloat16)
            return start, query, grad_out, probs_low, grad_scores

        def end(start, query, grad_out, probs_low, grad_scores):
            put(held, start, dot(values_t, probs_low, ((1,), (0,))) * query_live)
            put(dq_out, start, dot(keys_t, grad_scores, ((1,), (0,))))
            key_part = dot(grad_scores, query, ((1,), (0,)))
            value_part = dot(probs_low, grad_out, ((1,), (0,)))
            return key_part, value_part

        starts = range(0, FEAT, pair)
        parts = []
        coming, going = begin(starts[0]), None
        for i in range(len(starts)):
            now = coming
            if i + 1 < len(starts):
                coming = begin(starts[i + 1])
            done = middle(*now)
            if going is not None:
                parts.append(end(*going))
            going = done
        parts.append(end(*going))
        grad_keys = sum(part[0] for part in parts[1:]) + parts[0][0]
        grad_values = sum(part[1] for part in parts[1:]) + parts[0][1]

        for i, spot in enumerate(local):
            rows = slice(i * BLOCK, (i + 1) * BLOCK)
            owed[spot, :, :HEAD_DIM] += grad_keys[rows]
            owed[spot, :, HEAD_DIM:] += grad_values[rows]

        copy_out(block).start()

    for i in range(per_dev):
        rows = slice(i * BLOCK, (i + 1) * BLOCK)
        side_out[0, rows] = owed[i].astype(jnp.bfloat16)
        mid_out[rows] = owed[per_dev + i]
        side_out[1, rows] = owed[2 * per_dev + i].astype(jnp.bfloat16)
    for block in range(per_dev):
        copy_out(block).wait()


def attend(pattern, counts, query, cotangent, source):
    per_dev = TOK // BLOCK
    vmem = pl.BlockSpec(memory_space=pltpu.VMEM)
    smem = pl.BlockSpec(memory_space=pltpu.SMEM)
    low = jnp.bfloat16
    return pl.pallas_call(
        attend_kernel,
        name="attend",
        out_shape=(
            jax.ShapeDtypeStruct((TOK, FEAT), low),
            jax.ShapeDtypeStruct((TOK, FEAT), low),
            jax.ShapeDtypeStruct((2, TOK, KV), low),
            jax.ShapeDtypeStruct((TOK, KV), jnp.float32),
        ),
        in_specs=[smem, smem, vmem, vmem, vmem],
        out_specs=(pl.BlockSpec(memory_space=pl.ANY), vmem, vmem, vmem),
        scratch_shapes=[
            pltpu.VMEM((3 * per_dev, BLOCK, KV), jnp.float32),
            pltpu.VMEM((TOK, FEAT), low),
            pltpu.SemaphoreType.DMA((per_dev,)),
        ],
        compiler_params=pltpu.CompilerParams(vmem_limit_bytes=24 * MIB),
    )(pattern, counts, query, cotangent, source.reshape(3 * per_dev, BLOCK, KV))


def body(layer_input, w_query, w_key, w_value, counts, pattern, cotangent):
    query, source, full_wide = gather(layer_input, w_query, w_key, w_value)
    attended, grad_query, side, mid = attend(pattern, counts, query, cotangent, source)
    input_grad = scatter(grad_query, side, mid, full_wide)
    return attended, input_grad


def solution(mesh):
    placed = (
        P("row", "col"),
        P("row", "col"),
        P("row", "col"),
        P("row", "col"),
        P(),
        P("row", None),
        P("row", "col"),
    )
    return jax.shard_map(
        body,
        mesh=mesh,
        in_specs=placed,
        out_specs=(P("row", "col"), P("row", "col")),
        check_vma=False,
    )
```
